32 devices in a mesh: gx: 16 (over z, y, x), gy: 2 (over core).
Axes of the slice: x: 2, y: 2, z: 4, core: 2. Of those that a mesh axis runs over, the one named last changes fastest.
Arguments:
- displacement: float32 [3, 32, 128, 256], P(None, None, 'gx', 'gy'), may hold values from -6 to 6
- velocity: float32 [3, 32, 128, 256], P(None, None, 'gx', 'gy'), may hold values from -6 to 6
- slopes: float32 [2, 32, 128, 256], P(None, None, 'gx', 'gy'), may hold values from -0.5 to 0.5
- stretch: float32 [32, 128, 256], P(None, 'gx', 'gy'), may hold values from 0.6 to 1.4
- moduli: float32 [2, 32, 128, 256], P(None, None, 'gx', 'gy'), may hold values from 0.3 to 1
- buoyancy: float32 [32, 128, 256], P(None, 'gx', 'gy'), may hold values from 0.5 to 1.5
- probes: float32 [4, 128, 128], P(None, 'gy'), may hold values from -0.0048828125 to 0.0048828125
Outputs:
- final_displacement: float32 [3, 32, 128, 256], P(None, None, 'gx', 'gy')
- basis: float32 [64, 48, 128], P('gx', 'gy')
- factor: float32 [128, 128], replicated
The draws below stay inside these ranges and needn't reach their ends.
All inputs are finite; a program needn't handle non-finite values.
Results may differ from the reference program's by a relative error of at most 0.0003.
Values sent between devices are 32-bit elements; how exact they have to be, the bound alone decides.
No kernel may reach another device: no remote copies, remote signals or barrier semaphores. Data moves between devices by JAX's collectives and lax.ppermute only.
A program may use at most 64 MiB of HBM per device.

```python
import math
import jax
import jax.numpy as jnp
from jax import lax

NZ = 32
STEPS = 4
SKETCH = 128
NX = 128
NY = 256
ROWS = 3072


def shard_levels(stream_key, extent, shards, least, largest):
    gain = 1.0
    for dim, blocks in shards:
        heights = jax.random.uniform(jax.random.fold_in(jax.random.fold_in(stream_key, 6), dim), (blocks,), jnp.float32, least / len(shards), largest / len(shards))
        gain = gain * jnp.repeat(jnp.exp(heights), extent[dim] // blocks).reshape((-1,) + (1,) * (len(extent) - 1 - dim))
    return gain


def normal_values(own_key, extent, scale, most, split=(), kind=jnp.bfloat16):
    entries = scale * jax.random.normal(own_key, extent, jnp.float32)
    if split:
        entries = entries * shard_levels(own_key, extent, split, -0.22, 0.18)
    return jnp.clip(entries, -most, most).astype(kind)


def setup_inputs(seed: int = 0) -> dict:
    keys = jax.random.split(jax.random.key(seed), 8)
    displacement = normal_values(keys[0], (3, NZ, NX, NY), 1.0, 6.0, ((2, 16), (3, 2)), jnp.float32)
    velocity = normal_values(keys[1], (3, NZ, NX, NY), 1.0, 6.0, ((2, 16), (3, 2)), jnp.float32)
    slopes = jnp.clip(jax.random.uniform(keys[2], (2, NZ, NX, NY), jnp.float32, -0.5, 0.5) * shard_levels(keys[2], (2, NZ, NX, NY), ((2, 16), (3, 2)), -0.4, 0.0), -0.5, 0.5)
    stretch = jnp.clip(0.6 + 0.79999995 * jax.random.uniform(keys[3], (NZ, NX, NY), jnp.float32) ** shard_levels(keys[3], (NZ, NX, NY), ((1, 16), (2, 2)), -0.2, 0.2), 0.6, 1.4)
    moduli = jnp.clip(0.3 + 0.7 * jax.random.uniform(keys[4], (2, NZ, NX, NY), jnp.float32) ** shard_levels(keys[4], (2, NZ, NX, NY), ((2, 16), (3, 2)), -0.2, 0.2), 0.3, 1.0)
    buoyancy = jnp.clip(jnp.exp(math.log(1.5) - 1.0986123 * jax.random.uniform(keys[5], (NZ, NX, NY), jnp.float32) ** shard_levels(keys[5], (NZ, NX, NY), ((1, 16), (2, 2)), -0.2, 0.2)), 0.5, 1.5)
    probes = normal_values(keys[6], (STEPS, NY // 2, SKETCH), (STEPS * (NY // 2) * ROWS) ** -0.5, 0.0048828125, ((1, 2),), jnp.float32)
    return dict(displacement=displacement, velocity=velocity, slopes=slopes, stretch=stretch, moduli=moduli, buoyancy=buoyancy, probes=probes)


time_step = 0.12

def fourth(values, dimension):
    length_out = values.shape[dimension] - 4

    def segment(offset):
        return lax.slice_in_dim(values, offset, offset + length_out, axis=dimension)
    return (segment(0) - segment(4) + 8.0 * (segment(3) - segment(1))) / 12.0

def vertical(values):
    padded = jnp.pad(values, ((0, 0), (2, 2), (0, 0), (0, 0)))
    return fourth(padded, 1)

def gradient(padded, slope_x, slope_y, stretch):
    d_x = fourth(padded[:, :, :, 2:-2], 2)
    d_y = fourth(padded[:, :, 2:-2, :], 3)
    d_r = vertical(padded[:, :, 2:-2, 2:-2])
    return jnp.stack([d_x + slope_x * d_r, d_y + slope_y * d_r, stretch * d_r], axis=1)

def stresses(gradients, lame, shear):
    divergence = gradients[0, 0] + gradients[1, 1] + gradients[2, 2]
    pressure = lame * divergence
    return jnp.stack([pressure + 2.0 * shear * gradients[0, 0], pressure + 2.0 * shear * gradients[1, 1], pressure + 2.0 * shear * gradients[2, 2], shear * (gradients[0, 1] + gradients[1, 0]), shear * (gradients[0, 2] + gradients[2, 0]), shear * (gradients[1, 2] + gradients[2, 1])])

def forces(padded, slope_x, slope_y, stretch):
    d_x = fourth(padded[:, :, :, 2:-2], 2)
    d_y = fourth(padded[:, :, 2:-2, :], 3)
    d_r = vertical(padded[:, :, 2:-2, 2:-2])
    rows_x = (0, 3, 4)
    rows_y = (3, 1, 5)
    rows_z = (4, 5, 2)
    return jnp.stack([d_x[rows_x[component]] + slope_x * d_r[rows_x[component]] + d_y[rows_y[component]] + slope_y * d_r[rows_y[component]] + stretch * d_r[rows_z[component]] for component in range(3)])

def reference(displacement, velocity, slopes, stretch, moduli, buoyancy, probes):
    margin = ((0, 0), (0, 0), (2, 2), (2, 2))
    previous = displacement - time_step * velocity
    current = displacement
    sketch = jnp.zeros((NX // 2, 3 * (NZ // 2), SKETCH), jnp.float32)
    for moment in range(STEPS):
        gradients = gradient(jnp.pad(current, margin), slopes[0], slopes[1], stretch)
        stress = stresses(gradients, moduli[0], moduli[1])
        pushes = buoyancy * forces(jnp.pad(stress, margin), slopes[0], slopes[1], stretch)
        following = 2.0 * current - previous + time_step ** 2 * pushes
        velocities = (following - previous) / (2.0 * time_step)
        sampled = velocities[:, ::2, ::2, ::2]
        sketch_term = jnp.einsum('czxy,yk->xczk', sampled, probes[moment], precision=lax.Precision.HIGHEST)
        sketch = sketch + sketch_term.reshape(NX // 2, 3 * (NZ // 2), SKETCH)
        previous, current = (current, following)
    tall_block = sketch.reshape(-1, SKETCH)
    orthonormal, upper_part = jnp.linalg.qr(tall_block)
    diag_signs = jnp.sign(jnp.diagonal(upper_part))
    factor = upper_part * diag_signs[:, None]
    orthonormal = orthonormal * diag_signs[None, :]
    basis = (jnp.sqrt(jnp.float32(ROWS)) * orthonormal).reshape(sketch.shape)
    return (current, basis, factor)
```

```python
import math

import jax
import jax.numpy as jnp
from jax import lax
from jax.experimental import pallas as pl
from jax.experimental.pallas import tpu as pltpu
from jax.sharding import PartitionSpec as P

STEPS = 4
SUB = 8

time_step = 0.12


def roll(value, shift, axis=-1):
    axis = axis % value.ndim
    shift = shift % value.shape[axis]
    return value if shift == 0 else pltpu.roll(value, shift, axis)


def lanes_of(shape):
    return lax.broadcasted_iota(jnp.int32, shape, len(shape) - 1)


def layer_derivative(value):
    groups = value.shape[0] // SUB
    parts = [value[SUB * v : SUB * (v + 1)] for v in range(groups)]
    sub = lax.broadcasted_iota(jnp.int32, parts[0].shape, 0)
    shifted = {}

    def at(v):
        if 0 <= v < groups:
            return parts[v]
        if v not in shifted:
            if v >= groups:
                shifted[v] = jnp.where(sub < SUB - 1, roll(parts[v - groups], -1, 0), 0.0)
            else:
                shifted[v] = jnp.where(sub > 0, roll(parts[v + groups], 1, 0), 0.0)
        return shifted[v]

    return jnp.concatenate(
        [at(v - 2) - at(v + 2) + 8.0 * (at(v + 1) - at(v - 1)) for v in range(groups)], 0
    )


def band_matrix(count):
    row = lax.broadcasted_iota(jnp.int32, (count, count), 0)
    col = lax.broadcasted_iota(jnp.int32, (count, count), 1)
    away = row - col
    band = jnp.where(
        away == -2,
        1.0,
        jnp.where(away == 2, -1.0, jnp.where(away == 1, 8.0, jnp.where(away == -1, -8.0, 0.0))),
    )
    return band.astype(jnp.bfloat16)


def banded(value, band):
    high = value.astype(jnp.bfloat16)
    low = (value - high.astype(jnp.float32)).astype(jnp.bfloat16)
    return jnp.dot(high, band, preferred_element_type=jnp.float32) + jnp.dot(
        low, band, preferred_element_type=jnp.float32
    )


def edge_terms(edge, window):
    w = lanes_of(edge.shape) % window
    up_2, up_3 = roll(edge, 2), roll(edge, 3)
    down_2, down_3 = roll(edge, -2), roll(edge, -3)
    right = jnp.where(w == 7, 8.0 * up_3, 0.0) - up_2
    left = down_2 - jnp.where(w == 8, 8.0 * down_3, 0.0)
    return jnp.where((w == 6) | (w == 7), right, left)


def edge_spread(terms, place, window):
    count = terms.shape[-1]
    lane = lanes_of(terms.shape)
    return jnp.where((lane < 2) | (lane >= count - 2), roll(terms, count - 2 - window * place - 6), 0.0)


def edge_message(load, x_count, rows, y_count):
    window = y_count // x_count
    place = lanes_of((rows, y_count)) // window
    message = None
    for x in range(x_count):
        moved = roll(load(x), window * x + 4)
        message = moved if message is None else jnp.where(place == x, moved, message)
    return message


def corner_message(messages, first, window):
    place = lanes_of(messages[0].shape) // (2 * window)
    packed = None
    for c, message in enumerate(messages):
        moved = roll(message, 2 * window * c - window * first)
        packed = moved if packed is None else jnp.where(place == c, moved, packed)
    return packed


def edge_tile(own, from_left, from_right, has_left, has_right, window):
    w = lanes_of(own.shape) % window
    halo = jnp.where(w < 8, from_right * has_right, roll(from_left, 8) * has_left)
    mine = jnp.where(w < 4, own, roll(own, 8))
    return jnp.where((w >= 4) & (w < 12), halo, mine)


def begin_kernel(u_ref, low_ref, high_ref, edge_ref, up_ref, down_ref):
    comps, half, rows, y_count = low_ref.shape
    x_count = 2 * half
    window = y_count // x_count
    groups = rows // SUB
    messages = []
    for c in range(comps):

        def load(x):
            return jnp.concatenate(
                [
                    u_ref[c, pl.ds(x_count * v + x, SUB, stride=groups * x_count), :]
                    for v in range(groups)
                ],
                0,
            )

        slabs = [load(x) for x in range(x_count)]
        for x in range(x_count):
            (low_ref if x < half else high_ref)[c, x % half] = slabs[x]
        message = edge_message(lambda x: slabs[x], x_count, rows, y_count)
        edge_ref[c] = message
        messages.append(message)
    up_ref[...] = corner_message(messages, x_count - 2, window)
    down_ref[...] = corner_message(messages, 0, window)


def metric_kernel(
    u_ref, v_ref, slope_ref, stretch_ref, moduli_ref, buoyancy_ref,
    before_low, before_high, metric_ref, first_ref, last_ref, edge_ref, push_ref,
):
    comps, half, rows, y_count = before_low.shape
    x_count = 2 * half
    groups = rows // SUB

    def load(ref, *index):
        def at(x):
            return jnp.concatenate(
                [
                    ref[(*index, pl.ds(x_count * v + x, SUB, stride=groups * x_count), slice(None))]
                    for v in range(groups)
                ],
                0,
            )

        return at

    fields = [
        (load(slope_ref, 0), 1.0),
        (load(slope_ref, 1), 1.0),
        (load(stretch_ref), 1.0),
        (load(moduli_ref, 0), 1.0 / 12.0),
        (load(moduli_ref, 1), 1.0 / 12.0),
    ]
    for m, (at, scale) in enumerate(fields):
        slabs = [at(x) * scale if scale != 1.0 else at(x) for x in range(x_count)]
        for x in range(x_count):
            metric_ref[m, x] = slabs[x]
        for k in range(2):
            first_ref[m, k] = slabs[k]
            last_ref[m, k] = slabs[x_count - 2 + k]
        edge_ref[m] = edge_message(lambda x: slabs[x], x_count, rows, y_count)
    at = load(buoyancy_ref)
    for x in range(x_count):
        push_ref[x] = at(x) * (time_step**2 / 12.0)
    for c in range(comps):
        at, rate = load(u_ref, c), load(v_ref, c)
        for x in range(x_count):
            (before_low if x < half else before_high)[c, x % half] = at(x) - time_step * rate(x)


def all_stresses(grads, lame, shear):
    pressure = lame * (grads[0][0] + grads[1][1] + grads[2][2])
    twice = shear + shear
    return (
        pressure + twice * grads[0][0],
        pressure + twice * grads[1][1],
        pressure + twice * grads[2][2],
        shear * (grads[0][1] + grads[1][0]),
        shear * (grads[0][2] + grads[2][0]),
        shear * (grads[1][2] + grads[2][1]),
    )


def make_step(sides, first_step, last_step):
    def kernel(*refs):
        refs = list(refs)

        def take(count):
            out = refs[:count]
            del refs[:count]
            return out

        (side_ref,) = take(1)
        low_ref, high_ref, below_ref, above_ref = take(4)
        before_low, before_high = take(2)
        metric_ref, push_ref, metric_below, metric_above = take(4)
        (edge_ref,) = take(1)
        edge_in = take(sides)
        up_in = take(sides)
        down_in = take(sides)
        (metric_edge,) = take(1)
        metric_edge_in = take(sides)
        (probe_ref,) = take(1)
        sketch_in = None if first_step else take(1)[0]
        if last_step:
            out_ref, sketch_ref = take(2)
        else:
            out_low, out_high, out_edge, out_up, out_down, sketch_ref = take(6)
        ext, dyu, s_x, s_o, dys, rates, spread_probe = take(7)

        comps, half, rows, y_count = low_ref.shape
        x_count = 2 * half
        window = y_count // x_count
        groups = rows // SUB
        has_left, has_right = side_ref[0], side_ref[1]
        band = band_matrix(y_count)
        edge_shape = (rows, y_count)
        lane = lanes_of(edge_shape)
        w = lane % window
        place = lane // window

        for c in range(comps):
            for k in range(half):
                ext[c, k] = below_ref[c, k]
                ext[c, half + k] = low_ref[c, k]
                ext[c, 2 * half + k] = high_ref[c, k]
                ext[c, 3 * half + k] = above_ref[c, k]

        edges, corners = [], []
        for c in range(comps):
            edge = edge_tile(edge_ref[c], edge_in[0][c], edge_in[-1][c], has_left, has_right, window)
            size = 2 * window

            def beside(which):
                return jnp.where(
                    place >= x_count - 2,
                    roll(up_in[which][...], (x_count - 2) * window - size * c),
                    roll(down_in[which][...], -size * c),
                )

            corner = jnp.where(
                w < 8, beside(-1) * has_right, roll(beside(0), 8) * has_left
            )
            edges.append(edge)
            corners.append(corner)
            edge_add = edge_terms(edge, window)
            corner_add = edge_terms(corner, window)
            first, count = (half - 2, x_count + 4) if c < 2 else (half, x_count)
            flat = ext[c, first : first + count].reshape(count * rows, y_count)
            result = banded(flat, band)
            for k in range(count):
                x = first + k - half
                terms = edge_add if 0 <= x < x_count else corner_add
                dyu[c, first + k] = result[k * rows : (k + 1) * rows] + edge_spread(
                    terms, x % x_count, window
                )

        def gradients(at, metric, full):
            slope_x, slope_y, stretch = metric[:3]
            grads = []
            for c in range(comps):
                dr = layer_derivative(ext[c, at])
                dx = ext[c, at - 2] - ext[c, at + 2] + 8.0 * (ext[c, at + 1] - ext[c, at - 1])
                row = [dx + slope_x * dr, None, stretch * dr]
                if full or c < 2:
                    row[1] = dyu[c, at] + slope_y * dr
                else:
                    row[1] = dr
                grads.append(row)
            return grads

        def tile_row(x, carry):
            metric = [metric_ref[m, x] for m in range(5)]
            grads = gradients(x + half, metric, True)
            s11, s22, s33, s12, s13, s23 = all_stresses(grads, metric[3], metric[4])
            s_x[0, x + 2] = s11
            s_x[1, x + 2] = s12
            s_x[2, x + 2] = s13
            s_o[0, x] = s22
            s_o[1, x] = s23
            s_o[2, x] = s33
            return carry

        for k in range(2):
            for source, at in ((metric_below, half - 2 + k), (metric_above, half + x_count + k)):
                metric = [source[m, k] for m in range(5)]
                grads = gradients(at, metric, False)
                s11, _, _, s12, s13, _ = all_stresses(grads, metric[3], metric[4])
                s_x[0, at - half + 2] = s11
                s_x[1, at - half + 2] = s12
                s_x[2, at - half + 2] = s13
        lax.fori_loop(0, x_count, tile_row, 0)

        metric = [
            edge_tile(
                metric_edge[m], metric_edge_in[0][m], metric_edge_in[-1][m],
                has_left, has_right, window,
            )
            for m in range(5)
        ]
        grads = []
        for c in range(comps):
            edge, corner = edges[c], corners[c]

            def along(k):
                inside = (place + k < x_count) if k > 0 else (place + k >= 0)
                return jnp.where(inside, roll(edge, -window * k), roll(corner, -window * k))

            dr = layer_derivative(edge)
            if c < 2:
                dx = along(-2) - along(2) + 8.0 * (along(1) - along(-1))
            else:
                dx = dr
            dy = roll(edge, 2) - roll(edge, -2) + 8.0 * (roll(edge, -1) - roll(edge, 1))
            grads.append([dx + metric[0] * dr, dy + metric[1] * dr, metric[2] * dr])
        _, e22, _, e12, _, e23 = all_stresses(grads, metric[3], metric[4])

        for i, (edge, source) in enumerate(((e12, None), (e22, 0), (e23, 1))):
            value = s_x[1, 2 : 2 + x_count] if source is None else s_o[source]
            result = banded(value.reshape(x_count * rows, y_count), band)
            terms = edge_terms(edge, window)
            for x in range(x_count):
                dys[i, x] = result[x * rows : (x + 1) * rows] + edge_spread(terms, x, window)

        def update(x, keep):
            slope_x, slope_y, stretch = metric_ref[0, x], metric_ref[1, x], metric_ref[2, x]
            push = push_ref[x]
            r11, r12, r13 = (layer_derivative(s_x[k, x + 2]) for k in range(3))
            r22, r23, r33 = (layer_derivative(s_o[k, x]) for k in range(3))
            layers = ((r11, r12, r13), (r12, r22, r23), (r13, r23, r33))
            for c in range(comps):
                force = s_x[c, x] - s_x[c, x + 4] + 8.0 * (s_x[c, x + 3] - s_x[c, x + 1])
                force = force + slope_x * layers[c][0] + dys[c, x]
                force = force + slope_y * layers[c][1] + stretch * layers[c][2]
                keep(c, force * push)

        picked = groups // 2
        messages = [None] * comps
        for x in range(x_count):
            before = before_low if x < half else before_high

            def keep(c, change):
                past = before[c, x % half]
                following = 2.0 * ext[c, half + x] - past + change
                if last_step:
                    for v in range(groups):
                        out_ref[c, pl.ds(x_count * v + x, SUB, stride=groups * x_count), :] = (
                            following[SUB * v : SUB * (v + 1)]
                        )
                else:
                    (out_low if x < half else out_high)[c, x % half] = following
                    moved = roll(following, window * x + 4)
                    messages[c] = moved if x == 0 else jnp.where(place == x, moved, messages[c])
                if x % 2 == 0:
                    rate = (following - past) * (0.5 / time_step)
                    for v in range(0, groups, 2):
                        start = ((x // 2 * comps + c) * picked + v // 2) * SUB
                        rates[start : start + SUB] = rate[SUB * v : SUB * (v + 1)]

            update(x, keep)

        if not last_step:
            for c in range(comps):
                out_edge[c] = messages[c]
            out_up[...] = corner_message(messages, x_count - 2, window)
            out_down[...] = corner_message(messages, 0, window)

        spread_probe[...] = jnp.zeros_like(spread_probe)
        spread_probe[pl.ds(0, y_count // 2, stride=2), :] = probe_ref[...]
        sketch = jnp.dot(
            rates[...],
            spread_probe[...],
            precision=lax.Precision.HIGHEST,
            preferred_element_type=jnp.float32,
        )
        if sketch_in is not None:
            sketch = sketch + sketch_in[...]
        if last_step:
            for k in range(x_count // 2 * comps):
                for v in range(picked):
                    start = (k * picked + v) * SUB
                    sketch_ref[pl.ds(k * picked * SUB + v, SUB, stride=picked), :] = sketch[
                        start : start + SUB
                    ]
        else:
            sketch_ref[...] = sketch

    return kernel


def gram_kernel(first_ref, second_ref, sum_ref, gram_ref):
    total = first_ref[...] + second_ref[...]
    sum_ref[...] = total
    gram_ref[...] = lax.dot_general(
        total,
        total,
        (((0,), (0,)), ((), ())),
        precision=lax.Precision.HIGHEST,
        preferred_element_type=jnp.float32,
    )


def factor_kernel(scale):
    def kernel(side_ref, gram_ref, tall_ref, basis_ref, factor_ref):
        order = gram_ref.shape[0]
        blocks = order // SUB
        shape = (SUB, order)
        sub = lax.broadcasted_iota(jnp.int32, shape, 0)
        lane = lanes_of(shape)
        work = [gram_ref[SUB * q : SUB * (q + 1), :] for q in range(blocks)]
        other = [jnp.where(lane == sub + SUB * q, 1.0, 0.0) for q in range(blocks)]
        for j in range(order):
            p, k = divmod(j, SUB)
            columns = [jnp.broadcast_to(work[q][:, j : j + 1], shape) for q in range(p, blocks)]
            pivot = jnp.broadcast_to(columns[0][k : k + 1, :], shape)
            inverse = 1.0 / pivot
            row = jnp.broadcast_to(work[p][k : k + 1, :], shape) * inverse
            row_other = jnp.broadcast_to(other[p][k : k + 1, :], shape) * inverse
            for q in range(p, blocks):
                column = columns[q - p]
                if q == p:
                    column = jnp.where(sub > k, column, 0.0)
                work[q] = work[q] - column * row
                other[q] = other[q] - column * row_other
            root = lax.rsqrt(pivot)
            work[p] = jnp.where(sub == k, work[p] * root, work[p])
            other[p] = jnp.where(sub == k, other[p] * root, other[p])
        for q in range(blocks):
            factor_ref[SUB * q : SUB * (q + 1), :] = jnp.where(
                lane >= sub + SUB * q, work[q], 0.0
            )
        inverse_lower = jnp.concatenate(other, 0) * scale
        count, kept = basis_ref.shape[0], basis_ref.shape[1]
        start = pl.multiple_of(side_ref[0] * kept, SUB)
        for k in range(count):
            basis_ref[k] = lax.dot_general(
                tall_ref[k, pl.ds(start, kept), :],
                inverse_lower,
                (((1,), (1,)), ((), ())),
                precision=lax.Precision.HIGHEST,
                preferred_element_type=jnp.float32,
            )

    return kernel


def f32(*shape):
    return jax.ShapeDtypeStruct(shape, jnp.float32)


VMEM = pl.BlockSpec(memory_space=pltpu.MemorySpace.VMEM)
SMEM = pl.BlockSpec(memory_space=pltpu.MemorySpace.SMEM)


def call(kernel, outs, name, ins, scalars=0, scratch=(), flops=0):
    size = sum(math.prod(x.shape) * 4 for x in (*ins, *outs))
    return pl.pallas_call(
        kernel,
        out_shape=outs,
        in_specs=[SMEM] * scalars + [VMEM] * (len(ins) - scalars),
        out_specs=[VMEM] * len(outs),
        scratch_shapes=list(scratch),
        cost_estimate=pl.CostEstimate(flops=flops, bytes_accessed=size, transcendentals=0),
        name=name,
    )(*ins)


def butterfly(value, axis, last=False):
    count = lax.axis_size(axis)
    if count & (count - 1):
        total = lax.psum(value, axis)
        return (total, jnp.zeros_like(total)) if last else total
    bit = 1
    while bit < count:
        other = lax.ppermute(value, axis, [(i, i ^ bit) for i in range(count)])
        if last and 2 * bit == count:
            return value, other
        value = value + other
        bit *= 2
    return (value, jnp.zeros_like(value)) if last else value


def shards(displacement, velocity, slopes, stretch, moduli, buoyancy, probes):
    comps, layers, x_count, y_count = displacement.shape
    width = probes.shape[2]
    half = x_count // 2
    n_x, n_y = lax.axis_size("gx"), lax.axis_size("gy")
    side = lax.axis_index("gy")
    has = jnp.stack([side > 0, side < n_y - 1]).astype(jnp.float32)
    sides = 1 if n_y == 2 else 2

    def flat(array):
        return array.reshape(array.shape[:-3] + (layers * x_count, y_count))

    def along_x(value, step):
        pairs = [(i, i + step) for i in range(n_x) if 0 <= i + step < n_x]
        return lax.ppermute(value, "gx", pairs)

    def along_y(value):
        if sides == 1:
            return [lax.ppermute(value, "gy", [(0, 1), (1, 0)])]
        return [
            lax.ppermute(value, "gy", [(i, i + s) for i in range(n_y) if 0 <= i + s < n_y])
            for s in (1, -1)
        ]

    def diagonal(value, step):
        def pairs(moves):
            return [
                (i * n_y + k, (i + step) * n_y + k + s)
                for s in moves
                for i in range(n_x)
                for k in range(n_y)
                if 0 <= i + step < n_x and 0 <= k + s < n_y
            ]

        groups = [(1, -1)] if sides == 1 else [(1,), (-1,)]
        return [lax.ppermute(value, ("gx", "gy"), pairs(moves)) for moves in groups]

    u_flat = flat(displacement)
    part = f32(comps, half, layers, y_count)
    packed = f32(comps, layers, y_count)
    corner = f32(layers, y_count)
    low, high, edge, up, down = call(
        begin_kernel, [part, part, packed, corner, corner], "begin", [u_flat]
    )
    metric_rows = f32(5, 2, layers, y_count)
    before_low, before_high, metric, m_first, m_last, m_edge, push = call(
        metric_kernel,
        [
            part, part, f32(5, x_count, layers, y_count), metric_rows, metric_rows,
            f32(5, layers, y_count), f32(x_count, layers, y_count),
        ],
        "metrics",
        [u_flat, flat(velocity), flat(slopes), flat(stretch), flat(moduli), flat(buoyancy)],
    )
    m_below = along_x(m_last, 1)
    m_above = along_x(m_first, -1)
    m_edge_in = along_y(m_edge)

    sketch_rows = x_count // 2 * comps * (layers // 2)
    slab = (x_count, layers, y_count)
    scratch = [
        pltpu.VMEM((comps, 2 * x_count, layers, y_count), jnp.float32),
        pltpu.VMEM((comps, 2 * x_count, layers, y_count), jnp.float32),
        pltpu.VMEM((comps, x_count + 4, layers, y_count), jnp.float32),
        pltpu.VMEM((comps, *slab), jnp.float32),
        pltpu.VMEM((comps, *slab), jnp.float32),
        pltpu.VMEM((sketch_rows, y_count), jnp.float32),
        pltpu.VMEM((y_count, width), jnp.float32),
    ]
    sketch = []
    for moment in range(STEPS):
        last = moment == STEPS - 1
        below = along_x(high, 1)
        above = along_x(low, -1)
        edge_in = along_y(edge)
        up_in = diagonal(up, 1)
        down_in = diagonal(down, -1)
        outs = [f32(comps, layers * x_count, y_count)] if last else [part, part, packed, corner, corner]
        outs = outs + [f32(sketch_rows, width)]
        results = call(
            make_step(sides, moment == 0, last),
            outs,
            f"step_{moment}",
            [
                has, low, high, below, above, before_low, before_high, metric, push, m_below,
                m_above, edge, *edge_in, *up_in, *down_in, m_edge, *m_edge_in, probes[moment],
                *sketch,
            ],
            scalars=1,
            scratch=scratch,
            flops=30_000_000,
        )
        sketch = [results[-1]]
        if not last:
            before_low, before_high = low, high
            low, high, edge, up, down = results[:-1]
    final = results[0].reshape(displacement.shape)

    mine, theirs = butterfly(sketch[0], "gy", last=True)
    tall, gram = call(
        gram_kernel, [f32(sketch_rows, width), f32(width, width)], "gram", [mine, theirs]
    )
    gram = butterfly(gram, "gx")
    depth = comps * (layers // 2)
    rows_total = sketch_rows * n_x
    basis, factor = call(
        factor_kernel(math.sqrt(rows_total)),
        [f32(x_count // 2, depth // n_y, width), f32(width, width)],
        "factor",
        [side.reshape(1).astype(jnp.int32), gram, tall.reshape(x_count // 2, depth, width)],
        scalars=1,
    )
    return (final, basis, factor)


def solution(mesh):
    in_specs = (
        P(None, None, "gx", "gy"),
        P(None, None, "gx", "gy"),
        P(None, None, "gx", "gy"),
        P(None, "gx", "gy"),
        P(None, None, "gx", "gy"),
        P(None, "gx", "gy"),
        P(None, "gy", None),
    )
    out_specs = (P(None, None, "gx", "gy"), P("gx", "gy", None), P())
    return jax.shard_map(shards, mesh=mesh, in_specs=in_specs, out_specs=out_specs, check_vma=False)
```

```python
import math

import jax
import jax.numpy as jnp
from jax import lax
from jax.experimental import pallas as pl
from jax.experimental.pallas import tpu as pltpu
from jax.sharding import PartitionSpec as P

STEPS = 4
SUB = 8

time_step = 0.12


def roll(value, shift, axis=-1):
    axis = axis % value.ndim
    shift = shift % value.shape[axis]
    return value if shift == 0 else pltpu.roll(value, shift, axis)


def lanes_of(shape):
    return lax.broadcasted_iota(jnp.int32, shape, len(shape) - 1)


def layer_derivative(value):
    groups = value.shape[0] // SUB
    parts = [value[SUB * v : SUB * (v + 1)] for v in range(groups)]
    sub = lax.broadcasted_iota(jnp.int32, parts[0].shape, 0)
    shifted = {}

    def at(v):
        if 0 <= v < groups:
            return parts[v]
        if v not in shifted:
            if v >= groups:
                shifted[v] = jnp.where(sub < SUB - 1, roll(parts[v - groups], -1, 0), 0.0)
            else:
                shifted[v] = jnp.where(sub > 0, roll(parts[v + groups], 1, 0), 0.0)
        return shifted[v]

    return jnp.concatenate(
        [at(v - 2) - at(v + 2) + 8.0 * (at(v + 1) - at(v - 1)) for v in range(groups)], 0
    )


def band_matrix(count):
    row = lax.broadcasted_iota(jnp.int32, (count, count), 0)
    col = lax.broadcasted_iota(jnp.int32, (count, count), 1)
    away = row - col
    band = jnp.where(
        away == -2,
        1.0,
        jnp.where(away == 2, -1.0, jnp.where(away == 1, 8.0, jnp.where(away == -1, -8.0, 0.0))),
    )
    return band.astype(jnp.bfloat16)


def banded(value, band):
    high = value.astype(jnp.bfloat16)
    low = (value - high.astype(jnp.float32)).astype(jnp.bfloat16)
    return jnp.dot(high, band, preferred_element_type=jnp.float32) + jnp.dot(
        low, band, preferred_element_type=jnp.float32
    )


def edge_terms(edge, window):
    w = lanes_of(edge.shape) % window
    up_2, up_3 = roll(edge, 2), roll(edge, 3)
    down_2, down_3 = roll(edge, -2), roll(edge, -3)
    right = jnp.where(w == 7, 8.0 * up_3, 0.0) - up_2
    left = down_2 - jnp.where(w == 8, 8.0 * down_3, 0.0)
    return jnp.where((w == 6) | (w == 7), right, left)


def edge_spread(terms, place, window):
    count = terms.shape[-1]
    lane = lanes_of(terms.shape)
    return jnp.where((lane < 2) | (lane >= count - 2), roll(terms, count - 2 - window * place - 6), 0.0)


def edge_message(load, x_count, rows, y_count, which=None):
    window = y_count // x_count
    place = lanes_of((rows, y_count)) // window
    message = None
    for x in which or range(x_count):
        moved = roll(load(x), window * x + 4)
        message = moved if message is None else jnp.where(place == x, moved, message)
    return message


def edge_tile(own, from_left, from_right, has_left, has_right, window):
    w = lanes_of(own.shape) % window
    halo = jnp.where(w < 8, from_right * has_right, roll(from_left, 8) * has_left)
    mine = jnp.where(w < 4, own, roll(own, 8))
    return jnp.where((w >= 4) & (w < 12), halo, mine)


def begin_kernel(u_ref, low_ref, high_ref, edge_ref):
    comps, half, rows, y_count = low_ref.shape
    x_count = 2 * half
    window = y_count // x_count
    groups = rows // SUB
    for c in range(comps):

        def load(x):
            return jnp.concatenate(
                [
                    u_ref[c, pl.ds(x_count * v + x, SUB, stride=groups * x_count), :]
                    for v in range(groups)
                ],
                0,
            )

        slabs = [load(x) for x in range(x_count)]
        for x in range(x_count):
            (low_ref if x < half else high_ref)[c, x % half] = slabs[x]
        edge_ref[c] = edge_message(lambda x: slabs[x], x_count, rows, y_count)


def corner_kernel(below_ref, above_ref, corner_ref):
    half, rows, y_count = below_ref.shape[1:]
    x_count = 2 * half
    for c in range(corner_ref.shape[0]):

        def load(x):
            return below_ref[c, x - half] if x >= half else above_ref[c, x]

        corner_ref[c] = edge_message(load, x_count, rows, y_count, (0, 1, x_count - 2, x_count - 1))


def metric_kernel(
    u_ref, v_ref, slope_ref, stretch_ref, moduli_ref, buoyancy_ref,
    before_low, before_high, metric_ref, first_ref, last_ref, edge_ref, push_ref,
):
    comps, half, rows, y_count = before_low.shape
    x_count = 2 * half
    groups = rows // SUB

    def load(ref, *index):
        def at(x):
            return jnp.concatenate(
                [
                    ref[(*index, pl.ds(x_count * v + x, SUB, stride=groups * x_count), slice(None))]
                    for v in range(groups)
                ],
                0,
            )

        return at

    fields = [
        (load(slope_ref, 0), 1.0),
        (load(slope_ref, 1), 1.0),
        (load(stretch_ref), 1.0),
        (load(moduli_ref, 0), 1.0 / 12.0),
        (load(moduli_ref, 1), 1.0 / 12.0),
    ]
    for m, (at, scale) in enumerate(fields):
        slabs = [at(x) * scale if scale != 1.0 else at(x) for x in range(x_count)]
        for x in range(x_count):
            metric_ref[m, x] = slabs[x]
        for k in range(2):
            first_ref[m, k] = slabs[k]
            last_ref[m, k] = slabs[x_count - 2 + k]
        edge_ref[m] = edge_message(lambda x: slabs[x], x_count, rows, y_count)
    at = load(buoyancy_ref)
    for x in range(x_count):
        push_ref[x] = at(x) * (time_step**2 / 12.0)
    for c in range(comps):
        at, rate = load(u_ref, c), load(v_ref, c)
        for x in range(x_count):
            (before_low if x < half else before_high)[c, x % half] = at(x) - time_step * rate(x)


def all_stresses(grads, lame, shear):
    pressure = lame * (grads[0][0] + grads[1][1] + grads[2][2])
    twice = shear + shear
    return (
        pressure + twice * grads[0][0],
        pressure + twice * grads[1][1],
        pressure + twice * grads[2][2],
        shear * (grads[0][1] + grads[1][0]),
        shear * (grads[0][2] + grads[2][0]),
        shear * (grads[1][2] + grads[2][1]),
    )


def make_step(sides, first_step, last_step):
    def kernel(*refs):
        refs = list(refs)

        def take(count):
            out = refs[:count]
            del refs[:count]
            return out

        (side_ref,) = take(1)
        low_ref, high_ref, below_ref, above_ref = take(4)
        before_low, before_high = take(2)
        metric_ref, push_ref, metric_below, metric_above = take(4)
        (edge_ref,) = take(1)
        edge_in = take(sides)
        corner_in = take(sides)
        (metric_edge,) = take(1)
        metric_edge_in = take(sides)
        (probe_ref,) = take(1)
        sketch_in = None if first_step else take(1)[0]
        if last_step:
            out_ref, sketch_ref = take(2)
        else:
            out_low, out_high, out_edge, sketch_ref = take(4)
        ext, dyu, s_x, s_o, dys, rates, spread_probe = take(7)

        comps, half, rows, y_count = low_ref.shape
        x_count = 2 * half
        window = y_count // x_count
        groups = rows // SUB
        has_left, has_right = side_ref[0], side_ref[1]
        band = band_matrix(y_count)
        edge_shape = (rows, y_count)
        lane = lanes_of(edge_shape)
        w = lane % window
        place = lane // window

        for c in range(comps):
            for k in range(half):
                ext[c, k] = below_ref[c, k]
                ext[c, half + k] = low_ref[c, k]
                ext[c, 2 * half + k] = high_ref[c, k]
                ext[c, 3 * half + k] = above_ref[c, k]

        edges, corners = [], []
        for c in range(comps):
            edge = edge_tile(edge_ref[c], edge_in[0][c], edge_in[-1][c], has_left, has_right, window)
            if c < 2:
                corner = jnp.where(
                    w < 8, corner_in[-1][c] * has_right, roll(corner_in[0][c], 8) * has_left
                )
                corner_add = edge_terms(corner, window)
            else:
                corner = corner_add = None
            edges.append(edge)
            corners.append(corner)
            edge_add = edge_terms(edge, window)
            first, count = (half - 2, x_count + 4) if c < 2 else (half, x_count)
            flat = ext[c, first : first + count].reshape(count * rows, y_count)
            result = banded(flat, band)
            for k in range(count):
                x = first + k - half
                terms = edge_add if 0 <= x < x_count else corner_add
                dyu[c, first + k] = result[k * rows : (k + 1) * rows] + edge_spread(
                    terms, x % x_count, window
                )

        def gradients(at, metric, full):
            slope_x, slope_y, stretch = metric[:3]
            grads = []
            for c in range(comps):
                dr = layer_derivative(ext[c, at])
                dx = ext[c, at - 2] - ext[c, at + 2] + 8.0 * (ext[c, at + 1] - ext[c, at - 1])
                row = [dx + slope_x * dr, None, stretch * dr]
                if full or c < 2:
                    row[1] = dyu[c, at] + slope_y * dr
                else:
                    row[1] = dr
                grads.append(row)
            return grads

        def tile_row(x, carry):
            metric = [metric_ref[m, x] for m in range(5)]
            grads = gradients(x + half, metric, True)
            s11, s22, s33, s12, s13, s23 = all_stresses(grads, metric[3], metric[4])
            s_x[0, x + 2] = s11
            s_x[1, x + 2] = s12
            s_x[2, x + 2] = s13
            s_o[0, x] = s22
            s_o[1, x] = s23
            s_o[2, x] = s33
            return carry

        for k in range(2):
            for source, at in ((metric_below, half - 2 + k), (metric_above, half + x_count + k)):
                metric = [source[m, k] for m in range(5)]
                grads = gradients(at, metric, False)
                s11, _, _, s12, s13, _ = all_stresses(grads, metric[3], metric[4])
                s_x[0, at - half + 2] = s11
                s_x[1, at - half + 2] = s12
                s_x[2, at - half + 2] = s13
        lax.fori_loop(0, x_count, tile_row, 0)

        metric = [
            edge_tile(
                metric_edge[m], metric_edge_in[0][m], metric_edge_in[-1][m],
                has_left, has_right, window,
            )
            for m in range(5)
        ]
        grads = []
        for c in range(comps):
            edge, corner = edges[c], corners[c]

            def along(k):
                inside = (place + k < x_count) if k > 0 else (place + k >= 0)
                return jnp.where(inside, roll(edge, -window * k), roll(corner, -window * k))

            dr = layer_derivative(edge)
            if c < 2:
                dx = along(-2) - along(2) + 8.0 * (along(1) - along(-1))
            else:
                dx = dr
            dy = roll(edge, 2) - roll(edge, -2) + 8.0 * (roll(edge, -1) - roll(edge, 1))
            grads.append([dx + metric[0] * dr, dy + metric[1] * dr, metric[2] * dr])
        _, e22, _, e12, _, e23 = all_stresses(grads, metric[3], metric[4])

        for i, (edge, source) in enumerate(((e12, None), (e22, 0), (e23, 1))):
            value = s_x[1, 2 : 2 + x_count] if source is None else s_o[source]
            result = banded(value.reshape(x_count * rows, y_count), band)
            terms = edge_terms(edge, window)
            for x in range(x_count):
                dys[i, x] = result[x * rows : (x + 1) * rows] + edge_spread(terms, x, window)

        def update(x, keep):
            slope_x, slope_y, stretch = metric_ref[0, x], metric_ref[1, x], metric_ref[2, x]
            push = push_ref[x]
            r11, r12, r13 = (layer_derivative(s_x[k, x + 2]) for k in range(3))
            r22, r23, r33 = (layer_derivative(s_o[k, x]) for k in range(3))
            layers = ((r11, r12, r13), (r12, r22, r23), (r13, r23, r33))
            for c in range(comps):
                force = s_x[c, x] - s_x[c, x + 4] + 8.0 * (s_x[c, x + 3] - s_x[c, x + 1])
                force = force + slope_x * layers[c][0] + dys[c, x]
                force = force + slope_y * layers[c][1] + stretch * layers[c][2]
                keep(c, force * push)

        picked = groups // 2
        messages = [None] * comps
        for x in range(x_count):
            before = before_low if x < half else before_high

            def keep(c, change):
                past = before[c, x % half]
                following = 2.0 * ext[c, half + x] - past + change
                if last_step:
                    for v in range(groups):
                        out_ref[c, pl.ds(x_count * v + x, SUB, stride=groups * x_count), :] = (
                            following[SUB * v : SUB * (v + 1)]
                        )
                else:
                    (out_low if x < half else out_high)[c, x % half] = following
                    moved = roll(following, window * x + 4)
                    messages[c] = moved if x == 0 else jnp.where(place == x, moved, messages[c])
                if x % 2 == 0:
                    rate = (following - past) * (0.5 / time_step)
                    for v in range(0, groups, 2):
                        start = ((x // 2 * comps + c) * picked + v // 2) * SUB
                        rates[start : start + SUB] = rate[SUB * v : SUB * (v + 1)]

            update(x, keep)

        if not last_step:
            for c in range(comps):
                out_edge[c] = messages[c]

        spread_probe[...] = jnp.zeros_like(spread_probe)
        spread_probe[pl.ds(0, y_count // 2, stride=2), :] = probe_ref[...]
        sketch = jnp.dot(
            rates[...],
            spread_probe[...],
            precision=lax.Precision.HIGHEST,
            preferred_element_type=jnp.float32,
        )
        if sketch_in is not None:
            sketch = sketch + sketch_in[...]
        if last_step:
            for k in range(x_count // 2 * comps):
                for v in range(picked):
                    start = (k * picked + v) * SUB
                    sketch_ref[pl.ds(k * picked * SUB + v, SUB, stride=picked), :] = sketch[
                        start : start + SUB
                    ]
        else:
            sketch_ref[...] = sketch

    return kernel


def gram_kernel(first_ref, second_ref, sum_ref, gram_ref):
    total = first_ref[...] + second_ref[...]
    sum_ref[...] = total
    gram_ref[...] = lax.dot_general(
        total,
        total,
        (((0,), (0,)), ((), ())),
        precision=lax.Precision.HIGHEST,
        preferred_element_type=jnp.float32,
    )


def factor_kernel(scale):
    def kernel(side_ref, gram_ref, tall_ref, basis_ref, factor_ref):
        order = gram_ref.shape[0]
        blocks = order // SUB
        shape = (SUB, order)
        sub = lax.broadcasted_iota(jnp.int32, shape, 0)
        lane = lanes_of(shape)
        work = [gram_ref[SUB * q : SUB * (q + 1), :] for q in range(blocks)]
        other = [jnp.where(lane == sub + SUB * q, 1.0, 0.0) for q in range(blocks)]
        for j in range(order):
            p, k = divmod(j, SUB)
            columns = [jnp.broadcast_to(work[q][:, j : j + 1], shape) for q in range(p, blocks)]
            pivot = jnp.broadcast_to(columns[0][k : k + 1, :], shape)
            inverse = 1.0 / pivot
            row = jnp.broadcast_to(work[p][k : k + 1, :], shape) * inverse
            row_other = jnp.broadcast_to(other[p][k : k + 1, :], shape) * inverse
            for q in range(p, blocks):
                column = columns[q - p]
                if q == p:
                    column = jnp.where(sub > k, column, 0.0)
                work[q] = work[q] - column * row
                other[q] = other[q] - column * row_other
            root = lax.rsqrt(pivot)
            work[p] = jnp.where(sub == k, work[p] * root, work[p])
            other[p] = jnp.where(sub == k, other[p] * root, other[p])
        for q in range(blocks):
            factor_ref[SUB * q : SUB * (q + 1), :] = jnp.where(
                lane >= sub + SUB * q, work[q], 0.0
            )
        inverse_lower = jnp.concatenate(other, 0) * scale
        count, kept = basis_ref.shape[0], basis_ref.shape[1]
        start = pl.multiple_of(side_ref[0] * kept, SUB)
        for k in range(count):
            basis_ref[k] = lax.dot_general(
                tall_ref[k, pl.ds(start, kept), :],
                inverse_lower,
                (((1,), (1,)), ((), ())),
                precision=lax.Precision.HIGHEST,
                preferred_element_type=jnp.float32,
            )

    return kernel


def f32(*shape):
    return jax.ShapeDtypeStruct(shape, jnp.float32)


VMEM = pl.BlockSpec(memory_space=pltpu.MemorySpace.VMEM)
SMEM = pl.BlockSpec(memory_space=pltpu.MemorySpace.SMEM)


def call(kernel, outs, name, ins, scalars=0, scratch=(), flops=0):
    size = sum(math.prod(x.shape) * 4 for x in (*ins, *outs))
    return pl.pallas_call(
        kernel,
        out_shape=outs,
        in_specs=[SMEM] * scalars + [VMEM] * (len(ins) - scalars),
        out_specs=[VMEM] * len(outs),
        scratch_shapes=list(scratch),
        compiler_params=pltpu.CompilerParams(vmem_limit_bytes=24 * 2**20),
        cost_estimate=pl.CostEstimate(flops=flops, bytes_accessed=size, transcendentals=0),
        name=name,
    )(*ins)


def butterfly(value, axis, last=False):
    count = lax.axis_size(axis)
    if count & (count - 1):
        total = lax.psum(value, axis)
        return (total, jnp.zeros_like(total)) if last else total
    bit = 1
    while bit < count:
        other = lax.ppermute(value, axis, [(i, i ^ bit) for i in range(count)])
        if last and 2 * bit == count:
            return value, other
        value = value + other
        bit *= 2
    return (value, jnp.zeros_like(value)) if last else value


def shards(displacement, velocity, slopes, stretch, moduli, buoyancy, probes):
    comps, layers, x_count, y_count = displacement.shape
    width = probes.shape[2]
    half = x_count // 2
    n_x, n_y = lax.axis_size("gx"), lax.axis_size("gy")
    side = lax.axis_index("gy")
    has = jnp.stack([side > 0, side < n_y - 1]).astype(jnp.float32)
    sides = 1 if n_y == 2 else 2

    def flat(array):
        return array.reshape(array.shape[:-3] + (layers * x_count, y_count))

    def along_x(value, step):
        pairs = [(i, i + step) for i in range(n_x) if 0 <= i + step < n_x]
        return lax.ppermute(value, "gx", pairs)

    def along_y(value):
        if sides == 1:
            return [lax.ppermute(value, "gy", [(0, 1), (1, 0)])]
        return [
            lax.ppermute(value, "gy", [(i, i + s) for i in range(n_y) if 0 <= i + s < n_y])
            for s in (1, -1)
        ]

    u_flat = flat(displacement)
    part = f32(comps, half, layers, y_count)
    packed = f32(comps, layers, y_count)
    low, high, edge = call(begin_kernel, [part, part, packed], "begin", [u_flat])
    metric_rows = f32(5, 2, layers, y_count)
    before_low, before_high, metric, m_first, m_last, m_edge, push = call(
        metric_kernel,
        [
            part, part, f32(5, x_count, layers, y_count), metric_rows, metric_rows,
            f32(5, layers, y_count), f32(x_count, layers, y_count),
        ],
        "metrics",
        [u_flat, flat(velocity), flat(slopes), flat(stretch), flat(moduli), flat(buoyancy)],
    )
    m_below = along_x(m_last, 1)
    m_above = along_x(m_first, -1)
    m_edge_in = along_y(m_edge)

    sketch_rows = x_count // 2 * comps * (layers // 2)
    slab = (x_count, layers, y_count)
    scratch = [
        pltpu.VMEM((comps, 2 * x_count, layers, y_count), jnp.float32),
        pltpu.VMEM((comps, 2 * x_count, layers, y_count), jnp.float32),
        pltpu.VMEM((comps, x_count + 4, layers, y_count), jnp.float32),
        pltpu.VMEM((comps, *slab), jnp.float32),
        pltpu.VMEM((comps, *slab), jnp.float32),
        pltpu.VMEM((sketch_rows, y_count), jnp.float32),
        pltpu.VMEM((y_count, width), jnp.float32),
    ]
    sketch = []
    for moment in range(STEPS):
        last = moment == STEPS - 1
        below = along_x(high, 1)
        above = along_x(low, -1)
        edge_in = along_y(edge)
        (corner,) = call(
            corner_kernel, [f32(2, layers, y_count)], f"corner_{moment}", [below, above]
        )
        corner_in = along_y(corner)
        outs = [f32(comps, layers * x_count, y_count)] if last else [part, part, packed]
        outs = outs + [f32(sketch_rows, width)]
        results = call(
            make_step(sides, moment == 0, last),
            outs,
            f"step_{moment}",
            [
                has, low, high, below, above, before_low, before_high, metric, push, m_below,
                m_above, edge, *edge_in, *corner_in, m_edge, *m_edge_in, probes[moment],
                *sketch,
            ],
            scalars=1,
            scratch=scratch,
            flops=30_000_000,
        )
        sketch = [results[-1]]
        if not last:
            before_low, before_high = low, high
            low, high, edge = results[:-1]
    final = results[0].reshape(displacement.shape)

    mine, theirs = butterfly(sketch[0], "gy", last=True)
    tall, gram = call(
        gram_kernel, [f32(sketch_rows, width), f32(width, width)], "gram", [mine, theirs]
    )
    gram = butterfly(gram, "gx")
    depth = comps * (layers // 2)
    rows_total = sketch_rows * n_x
    basis, factor = call(
        factor_kernel(math.sqrt(rows_total)),
        [f32(x_count // 2, depth // n_y, width), f32(width, width)],
        "factor",
        [side.reshape(1).astype(jnp.int32), gram, tall.reshape(x_count // 2, depth, width)],
        scalars=1,
    )
    return (final, basis, factor)


def solution(mesh):
    in_specs = (
        P(None, None, "gx", "gy"),
        P(None, None, "gx", "gy"),
        P(None, None, "gx", "gy"),
        P(None, "gx", "gy"),
        P(None, None, "gx", "gy"),
        P(None, "gx", "gy"),
        P(None, "gy", None),
    )
    out_specs = (P(None, None, "gx", "gy"), P("gx", "gy", None), P())
    return jax.shard_map(shards, mesh=mesh, in_specs=in_specs, out_specs=out_specs, check_vma=False)
```

```python
import math
from functools import partial

import jax
import jax.numpy as jnp
from jax import lax
from jax.experimental import pallas as pl
from jax.experimental.pallas import tpu as pltpu
from jax.sharding import PartitionSpec as P

STEPS = 4
SUB = 8

time_step = 0.12


def roll(value, shift, axis=-1):
    axis = axis % value.ndim
    shift = shift % value.shape[axis]
    return value if shift == 0 else pltpu.roll(value, shift, axis)


def lanes_of(shape):
    return lax.broadcasted_iota(jnp.int32, shape, len(shape) - 1)


def layer_derivative(value):
    groups = value.shape[0] // SUB
    parts = [value[SUB * v : SUB * (v + 1)] for v in range(groups)]
    sub = lax.broadcasted_iota(jnp.int32, parts[0].shape, 0)
    shifted = {}

    def at(v):
        if 0 <= v < groups:
            return parts[v]
        if v not in shifted:
            if v >= groups:
                shifted[v] = jnp.where(sub < SUB - 1, roll(parts[v - groups], -1, 0), 0.0)
            else:
                shifted[v] = jnp.where(sub > 0, roll(parts[v + groups], 1, 0), 0.0)
        return shifted[v]

    return jnp.concatenate(
        [at(v - 2) - at(v + 2) + 8.0 * (at(v + 1) - at(v - 1)) for v in range(groups)], 0
    )


def band_matrix(count):
    row = lax.broadcasted_iota(jnp.int32, (count, count), 0)
    col = lax.broadcasted_iota(jnp.int32, (count, count), 1)
    away = row - col
    band = jnp.where(
        away == -2,
        1.0,
        jnp.where(away == 2, -1.0, jnp.where(away == 1, 8.0, jnp.where(away == -1, -8.0, 0.0))),
    )
    return band.astype(jnp.bfloat16)


def banded(value, band):
    high = value.astype(jnp.bfloat16)
    low = (value - high.astype(jnp.float32)).astype(jnp.bfloat16)
    return jnp.dot(high, band, preferred_element_type=jnp.float32) + jnp.dot(
        low, band, preferred_element_type=jnp.float32
    )


def edge_terms(edge, window):
    w = lanes_of(edge.shape) % window
    up_2, up_3 = roll(edge, 2), roll(edge, 3)
    down_2, down_3 = roll(edge, -2), roll(edge, -3)
    right = jnp.where(w == 7, 8.0 * up_3, 0.0) - up_2
    left = down_2 - jnp.where(w == 8, 8.0 * down_3, 0.0)
    return jnp.where((w == 6) | (w == 7), right, left)


def edge_spread(terms, place, window):
    count = terms.shape[-1]
    lane = lanes_of(terms.shape)
    return jnp.where((lane < 2) | (lane >= count - 2), roll(terms, count - 2 - window * place - 6), 0.0)


def edge_message(load, x_count, rows, y_count, which=None):
    window = y_count // x_count
    place = lanes_of((rows, y_count)) // window
    message = None
    for x in which or range(x_count):
        moved = roll(load(x), window * x + 4)
        message = moved if message is None else jnp.where(place == x, moved, message)
    return message


def neighbours():
    at = lax.axis_index("gy")
    return (at > 0).astype(jnp.float32), (at < lax.axis_size("gy") - 1).astype(jnp.float32)


def edge_tile(own, from_left, from_right, has_left, has_right, window):
    w = lanes_of(own.shape) % window
    halo = jnp.where(w < 8, from_right * has_right, roll(from_left, 8) * has_left)
    mine = jnp.where(w < 4, own, roll(own, 8))
    return jnp.where((w >= 4) & (w < 12), halo, mine)


def strided(ref, x_count, rows, index=()):
    groups = rows // SUB

    def at(x):
        return jnp.concatenate(
            [
                ref[(*index, pl.ds(x_count * v + x, SUB, stride=groups * x_count), slice(None))]
                for v in range(groups)
            ],
            0,
        )

    return at


def central(far_low, near_low, near_high, far_high):
    def minus(first, second):
        if second is None:
            return first
        return -second if first is None else first - second

    near, far = minus(near_high, near_low), minus(far_low, far_high)
    if near is None:
        return far
    return 8.0 * near if far is None else far + 8.0 * near


def halves(low_ref, high_ref, half):
    def at(c, x):
        return low_ref[c * half + x] if x < half else high_ref[c * half + x - half]

    return at


def begin_kernel(*refs):
    sources, (down_ref, up_ref, edge_ref, metric_ref) = refs[:4], refs[4:8]
    u_ref, slope_ref, stretch_ref, moduli_ref = refs[8:12]
    sems = refs[12]
    copies = [
        pltpu.make_async_copy(source, target, sems.at[i])
        for i, (source, target) in enumerate(zip(sources, refs[8:12]))
    ]
    for copy in copies:
        copy.start()
    copies[0].wait()
    x_count, rows, y_count = metric_ref.shape[1:]
    half = x_count // 2
    comps = u_ref.shape[0]
    for c in range(comps):
        at = strided(u_ref, x_count, rows, (c,))
        slabs = [at(x) for x in range(x_count)]
        for k in range(half):
            down_ref[c * half + k] = slabs[k]
            up_ref[c * half + k] = slabs[half + k]
        edge_ref[c] = edge_message(lambda x: slabs[x], x_count, rows, y_count)
    for copy in copies[1:]:
        copy.wait()
    fields = [
        (strided(slope_ref, x_count, rows, (0,)), None),
        (strided(slope_ref, x_count, rows, (1,)), None),
        (strided(stretch_ref, x_count, rows), None),
        (strided(moduli_ref, x_count, rows, (0,)), 1.0 / 12.0),
        (strided(moduli_ref, x_count, rows, (1,)), 1.0 / 12.0),
    ]
    for m, (at, scale) in enumerate(fields):
        slabs = [at(x) if scale is None else at(x) * scale for x in range(x_count)]
        for x in range(x_count):
            metric_ref[m, x] = slabs[x]
        for k in range(2):
            down_ref[comps * half + 2 * m + k] = slabs[k]
            up_ref[comps * half + 2 * m + k] = slabs[x_count - 2 + k]
        edge_ref[comps + m] = edge_message(lambda x: slabs[x], x_count, rows, y_count)


def rest_kernel(u_ref, v_ref, buoyancy_ref, before_low, before_high, push_ref):
    x_count, rows, _ = push_ref.shape
    half = x_count // 2
    at = strided(buoyancy_ref, x_count, rows)
    for x in range(x_count):
        push_ref[x] = at(x) * (time_step**2 / 12.0)
    for c in range(u_ref.shape[0]):
        at, rate = strided(u_ref, x_count, rows, (c,)), strided(v_ref, x_count, rows, (c,))
        for x in range(x_count):
            (before_low if x < half else before_high)[c * half + x % half] = (
                at(x) - time_step * rate(x)
            )


def corner_kernel(half, below_ref, above_ref, *refs):
    corner_ref = refs[-1]
    rows, y_count = below_ref.shape[1:]
    x_count = 2 * half
    for c in range(corner_ref.shape[0]):

        def load(x):
            return below_ref[c * half + x - half] if x >= half else above_ref[c * half + x]

        corner_ref[c] = edge_message(load, x_count, rows, y_count, (0, 1, x_count - 2, x_count - 1))


def all_stresses(grads, lame, shear):
    pressure = lame * (grads[0][0] + grads[1][1] + grads[2][2])
    twice = shear + shear
    return (
        pressure + twice * grads[0][0],
        pressure + twice * grads[1][1],
        pressure + twice * grads[2][2],
        shear * (grads[0][1] + grads[1][0]),
        shear * (grads[0][2] + grads[2][0]),
        shear * (grads[1][2] + grads[2][1]),
    )


def tile_kernel(sides, comps, *refs):
    low_ref, high_ref, edge_ref = refs[:3]
    edge_in = refs[3 : 3 + sides]
    metric_ref, first_edge = refs[3 + sides : 5 + sides]
    first_edge_in = refs[5 + sides : 5 + 2 * sides]
    s_x, s_o, e_s = refs[5 + 2 * sides :]
    x_count, rows, y_count = metric_ref.shape[1:]
    half, window = x_count // 2, y_count // x_count
    has_left, has_right = neighbours()
    place = lanes_of((rows, y_count)) // window
    u = halves(low_ref, high_ref, half)
    band = band_matrix(y_count)

    edges, across = [], []
    for c in range(comps):
        edge = edge_tile(edge_ref[c], edge_in[0][c], edge_in[-1][c], has_left, has_right, window)
        terms = edge_terms(edge, window)
        result = banded(jnp.concatenate([u(c, x) for x in range(x_count)], 0), band)
        edges.append(edge)
        across.append(
            [
                result[x * rows : (x + 1) * rows] + edge_spread(terms, x, window)
                for x in range(x_count)
            ]
        )

    def gradients(along, beside, layers, metric):
        return [
            [
                along[c] + metric[0] * layers[c],
                beside[c] + metric[1] * layers[c],
                metric[2] * layers[c],
            ]
            for c in range(comps)
        ]

    for x in range(x_count):
        metric = [metric_ref[m, x] for m in range(5)]

        def near(c, k):
            return u(c, x + k) if 0 <= x + k < x_count else None

        along = [central(*(near(c, k) for k in (-2, -1, 1, 2))) for c in range(comps)]
        layers = [layer_derivative(u(c, x)) for c in range(comps)]
        grads = gradients(along, [across[c][x] for c in range(comps)], layers, metric)
        s11, s22, s33, s12, s13, s23 = all_stresses(grads, metric[3], metric[4])
        s_x[0, x], s_x[1, x], s_x[2, x] = s11, s12, s13
        s_o[0, x], s_o[1, x], s_o[2, x] = s22, s23, s33

    metric = [
        edge_tile(
            first_edge[comps + m], first_edge_in[0][comps + m], first_edge_in[-1][comps + m],
            has_left, has_right, window,
        )
        for m in range(5)
    ]
    along, beside = [], []
    for edge in edges:

        def near(k):
            inside = (place + k < x_count) if k > 0 else (place + k >= 0)
            return jnp.where(inside, roll(edge, -window * k), 0.0)

        along.append(central(*(near(k) for k in (-2, -1, 1, 2))))
        beside.append(central(*(roll(edge, -k) for k in (-2, -1, 1, 2))))
    grads = gradients(along, beside, [layer_derivative(edge) for edge in edges], metric)
    _, e22, _, e12, _, e23 = all_stresses(grads, metric[3], metric[4])
    e_s[0], e_s[1], e_s[2], e_s[3], e_s[4] = e12, e22, e23, metric[3], metric[4]


def wide_kernel(
    low_ref, high_ref, below_ref, above_ref, before_low, before_high, metric_ref, push_ref,
    first_below, first_above, s_x, s_o, e_s, out_low, out_high, out_edge,
):
    x_count, rows, y_count = metric_ref.shape[1:]
    half, window = x_count // 2, y_count // x_count
    comps = s_x.shape[0]
    inner = halves(low_ref, high_ref, half)
    past = halves(before_low, before_high, half)
    band = band_matrix(y_count)

    def u(c, x):
        if x < 0:
            return below_ref[c * half + half + x]
        return above_ref[c * half + x - x_count] if x >= x_count else inner(c, x)

    along_x, others = {}, {}
    for x in range(x_count):
        near = {k: x + k for k in (-2, -1, 1, 2) if not 0 <= x + k < x_count}
        values = [s_x[i, x] for i in range(3)]
        rest = [s_o[i, x] for i in range(3)]
        if near:
            add = [
                central(*(u(c, near[k]) if k in near else None for k in (-2, -1, 1, 2)))
                for c in range(comps)
            ]
            lame, shear = metric_ref[3, x], metric_ref[4, x]
            pressure = lame * add[0]
            values[0] = values[0] + pressure + (shear + shear) * add[0]
            values[1] = values[1] + shear * add[1]
            values[2] = values[2] + shear * add[2]
            rest[0] = rest[0] + pressure
            rest[2] = rest[2] + pressure
        along_x[x], others[x] = values, rest

    outside = (-2, -1, x_count, x_count + 1)
    across = [
        banded(jnp.concatenate([u(c, x) for x in outside], 0), band) for c in range(2)
    ]
    for place, x in enumerate(outside):
        source, k = (first_below, place) if x < 0 else (first_above, place - 2)
        slope_x, slope_y, stretch, lame, shear = (
            source[comps * half + 2 * m + k] for m in range(5)
        )
        dr = [layer_derivative(u(c, x)) for c in range(comps)]
        dx = [central(*(u(c, x + j) for j in (-2, -1, 1, 2))) for c in range(comps)]
        dy = [across[c][place * rows : (place + 1) * rows] for c in range(2)]
        g11 = dx[0] + slope_x * dr[0]
        pressure = lame * (g11 + dy[1] + slope_y * dr[1] + stretch * dr[2])
        along_x[x] = [
            pressure + (shear + shear) * g11,
            shear * (dy[0] + slope_y * dr[0] + dx[1] + slope_x * dr[1]),
            shear * (stretch * dr[0] + dx[2] + slope_x * dr[2]),
        ]

    def across_of(i, x):
        return along_x[x][1] if i == 0 else others[x][i - 1]

    beside = []
    for i in range(comps):
        result = banded(jnp.concatenate([across_of(i, x) for x in range(x_count)], 0), band)
        terms = edge_terms(e_s[i], window)
        beside.append(
            [
                result[x * rows : (x + 1) * rows] + edge_spread(terms, x, window)
                for x in range(x_count)
            ]
        )

    place = lanes_of((rows, y_count)) // window
    messages = [None] * comps
    for x in range(x_count):
        slope_x, slope_y, stretch = (metric_ref[m, x] for m in range(3))
        r11, r12, r13 = (layer_derivative(value) for value in along_x[x])
        r22, r23, r33 = (layer_derivative(value) for value in others[x])
        layers = ((r11, r12, r13), (r12, r22, r23), (r13, r23, r33))
        for c in range(comps):
            force = central(*(along_x[x + k][c] for k in (-2, -1, 1, 2))) + beside[c][x]
            force = force + slope_x * layers[c][0] + slope_y * layers[c][1]
            force = force + stretch * layers[c][2]
            following = 2.0 * u(c, x) - past(c, x) + force * push_ref[x]
            (out_low if x < half else out_high)[c * half + x % half] = following
            moved = roll(following, window * x + 4)
            messages[c] = moved if x == 0 else jnp.where(place == x, moved, messages[c])
    for c in range(comps):
        out_edge[c] = messages[c]


def fix_kernel(sides, *refs):
    corner_in = refs[:sides]
    first_below, first_above, e_s, push_ref, low_ref, high_ref, edge_ref = refs[sides : 7 + sides]
    out_low, out_high, *out_edge = refs[7 + sides :]
    x_count, rows, y_count = push_ref.shape
    half, window = x_count // 2, y_count // x_count
    comps = edge_ref.shape[0]
    has_left, has_right = neighbours()
    lane = lanes_of((rows, y_count))
    place, w = lane // window, lane % window
    lame, shear = 3, 4

    corners = [
        jnp.where(w < 8, corner_in[-1][c] * has_right, roll(corner_in[0][c], 8) * has_left)
        for c in range(2)
    ]
    terms = [edge_terms(corner, window) for corner in corners]

    def edge_change(corner):
        def near(k):
            inside = (place + k < x_count) if k > 0 else (place + k >= 0)
            return jnp.where(inside, 0.0, roll(corner, -window * k))

        return central(*(near(k) for k in (-2, -1, 1, 2)))

    beside = [
        edge_terms(e_s[shear] * edge_change(corners[1]), window),
        edge_terms(e_s[lame] * edge_change(corners[0]), window),
    ]

    def stress_change(c, x):
        source, k = (first_below, x + 2) if x < 0 else (first_above, x - x_count)
        modulus = source[comps * half + 2 * (lame if c == 0 else shear) + k]
        return modulus * edge_spread(terms[1 - c], x % x_count, window)

    for c in range(comps):
        changes = {}
        if c < 2:
            changes = {x: stress_change(c, x) for x in (-2, -1, x_count, x_count + 1)}
        message = edge_ref[c]
        for x in range(x_count):
            at = c * half + x % half
            value = (low_ref if x < half else high_ref)[at]
            near = [changes.get(x + k) for k in (-2, -1, 1, 2)]
            if any(item is not None for item in near):
                change = central(*near) + edge_spread(beside[c], x, window)
                value = value + change * push_ref[x]
                message = jnp.where(place == x, roll(value, window * x + 4), message)
            (out_low if x < half else out_high)[at] = value
        if out_edge:
            out_edge[0][c] = message


def sketch_kernel(moment, last, shape, *refs):
    comps, half, rows, y_count = shape
    low_ref, high_ref, before_low, before_high, probe_ref = refs[:5]
    sketch_in = None if moment == 0 else refs[5]
    sketch_ref, spread = refs[-2:]
    x_count = 2 * half
    groups = rows // SUB
    picked = groups // 2
    now = halves(low_ref, high_ref, half)
    past = halves(before_low, before_high, half)
    spread[...] = jnp.zeros_like(spread)
    spread[pl.ds(0, y_count // 2, stride=2), :] = probe_ref[moment]
    rates = []
    for x in range(0, x_count, 2):
        for c in range(comps):
            rate = (now(c, x) - past(c, x)) * (0.5 / time_step)
            rates += [rate[SUB * v : SUB * (v + 1)] for v in range(0, groups, 2)]
    sketch = jnp.dot(
        jnp.concatenate(rates, 0),
        spread[...],
        precision=lax.Precision.HIGHEST,
        preferred_element_type=jnp.float32,
    )
    if sketch_in is not None:
        sketch = sketch + sketch_in[...]
    if last:
        for k in range(half * comps):
            for v in range(picked):
                start = (k * picked + v) * SUB
                sketch_ref[pl.ds(k * picked * SUB + v, SUB, stride=picked), :] = sketch[
                    start : start + SUB
                ]
    else:
        sketch_ref[...] = sketch


def finish_kernel(half, rows, low_ref, high_ref, out_ref):
    x_count, groups = 2 * half, rows // SUB
    now = halves(low_ref, high_ref, half)
    for c in range(out_ref.shape[0]):
        for x in range(x_count):
            value = now(c, x)
            for v in range(groups):
                out_ref[c, pl.ds(x_count * v + x, SUB, stride=groups * x_count), :] = value[
                    SUB * v : SUB * (v + 1)
                ]


def gram_kernel(first_ref, second_ref, sum_ref, packed_ref):
    total = first_ref[...] + second_ref[...]
    sum_ref[...] = total
    gram = lax.dot_general(
        total,
        total,
        (((0,), (0,)), ((), ())),
        precision=lax.Precision.HIGHEST,
        preferred_element_type=jnp.float32,
    )
    order = gram.shape[0]
    mid = order // 2
    top, bottom = gram[:mid], gram[mid:]
    row = lax.broadcasted_iota(jnp.int32, (mid, order), 0)
    column = lanes_of((mid, order)) - mid
    packed_ref[:mid] = jnp.where((column >= 0) & (row >= column), roll(top, mid), bottom)
    diagonal = jnp.sum(jnp.where(row == column, bottom, 0.0), 0, keepdims=True)
    packed_ref[mid:] = jnp.broadcast_to(diagonal, (packed_ref.shape[0] - mid, order))


def unpacked(packed):
    order = packed.shape[1]
    mid = order // 2
    row = lax.broadcasted_iota(jnp.int32, (mid, order), 0)
    lane = lanes_of((mid, order))
    column = lane - mid
    main = packed[:mid]
    diagonal = jnp.broadcast_to(packed[mid : mid + 1], (mid, order))
    moved = roll(main, mid)
    top = jnp.where(row > lane, moved, jnp.where(row == lane, 0.5 * moved, 0.0))
    bottom = jnp.where(
        (column < 0) | (row < column), main, jnp.where(row == column, 0.5 * diagonal, 0.0)
    )
    part = jnp.concatenate([top, bottom], 0)
    return part + part.T


def factor_kernel(scale, first_ref, second_ref, tall_ref, basis_ref, factor_ref):
    gram = unpacked(first_ref[...] + second_ref[...])
    order = gram.shape[0]
    blocks = order // SUB
    shape = (SUB, order)
    sub = lax.broadcasted_iota(jnp.int32, shape, 0)
    lane = lanes_of(shape)
    work = [gram[SUB * q : SUB * (q + 1)] for q in range(blocks)]
    other = [jnp.where(lane == sub + SUB * q, 1.0, 0.0) for q in range(blocks)]
    inverse_rows = []

    def row_of(value, k):
        return jnp.broadcast_to(value[k : k + 1, :], value.shape)

    def column_of(value, j):
        return jnp.broadcast_to(value[:, j : j + 1], value.shape)

    for p in range(blocks):
        columns = [column_of(work[p], SUB * p + k) for k in range(SUB)]
        ahead = [column_of(work[p + 1], SUB * p + k) for k in range(SUB)] if p + 1 < blocks else []
        upper = solved = work[p]
        lower = solved_other = other[p]
        pivots = inverses = columns[0]
        for k in range(SUB):
            pivot = row_of(columns[k], k)
            inverse = 1.0 / pivot
            every = jnp.where(sub != k, columns[k] * inverse, 0.0)
            after = jnp.where(sub > k, every, 0.0)
            for m in range(k + 1, SUB):
                columns[m] = columns[m] - every * row_of(columns[m], k)
            upper = upper - after * row_of(upper, k)
            lower = lower - after * row_of(lower, k)
            solved = solved - every * row_of(solved, k)
            solved_other = solved_other - every * row_of(solved_other, k)
            pivots = jnp.where(sub == k, pivot, pivots)
            inverses = jnp.where(sub == k, inverse, inverses)
        root = lax.rsqrt(pivots)
        factor_ref[SUB * p : SUB * (p + 1), :] = jnp.where(lane >= sub + SUB * p, upper * root, 0.0)
        inverse_rows.append(lower * root * scale)
        solved, solved_other = solved * inverses, solved_other * inverses
        for k, column in enumerate(ahead):
            work[p + 1] = work[p + 1] - column * row_of(solved, k)
            other[p + 1] = other[p + 1] - column * row_of(solved_other, k)
        if p + 2 < blocks:
            both = jnp.concatenate([solved, solved_other], 1)
            parts = [jnp.zeros((SUB * p, 2 * order), jnp.float32)] if p else []
            parts += [both, jnp.zeros((order - SUB * (p + 1), 2 * order), jnp.float32)]
            change = jnp.dot(
                jnp.concatenate(work[p + 2 :], 0),
                jnp.concatenate(parts, 0),
                precision=lax.Precision.HIGHEST,
                preferred_element_type=jnp.float32,
            )
            for i, q in enumerate(range(p + 2, blocks)):
                work[q] = work[q] - change[SUB * i : SUB * (i + 1), :order]
                other[q] = other[q] - change[SUB * i : SUB * (i + 1), order:]

    inverse_lower = jnp.concatenate(inverse_rows, 0)
    count, kept = basis_ref.shape[0], basis_ref.shape[1]
    start = pl.multiple_of(lax.axis_index("gy") * kept, SUB)
    tall = jnp.concatenate([tall_ref[k, pl.ds(start, kept), :] for k in range(count)], 0)
    basis = lax.dot_general(
        tall,
        inverse_lower,
        (((1,), (1,)), ((), ())),
        precision=lax.Precision.HIGHEST,
        preferred_element_type=jnp.float32,
    )
    for k in range(count):
        basis_ref[k] = basis[k * kept : (k + 1) * kept]


def f32(*shape):
    return jax.ShapeDtypeStruct(shape, jnp.float32)


VMEM = pl.BlockSpec(memory_space=pltpu.MemorySpace.VMEM)
ANY = pl.BlockSpec(memory_space=pl.ANY)
HBM = pl.BlockSpec(memory_space=pltpu.MemorySpace.HBM)


def call(kernel, outs, name, ins, specs=None, scratch=(), flops=0):
    size = sum(math.prod(x.shape) * 4 for x in (*ins, *outs))
    return pl.pallas_call(
        kernel,
        out_shape=outs,
        in_specs=specs or [VMEM] * len(ins),
        out_specs=[VMEM] * len(outs),
        scratch_shapes=list(scratch),
        compiler_params=pltpu.CompilerParams(vmem_limit_bytes=24 * 2**20),
        cost_estimate=pl.CostEstimate(flops=flops, bytes_accessed=size, transcendentals=0),
        name=name,
    )(*ins)


def butterfly(value, axis, last=False):
    count = lax.axis_size(axis)
    if count & (count - 1):
        total = lax.psum(value, axis)
        return (total, jnp.zeros_like(total)) if last else total
    bit = 1
    while bit < count:
        other = lax.ppermute(value, axis, [(i, i ^ bit) for i in range(count)])
        if last and 2 * bit == count:
            return value, other
        value = value + other
        bit *= 2
    return (value, jnp.zeros_like(value)) if last else value


def shards(displacement, velocity, slopes, stretch, moduli, buoyancy, probes):
    comps, layers, x_count, y_count = displacement.shape
    width = probes.shape[2]
    half = x_count // 2
    n_x, n_y = lax.axis_size("gx"), lax.axis_size("gy")
    sides = 1 if n_y == 2 else 2

    def flat(array):
        return array.reshape(array.shape[:-3] + (layers * x_count, y_count))

    def along_x(value, step):
        pairs = [(i, i + step) for i in range(n_x) if 0 <= i + step < n_x]
        return lax.ppermute(value, "gx", pairs)

    def along_y(value):
        if sides == 1:
            return [lax.ppermute(value, "gy", [(0, 1), (1, 0)])]
        return [
            lax.ppermute(value, "gy", [(i, i + s) for i in range(n_y) if 0 <= i + s < n_y])
            for s in (1, -1)
        ]

    def slabs(count):
        return f32(count, layers, y_count)

    u_flat = flat(displacement)
    fields = [u_flat, flat(slopes), flat(stretch), flat(moduli)]
    down, up, edge, metric = call(
        begin_kernel,
        [slabs(comps * half + 10), slabs(comps * half + 10), slabs(comps + 5), f32(5, x_count, layers, y_count)],
        "begin",
        fields,
        specs=[HBM] * 4,
        scratch=[pltpu.VMEM(field.shape, jnp.float32) for field in fields]
        + [pltpu.SemaphoreType.DMA((4,))],
    )
    before_low, before_high, push = call(
        rest_kernel,
        [slabs(comps * half), slabs(comps * half), slabs(x_count)],
        "rest",
        [u_flat, flat(velocity), flat(buoyancy)],
    )

    low, high = down, up
    sketch_rows = half * comps * (layers // 2)
    sketch = []
    for moment in range(STEPS):
        last = moment == STEPS - 1
        edge_in = along_y(edge)
        above = along_x(low, -1)
        below = along_x(high, 1)
        if moment == 0:
            first_edge, first_edge_in, first_below, first_above = edge, edge_in, below, above
        s_x, s_o, e_s = call(
            partial(tile_kernel, sides, comps),
            [f32(comps, x_count, layers, y_count), f32(3, x_count, layers, y_count), slabs(5)],
            f"tile_{moment}",
            [low, high, edge, *edge_in, metric, first_edge, *first_edge_in],
            flops=20_000_000,
        )
        (corner,) = call(
            partial(corner_kernel, half),
            [slabs(2)],
            f"corner_{moment}",
            [below, above, e_s, *(sketch or [push])],
            specs=[VMEM, VMEM, ANY, ANY],
        )
        corner_in = along_y(corner)
        next_low, next_high, edge = call(
            wide_kernel,
            [slabs(comps * half), slabs(comps * half), slabs(comps)],
            f"wide_{moment}",
            [
                low, high, below, above, before_low, before_high, metric, push, first_below,
                first_above, s_x, s_o, e_s,
            ],
            flops=20_000_000,
        )
        next_low, next_high, *edge = call(
            partial(fix_kernel, sides),
            [slabs(comps * half), slabs(comps * half)] + ([] if last else [slabs(comps)]),
            f"fix_{moment}",
            [*corner_in, first_below, first_above, e_s, push, next_low, next_high, edge],
        )
        sketch = call(
            partial(sketch_kernel, moment, last, (comps, half, layers, y_count)),
            [f32(sketch_rows, width)],
            f"sketch_{moment}",
            [next_low, next_high, before_low, before_high, probes, *sketch],
            scratch=[pltpu.VMEM((y_count, width), jnp.float32)],
        )
        before_low, before_high, low, high = low, high, next_low, next_high
        edge = None if last else edge[0]
    (final,) = call(
        partial(finish_kernel, half, layers),
        [f32(comps, layers * x_count, y_count)],
        "finish",
        [low, high],
    )
    final = final.reshape(displacement.shape)

    mine, theirs = butterfly(sketch[0], "gy", last=True)
    tall, packed = call(
        gram_kernel,
        [f32(sketch_rows, width), f32(width // 2 + SUB, width)],
        "gram",
        [mine, theirs],
    )
    first, second = butterfly(packed, "gx", last=True)
    depth = comps * (layers // 2)
    basis, factor = call(
        partial(factor_kernel, math.sqrt(sketch_rows * n_x)),
        [f32(half, depth // n_y, width), f32(width, width)],
        "factor",
        [first, second, tall.reshape(half, depth, width)],
    )
    return (final, basis, factor)


def solution(mesh):
    in_specs = (
        P(None, None, "gx", "gy"),
        P(None, None, "gx", "gy"),
        P(None, None, "gx", "gy"),
        P(None, "gx", "gy"),
        P(None, None, "gx", "gy"),
        P(None, "gx", "gy"),
        P(None, "gy", None),
    )
    out_specs = (P(None, None, "gx", "gy"), P("gx", "gy", None), P())
    return jax.shard_map(shards, mesh=mesh, in_specs=in_specs, out_specs=out_specs, check_vma=False)
```

```python
import math
from functools import partial

import jax
import jax.numpy as jnp
from jax import lax
from jax.experimental import pallas as pl
from jax.experimental.pallas import tpu as pltpu
from jax.sharding import PartitionSpec as P

STEPS = 4
SUB = 8

time_step = 0.12


def roll(value, shift, axis=-1):
    axis = axis % value.ndim
    shift = shift % value.shape[axis]
    return value if shift == 0 else pltpu.roll(value, shift, axis)


def lanes_of(shape):
    return lax.broadcasted_iota(jnp.int32, shape, len(shape) - 1)


def layer_derivative(value):
    groups = value.shape[0] // SUB
    parts = [value[SUB * v : SUB * (v + 1)] for v in range(groups)]
    sub = lax.broadcasted_iota(jnp.int32, parts[0].shape, 0)
    shifted = {}

    def at(v):
        if 0 <= v < groups:
            return parts[v]
        if v not in shifted:
            if v >= groups:
                shifted[v] = jnp.where(sub < SUB - 1, roll(parts[v - groups], -1, 0), 0.0)
            else:
                shifted[v] = jnp.where(sub > 0, roll(parts[v + groups], 1, 0), 0.0)
        return shifted[v]

    return jnp.concatenate(
        [at(v - 2) - at(v + 2) + 8.0 * (at(v + 1) - at(v - 1)) for v in range(groups)], 0
    )


def band_matrix(count):
    row = lax.broadcasted_iota(jnp.int32, (count, count), 0)
    col = lax.broadcasted_iota(jnp.int32, (count, count), 1)
    away = row - col
    band = jnp.where(
        away == -2,
        1.0,
        jnp.where(away == 2, -1.0, jnp.where(away == 1, 8.0, jnp.where(away == -1, -8.0, 0.0))),
    )
    return band.astype(jnp.bfloat16)


def banded(value, band):
    high = value.astype(jnp.bfloat16)
    low = (value - high.astype(jnp.float32)).astype(jnp.bfloat16)
    return jnp.dot(high, band, preferred_element_type=jnp.float32) + jnp.dot(
        low, band, preferred_element_type=jnp.float32
    )


def edge_terms(edge, window):
    w = lanes_of(edge.shape) % window
    up_2, up_3 = roll(edge, 2), roll(edge, 3)
    down_2, down_3 = roll(edge, -2), roll(edge, -3)
    right = jnp.where(w == 7, 8.0 * up_3, 0.0) - up_2
    left = down_2 - jnp.where(w == 8, 8.0 * down_3, 0.0)
    return jnp.where((w == 6) | (w == 7), right, left)


def edge_spread(terms, place, window):
    count = terms.shape[-1]
    lane = lanes_of(terms.shape)
    return jnp.where((lane < 2) | (lane >= count - 2), roll(terms, count - 2 - window * place - 6), 0.0)


def edge_message(load, x_count, rows, y_count, which=None):
    window = y_count // x_count
    place = lanes_of((rows, y_count)) // window
    message = None
    for x in which or range(x_count):
        moved = roll(load(x), window * x + 4)
        message = moved if message is None else jnp.where(place == x, moved, message)
    return message


def neighbours():
    at = lax.axis_index("gy")
    return (at > 0).astype(jnp.float32), (at < lax.axis_size("gy") - 1).astype(jnp.float32)


def edge_tile(own, from_left, from_right, has_left, has_right, window):
    w = lanes_of(own.shape) % window
    halo = jnp.where(w < 8, from_right * has_right, roll(from_left, 8) * has_left)
    mine = jnp.where(w < 4, own, roll(own, 8))
    return jnp.where((w >= 4) & (w < 12), halo, mine)


def strided(ref, x_count, rows, index=()):
    groups = rows // SUB

    def at(x):
        return jnp.concatenate(
            [
                ref[(*index, pl.ds(x_count * v + x, SUB, stride=groups * x_count), slice(None))]
                for v in range(groups)
            ],
            0,
        )

    return at


def central(far_low, near_low, near_high, far_high):
    def minus(first, second):
        if second is None:
            return first
        return -second if first is None else first - second

    near, far = minus(near_high, near_low), minus(far_low, far_high)
    if near is None:
        return far
    return 8.0 * near if far is None else far + 8.0 * near


def halves(far_ref, near_ref, half):
    def at(c, x):
        return far_ref[c * half + x] if x < half else near_ref[c * half + x - half]

    return at


def is_odd():
    return lax.axis_index("gx") % 2 == 1


def mirrored(values, odd, flip=False):
    other = [-value if flip else value for value in values[::-1]]
    return [jnp.where(odd, second, first) for first, second in zip(values, other)]


class Side:
    def __init__(self, far, x_count):
        self.far, self.half, self.x_count = far, x_count // 2, x_count
        self.inside = range(self.half) if far else range(self.half, x_count)
        self.outside = (-2, -1) if far else (x_count, x_count + 1)

    def depth(self, x):
        return -1 - x if self.far else x - self.x_count

    def halo(self, ref, c, x):
        place = self.depth(x) if self.far else self.half - 1 - self.depth(x)
        value = ref[c * self.half + place]
        return -value if c == 0 else value

    def metric(self, ref, comps, m, x):
        place = self.depth(x) if self.far else 1 - self.depth(x)
        value = ref[comps * self.half + 2 * m + place]
        return -value if m == 0 else value


def begin_kernel(*refs):
    sources, (far_ref, near_ref, edge_ref, metric_ref) = refs[:4], refs[4:8]
    u_ref, slope_ref, stretch_ref, moduli_ref = refs[8:12]
    sems = refs[12]
    copies = [
        pltpu.make_async_copy(source, target, sems.at[i])
        for i, (source, target) in enumerate(zip(sources, refs[8:12]))
    ]
    for copy in copies:
        copy.start()
    copies[0].wait()
    x_count, rows, y_count = metric_ref.shape[1:]
    half = x_count // 2
    comps = u_ref.shape[0]
    odd = is_odd()
    for c in range(comps):
        at = strided(u_ref, x_count, rows, (c,))
        slabs = mirrored([at(x) for x in range(x_count)], odd, c == 0)
        for k in range(half):
            far_ref[c * half + k] = slabs[k]
            near_ref[c * half + k] = slabs[half + k]
        edge_ref[c] = edge_message(lambda x: slabs[x], x_count, rows, y_count)
    for copy in copies[1:]:
        copy.wait()
    fields = [
        (strided(slope_ref, x_count, rows, (0,)), None),
        (strided(slope_ref, x_count, rows, (1,)), None),
        (strided(stretch_ref, x_count, rows), None),
        (strided(moduli_ref, x_count, rows, (0,)), 1.0 / 12.0),
        (strided(moduli_ref, x_count, rows, (1,)), 1.0 / 12.0),
    ]
    for m, (at, scale) in enumerate(fields):
        slabs = mirrored([at(x) for x in range(x_count)], odd, m == 0)
        if scale is not None:
            slabs = [slab * scale for slab in slabs]
        for x in range(x_count):
            metric_ref[m, x] = slabs[x]
        for k in range(2):
            far_ref[comps * half + 2 * m + k] = slabs[k]
            near_ref[comps * half + 2 * m + k] = slabs[x_count - 2 + k]
        edge_ref[comps + m] = edge_message(lambda x: slabs[x], x_count, rows, y_count)


def rest_kernel(u_ref, v_ref, buoyancy_ref, before_far, before_near, push_ref):
    x_count, rows, _ = push_ref.shape
    half = x_count // 2
    odd = is_odd()
    at = strided(buoyancy_ref, x_count, rows)
    for x, value in enumerate(mirrored([at(x) for x in range(x_count)], odd)):
        push_ref[x] = value * (time_step**2 / 12.0)
    for c in range(u_ref.shape[0]):
        at, rate = strided(u_ref, x_count, rows, (c,)), strided(v_ref, x_count, rows, (c,))
        before = [at(x) - time_step * rate(x) for x in range(x_count)]
        for x, value in enumerate(mirrored(before, odd, c == 0)):
            (before_far if x < half else before_near)[c * half + x % half] = value


def corner_kernel(far, half, halo_ref, *refs):
    corner_ref = refs[-1]
    rows, y_count = halo_ref.shape[1:]
    side = Side(far, 2 * half)
    places = {x % side.x_count: x for x in side.outside}
    for c in range(corner_ref.shape[0]):
        corner_ref[c] = edge_message(
            lambda place: side.halo(halo_ref, c, places[place]),
            side.x_count, rows, y_count, tuple(places),
        )


def all_stresses(grads, lame, shear):
    pressure = lame * (grads[0][0] + grads[1][1] + grads[2][2])
    twice = shear + shear
    return (
        pressure + twice * grads[0][0],
        pressure + twice * grads[1][1],
        pressure + twice * grads[2][2],
        shear * (grads[0][1] + grads[1][0]),
        shear * (grads[0][2] + grads[2][0]),
        shear * (grads[1][2] + grads[2][1]),
    )


def tile_kernel(sides, comps, *refs):
    low_ref, high_ref, edge_ref = refs[:3]
    edge_in = refs[3 : 3 + sides]
    metric_ref, first_edge = refs[3 + sides : 5 + sides]
    first_edge_in = refs[5 + sides : 5 + 2 * sides]
    s_x, s_o, e_s = refs[5 + 2 * sides :]
    x_count, rows, y_count = metric_ref.shape[1:]
    half, window = x_count // 2, y_count // x_count
    has_left, has_right = neighbours()
    place = lanes_of((rows, y_count)) // window
    u = halves(low_ref, high_ref, half)
    band = band_matrix(y_count)

    edges, across = [], []
    for c in range(comps):
        edge = edge_tile(edge_ref[c], edge_in[0][c], edge_in[-1][c], has_left, has_right, window)
        terms = edge_terms(edge, window)
        result = banded(jnp.concatenate([u(c, x) for x in range(x_count)], 0), band)
        edges.append(edge)
        across.append(
            [
                result[x * rows : (x + 1) * rows] + edge_spread(terms, x, window)
                for x in range(x_count)
            ]
        )

    def gradients(along, beside, layers, metric):
        return [
            [
                along[c] + metric[0] * layers[c],
                beside[c] + metric[1] * layers[c],
                metric[2] * layers[c],
            ]
            for c in range(comps)
        ]

    for x in range(x_count):
        metric = [metric_ref[m, x] for m in range(5)]

        def near(c, k):
            return u(c, x + k) if 0 <= x + k < x_count else None

        along = [central(*(near(c, k) for k in (-2, -1, 1, 2))) for c in range(comps)]
        layers = [layer_derivative(u(c, x)) for c in range(comps)]
        grads = gradients(along, [across[c][x] for c in range(comps)], layers, metric)
        s11, s22, s33, s12, s13, s23 = all_stresses(grads, metric[3], metric[4])
        s_x[0, x], s_x[1, x], s_x[2, x] = s11, s12, s13
        s_o[0, x], s_o[1, x], s_o[2, x] = s22, s23, s33

    metric = [
        edge_tile(
            first_edge[comps + m], first_edge_in[0][comps + m], first_edge_in[-1][comps + m],
            has_left, has_right, window,
        )
        for m in range(5)
    ]
    along, beside = [], []
    for edge in edges:

        def near(k):
            inside = (place + k < x_count) if k > 0 else (place + k >= 0)
            return jnp.where(inside, roll(edge, -window * k), 0.0)

        along.append(central(*(near(k) for k in (-2, -1, 1, 2))))
        beside.append(central(*(roll(edge, -k) for k in (-2, -1, 1, 2))))
    grads = gradients(along, beside, [layer_derivative(edge) for edge in edges], metric)
    _, e22, _, e12, _, e23 = all_stresses(grads, metric[3], metric[4])
    e_s[0], e_s[1], e_s[2], e_s[3], e_s[4] = e12, e22, e23, metric[3], metric[4]


def wide_kernel(
    far, far_ref, near_ref, halo_ref, before_ref, metric_ref, push_ref, first_halo, s_x, s_o, e_s,
    out_ref, out_edge,
):
    x_count, rows, y_count = metric_ref.shape[1:]
    half, window = x_count // 2, y_count // x_count
    comps = s_x.shape[0]
    side = Side(far, x_count)
    inner = halves(far_ref, near_ref, half)
    band = band_matrix(y_count)
    steps = (-2, -1, 1, 2)

    def u(c, x):
        return inner(c, x) if 0 <= x < x_count else side.halo(halo_ref, c, x)

    def beyond(x):
        return x < 0 if far else x >= x_count

    along_x, others = {}, {}
    for x in range(side.inside[0] - 2, side.inside[-1] + 3):
        if beyond(x):
            continue
        values = [s_x[i, x] for i in range(3)]
        rest = [s_o[i, x] for i in range(3)] if x in side.inside else None
        if any(beyond(x + k) for k in steps):
            add = [
                central(*(u(c, x + k) if beyond(x + k) else None for k in steps))
                for c in range(comps)
            ]
            lame, shear = metric_ref[3, x], metric_ref[4, x]
            pressure = lame * add[0]
            values[0] = values[0] + pressure + (shear + shear) * add[0]
            values[1] = values[1] + shear * add[1]
            values[2] = values[2] + shear * add[2]
            rest[0] = rest[0] + pressure
            rest[2] = rest[2] + pressure
        along_x[x], others[x] = values, rest

    across = [
        banded(jnp.concatenate([u(c, x) for x in side.outside], 0), band) for c in range(2)
    ]
    for place, x in enumerate(side.outside):
        slope_x, slope_y, stretch, lame, shear = (
            side.metric(first_halo, comps, m, x) for m in range(5)
        )
        dr = [layer_derivative(u(c, x)) for c in range(comps)]
        dx = [central(*(u(c, x + k) for k in steps)) for c in range(comps)]
        dy = [across[c][place * rows : (place + 1) * rows] for c in range(2)]
        g11 = dx[0] + slope_x * dr[0]
        pressure = lame * (g11 + dy[1] + slope_y * dr[1] + stretch * dr[2])
        along_x[x] = [
            pressure + (shear + shear) * g11,
            shear * (dy[0] + slope_y * dr[0] + dx[1] + slope_x * dr[1]),
            shear * (stretch * dr[0] + dx[2] + slope_x * dr[2]),
        ]

    def across_of(i, x):
        return along_x[x][1] if i == 0 else others[x][i - 1]

    beside = []
    for i in range(comps):
        result = banded(jnp.concatenate([across_of(i, x) for x in side.inside], 0), band)
        terms = edge_terms(e_s[i], window)
        beside.append(
            {
                x: result[k * rows : (k + 1) * rows] + edge_spread(terms, x, window)
                for k, x in enumerate(side.inside)
            }
        )

    place = lanes_of((rows, y_count)) // window
    messages = [None] * comps
    for k, x in enumerate(side.inside):
        slope_x, slope_y, stretch = (metric_ref[m, x] for m in range(3))
        r11, r12, r13 = (layer_derivative(value) for value in along_x[x])
        r22, r23, r33 = (layer_derivative(value) for value in others[x])
        layers = ((r11, r12, r13), (r12, r22, r23), (r13, r23, r33))
        for c in range(comps):
            force = central(*(along_x[x + j][c] for j in steps)) + beside[c][x]
            force = force + slope_x * layers[c][0] + slope_y * layers[c][1]
            force = force + stretch * layers[c][2]
            at = c * half + k
            following = 2.0 * inner(c, x) - before_ref[at] + force * push_ref[x]
            out_ref[at] = following
            moved = roll(following, window * x + 4)
            messages[c] = moved if k == 0 else jnp.where(place == x, moved, messages[c])
    for c in range(comps):
        out_edge[c] = messages[c]


def fix_kernel(far, sides, merge, *refs):
    corner_in = refs[:sides]
    first_halo, e_s, push_ref, in_ref, edge_ref = refs[sides : 5 + sides]
    far_edge = refs[5 + sides] if merge else None
    out_ref, *out_edge = refs[5 + sides + bool(merge) :]
    x_count, rows, y_count = push_ref.shape
    half, window = x_count // 2, y_count // x_count
    comps = edge_ref.shape[0]
    side = Side(far, x_count)
    has_left, has_right = neighbours()
    lane = lanes_of((rows, y_count))
    place, w = lane // window, lane % window
    lame, shear = 3, 4
    steps = (-2, -1, 1, 2)

    corners = [
        jnp.where(w < 8, corner_in[-1][c] * has_right, roll(corner_in[0][c], 8) * has_left)
        for c in range(2)
    ]
    terms = [edge_terms(corner, window) for corner in corners]

    def edge_change(corner):
        def near(k):
            if (k < 0) != far:
                return None
            inside = (place + k < x_count) if k > 0 else (place + k >= 0)
            return jnp.where(inside, 0.0, roll(corner, -window * k))

        return central(*(near(k) for k in steps))

    beside = [
        edge_terms(e_s[shear] * edge_change(corners[1]), window),
        edge_terms(e_s[lame] * edge_change(corners[0]), window),
    ]

    for c in range(comps):
        changes = {}
        if c < 2:
            changes = {
                x: side.metric(first_halo, comps, lame if c == 0 else shear, x)
                * edge_spread(terms[1 - c], x % x_count, window)
                for x in side.outside
            }
        message = edge_ref[c]
        for k, x in enumerate(side.inside):
            value = in_ref[c * half + k]
            near = [changes.get(x + j) for j in steps]
            if any(item is not None for item in near):
                change = central(*near) + edge_spread(beside[c], x, window)
                value = value + change * push_ref[x]
                message = jnp.where(place == x, roll(value, window * x + 4), message)
            out_ref[c * half + k] = value
        if out_edge:
            if merge:
                message = jnp.where(place < half, far_edge[c], message)
            out_edge[0][c] = message


def sketch_kernel(moment, last, shape, *refs):
    comps, half, rows, y_count = shape
    far_ref, near_ref, before_far, before_near, probe_ref = refs[:5]
    sketch_in = None if moment == 0 else refs[5]
    sketch_ref, spread = refs[-2:]
    x_count = 2 * half
    groups = rows // SUB
    picked = groups // 2
    now = halves(far_ref, near_ref, half)
    past = halves(before_far, before_near, half)
    odd = is_odd()
    spread[...] = jnp.zeros_like(spread)
    spread[pl.ds(0, y_count // 2, stride=2), :] = probe_ref[moment]
    rates = []
    for x in range(0, x_count, 2):
        for c in range(comps):
            rate = now(c, x) - past(c, x)
            other = now(c, x_count - 1 - x) - past(c, x_count - 1 - x)
            rate = jnp.where(odd, -other if c == 0 else other, rate) * (0.5 / time_step)
            rates += [rate[SUB * v : SUB * (v + 1)] for v in range(0, groups, 2)]
    sketch = jnp.dot(
        jnp.concatenate(rates, 0),
        spread[...],
        precision=lax.Precision.HIGHEST,
        preferred_element_type=jnp.float32,
    )
    if sketch_in is not None:
        sketch = sketch + sketch_in[...]
    if last:
        for k in range(half * comps):
            for v in range(picked):
                start = (k * picked + v) * SUB
                sketch_ref[pl.ds(k * picked * SUB + v, SUB, stride=picked), :] = sketch[
                    start : start + SUB
                ]
    else:
        sketch_ref[...] = sketch


def finish_kernel(half, rows, far_ref, near_ref, out_ref):
    x_count, groups = 2 * half, rows // SUB
    now = halves(far_ref, near_ref, half)
    odd = is_odd()
    for c in range(out_ref.shape[0]):
        values = mirrored([now(c, x) for x in range(x_count)], odd, c == 0)
        for x, value in enumerate(values):
            for v in range(groups):
                out_ref[c, pl.ds(x_count * v + x, SUB, stride=groups * x_count), :] = value[
                    SUB * v : SUB * (v + 1)
                ]


def gram_kernel(first_ref, second_ref, sum_ref, packed_ref):
    total = first_ref[...] + second_ref[...]
    sum_ref[...] = total
    gram = lax.dot_general(
        total,
        total,
        (((0,), (0,)), ((), ())),
        precision=lax.Precision.HIGHEST,
        preferred_element_type=jnp.float32,
    )
    order = gram.shape[0]
    mid = order // 2
    top, bottom = gram[:mid], gram[mid:]
    row = lax.broadcasted_iota(jnp.int32, (mid, order), 0)
    column = lanes_of((mid, order)) - mid
    packed_ref[:mid] = jnp.where((column >= 0) & (row >= column), roll(top, mid), bottom)
    diagonal = jnp.sum(jnp.where(row == column, bottom, 0.0), 0, keepdims=True)
    packed_ref[mid:] = jnp.broadcast_to(diagonal, (packed_ref.shape[0] - mid, order))


def unpacked(packed):
    order = packed.shape[1]
    mid = order // 2
    row = lax.broadcasted_iota(jnp.int32, (mid, order), 0)
    lane = lanes_of((mid, order))
    column = lane - mid
    main = packed[:mid]
    diagonal = jnp.broadcast_to(packed[mid : mid + 1], (mid, order))
    moved = roll(main, mid)
    top = jnp.where(row > lane, moved, jnp.where(row == lane, 0.5 * moved, 0.0))
    bottom = jnp.where(
        (column < 0) | (row < column), main, jnp.where(row == column, 0.5 * diagonal, 0.0)
    )
    part = jnp.concatenate([top, bottom], 0)
    return part + part.T


def factor_kernel(scale, first_ref, second_ref, tall_ref, basis_ref, factor_ref):
    gram = unpacked(first_ref[...] + second_ref[...])
    order = gram.shape[0]
    blocks = order // SUB
    shape = (SUB, order)
    sub = lax.broadcasted_iota(jnp.int32, shape, 0)
    lane = lanes_of(shape)
    work = [gram[SUB * q : SUB * (q + 1)] for q in range(blocks)]
    other = [jnp.where(lane == sub + SUB * q, 1.0, 0.0) for q in range(blocks)]
    inverse_rows = []

    def row_of(value, k):
        return jnp.broadcast_to(value[k : k + 1, :], value.shape)

    def column_of(value, j):
        return jnp.broadcast_to(value[:, j : j + 1], value.shape)

    for p in range(blocks):
        columns = [column_of(work[p], SUB * p + k) for k in range(SUB)]
        ahead = [column_of(work[p + 1], SUB * p + k) for k in range(SUB)] if p + 1 < blocks else []
        upper = solved = work[p]
        lower = solved_other = other[p]
        pivots = inverses = columns[0]
        for k in range(SUB):
            pivot = row_of(columns[k], k)
            inverse = 1.0 / pivot
            every = jnp.where(sub != k, columns[k] * inverse, 0.0)
            after = jnp.where(sub > k, every, 0.0)
            for m in range(k + 1, SUB):
                columns[m] = columns[m] - every * row_of(columns[m], k)
            upper = upper - after * row_of(upper, k)
            lower = lower - after * row_of(lower, k)
            solved = solved - every * row_of(solved, k)
            solved_other = solved_other - every * row_of(solved_other, k)
            pivots = jnp.where(sub == k, pivot, pivots)
            inverses = jnp.where(sub == k, inverse, inverses)
        root = lax.rsqrt(pivots)
        factor_ref[SUB * p : SUB * (p + 1), :] = jnp.where(lane >= sub + SUB * p, upper * root, 0.0)
        inverse_rows.append(lower * root * scale)
        solved, solved_other = solved * inverses, solved_other * inverses
        for k, column in enumerate(ahead):
            work[p + 1] = work[p + 1] - column * row_of(solved, k)
            other[p + 1] = other[p + 1] - column * row_of(solved_other, k)
        if p + 2 < blocks:
            both = jnp.concatenate([solved, solved_other], 1)
            parts = [jnp.zeros((SUB * p, 2 * order), jnp.float32)] if p else []
            parts += [both, jnp.zeros((order - SUB * (p + 1), 2 * order), jnp.float32)]
            change = jnp.dot(
                jnp.concatenate(work[p + 2 :], 0),
                jnp.concatenate(parts, 0),
                precision=lax.Precision.HIGHEST,
                preferred_element_type=jnp.float32,
            )
            for i, q in enumerate(range(p + 2, blocks)):
                work[q] = work[q] - change[SUB * i : SUB * (i + 1), :order]
                other[q] = other[q] - change[SUB * i : SUB * (i + 1), order:]

    inverse_lower = jnp.concatenate(inverse_rows, 0)
    count, kept = basis_ref.shape[0], basis_ref.shape[1]
    start = pl.multiple_of(lax.axis_index("gy") * kept, SUB)
    tall = jnp.concatenate([tall_ref[k, pl.ds(start, kept), :] for k in range(count)], 0)
    basis = lax.dot_general(
        tall,
        inverse_lower,
        (((1,), (1,)), ((), ())),
        precision=lax.Precision.HIGHEST,
        preferred_element_type=jnp.float32,
    )
    for k in range(count):
        basis_ref[k] = basis[k * kept : (k + 1) * kept]


def f32(*shape):
    return jax.ShapeDtypeStruct(shape, jnp.float32)


VMEM = pl.BlockSpec(memory_space=pltpu.MemorySpace.VMEM)
ANY = pl.BlockSpec(memory_space=pl.ANY)
HBM = pl.BlockSpec(memory_space=pltpu.MemorySpace.HBM)


def call(kernel, outs, name, ins, specs=None, scratch=(), flops=0):
    size = sum(math.prod(x.shape) * 4 for x in (*ins, *outs))
    return pl.pallas_call(
        kernel,
        out_shape=outs,
        in_specs=specs or [VMEM] * len(ins),
        out_specs=[VMEM] * len(outs),
        scratch_shapes=list(scratch),
        compiler_params=pltpu.CompilerParams(vmem_limit_bytes=24 * 2**20),
        cost_estimate=pl.CostEstimate(flops=flops, bytes_accessed=size, transcendentals=0),
        name=name,
    )(*ins)


def butterfly(value, axis, last=False):
    count = lax.axis_size(axis)
    if count & (count - 1):
        total = lax.psum(value, axis)
        return (total, jnp.zeros_like(total)) if last else total
    bit = 1
    while bit < count:
        other = lax.ppermute(value, axis, [(i, i ^ bit) for i in range(count)])
        if last and 2 * bit == count:
            return value, other
        value = value + other
        bit *= 2
    return (value, jnp.zeros_like(value)) if last else value


def shards(displacement, velocity, slopes, stretch, moduli, buoyancy, probes):
    comps, layers, x_count, y_count = displacement.shape
    width = probes.shape[2]
    half = x_count // 2
    n_x, n_y = lax.axis_size("gx"), lax.axis_size("gy")
    sides = 1 if n_y == 2 else 2

    def flat(array):
        return array.reshape(array.shape[:-3] + (layers * x_count, y_count))

    def exchange(value, far):
        pairs = [(i, i + 1) for i in range(1 if far else 0, n_x - 1, 2)]
        return lax.ppermute(value, "gx", pairs + [(k, i) for i, k in pairs])

    def along_y(value):
        if sides == 1:
            return [lax.ppermute(value, "gy", [(0, 1), (1, 0)])]
        return [
            lax.ppermute(value, "gy", [(i, i + s) for i in range(n_y) if 0 <= i + s < n_y])
            for s in (1, -1)
        ]

    def slabs(count):
        return f32(count, layers, y_count)

    u_flat = flat(displacement)
    fields = [u_flat, flat(slopes), flat(stretch), flat(moduli)]
    u_far, u_near, edge, metric = call(
        begin_kernel,
        [slabs(comps * half + 10), slabs(comps * half + 10), slabs(comps + 5), f32(5, x_count, layers, y_count)],
        "begin",
        fields,
        specs=[HBM] * 4,
        scratch=[pltpu.VMEM(field.shape, jnp.float32) for field in fields]
        + [pltpu.SemaphoreType.DMA((4,))],
    )
    before_far, before_near, push = call(
        rest_kernel,
        [slabs(comps * half), slabs(comps * half), slabs(x_count)],
        "rest",
        [u_flat, flat(velocity), flat(buoyancy)],
    )

    sketch_rows = half * comps * (layers // 2)
    sketch = []

    def half_step(far, moment, halo, first_halo, before, tokens, far_edge):
        name = f"{'far' if far else 'near'}_{moment}"
        last = moment == STEPS - 1
        (corner,) = call(
            partial(corner_kernel, far, half),
            [slabs(2)],
            f"corner_{name}",
            [halo, *tokens],
            specs=[VMEM] + [ANY] * len(tokens),
        )
        corner_in = along_y(corner)
        value, own_edge = call(
            partial(wide_kernel, far),
            [slabs(comps * half), slabs(comps)],
            f"wide_{name}",
            [u_far, u_near, halo, before, metric, push, first_halo, s_x, s_o, e_s],
            flops=10_000_000,
        )
        merge = [] if far_edge is None else [far_edge]
        value, *own_edge = call(
            partial(fix_kernel, far, sides, len(merge)),
            [slabs(comps * half)] + ([] if last else [slabs(comps)]),
            f"fix_{name}",
            [*corner_in, first_halo, e_s, push, value, own_edge, *merge],
        )
        return value, (own_edge[0] if own_edge else None)

    for moment in range(STEPS):
        last = moment == STEPS - 1
        if moment == 0:
            far_halo = exchange(u_far, True)
            near_halo = exchange(u_near, False)
        edge_in = along_y(edge)
        if moment == 0:
            first_edge, first_edge_in, first_far, first_near = edge, edge_in, far_halo, near_halo
        s_x, s_o, e_s = call(
            partial(tile_kernel, sides, comps),
            [f32(comps, x_count, layers, y_count), f32(3, x_count, layers, y_count), slabs(5)],
            f"tile_{moment}",
            [u_far, u_near, edge, *edge_in, metric, first_edge, *first_edge_in],
            flops=20_000_000,
        )
        next_far, far_edge = half_step(
            True, moment, far_halo, first_far, before_far, [e_s, *(sketch or [push])], None
        )
        if not last:
            far_halo = exchange(next_far, True)
        next_near, edge = half_step(
            False, moment, near_halo, first_near, before_near, [next_far], far_edge
        )
        if not last:
            near_halo = exchange(next_near, False)
        sketch = call(
            partial(sketch_kernel, moment, last, (comps, half, layers, y_count)),
            [f32(sketch_rows, width)],
            f"sketch_{moment}",
            [next_far, next_near, before_far, before_near, probes, *sketch],
            scratch=[pltpu.VMEM((y_count, width), jnp.float32)],
        )
        before_far, before_near, u_far, u_near = u_far, u_near, next_far, next_near
    (final,) = call(
        partial(finish_kernel, half, layers),
        [f32(comps, layers * x_count, y_count)],
        "finish",
        [u_far, u_near],
    )
    final = final.reshape(displacement.shape)

    mine, theirs = butterfly(sketch[0], "gy", last=True)
    tall, packed = call(
        gram_kernel,
        [f32(sketch_rows, width), f32(width // 2 + SUB, width)],
        "gram",
        [mine, theirs],
    )
    first, second = butterfly(packed, "gx", last=True)
    depth = comps * (layers // 2)
    basis, factor = call(
        partial(factor_kernel, math.sqrt(sketch_rows * n_x)),
        [f32(half, depth // n_y, width), f32(width, width)],
        "factor",
        [first, second, tall.reshape(half, depth, width)],
    )
    return (final, basis, factor)


def solution(mesh):
    in_specs = (
        P(None, None, "gx", "gy"),
        P(None, None, "gx", "gy"),
        P(None, None, "gx", "gy"),
        P(None, "gx", "gy"),
        P(None, None, "gx", "gy"),
        P(None, "gx", "gy"),
        P(None, "gy", None),
    )
    out_specs = (P(None, None, "gx", "gy"), P("gx", "gy", None), P())
    return jax.shard_map(shards, mesh=mesh, in_specs=in_specs, out_specs=out_specs, check_vma=False)
```

```python
import math
from functools import partial

import jax
import jax.numpy as jnp
from jax import lax
from jax.experimental import pallas as pl
from jax.experimental.pallas import tpu as pltpu
from jax.sharding import PartitionSpec as P


STEPS = 4
SUB = 8

time_step = 0.12


def roll(value, shift, axis=-1):
    axis = axis % value.ndim
    shift = shift % value.shape[axis]
    return value if shift == 0 else pltpu.roll(value, shift, axis)


def lanes_of(shape):
    return lax.broadcasted_iota(jnp.int32, shape, len(shape) - 1)


def layer_derivative(value):
    groups = value.shape[0] // SUB
    parts = [value[SUB * v : SUB * (v + 1)] for v in range(groups)]
    sub = lax.broadcasted_iota(jnp.int32, parts[0].shape, 0)
    shifted = {}

    def at(v):
        if 0 <= v < groups:
            return parts[v]
        if v not in shifted:
            if v >= groups:
                shifted[v] = jnp.where(sub < SUB - 1, roll(parts[v - groups], -1, 0), 0.0)
            else:
                shifted[v] = jnp.where(sub > 0, roll(parts[v + groups], 1, 0), 0.0)
        return shifted[v]

    return jnp.concatenate(
        [at(v - 2) - at(v + 2) + 8.0 * (at(v + 1) - at(v - 1)) for v in range(groups)], 0
    )


def band_matrix(count):
    row = lax.broadcasted_iota(jnp.int32, (count, count), 0)
    col = lax.broadcasted_iota(jnp.int32, (count, count), 1)
    away = row - col
    band = jnp.where(
        away == -2,
        1.0,
        jnp.where(away == 2, -1.0, jnp.where(away == 1, 8.0, jnp.where(away == -1, -8.0, 0.0))),
    )
    return band.astype(jnp.bfloat16)


def banded(value, band):
    high = value.astype(jnp.bfloat16)
    low = (value - high.astype(jnp.float32)).astype(jnp.bfloat16)
    return jnp.dot(high, band, preferred_element_type=jnp.float32) + jnp.dot(
        low, band, preferred_element_type=jnp.float32
    )


def edge_terms(edge, window):
    w = lanes_of(edge.shape) % window
    up_2, up_3 = roll(edge, 2), roll(edge, 3)
    down_2, down_3 = roll(edge, -2), roll(edge, -3)
    right = jnp.where(w == 7, 8.0 * up_3, 0.0) - up_2
    left = down_2 - jnp.where(w == 8, 8.0 * down_3, 0.0)
    return jnp.where((w == 6) | (w == 7), right, left)


def edge_spread(terms, place, window):
    count = terms.shape[-1]
    lane = lanes_of(terms.shape)
    return jnp.where((lane < 2) | (lane >= count - 2), roll(terms, count - 2 - window * place - 6), 0.0)


def edge_message(load, x_count, rows, y_count, which=None):
    window = y_count // x_count
    place = lanes_of((rows, y_count)) // window
    message = None
    for x in which or range(x_count):
        moved = roll(load(x), window * x + 4)
        message = moved if message is None else jnp.where(place == x, moved, message)
    return message


def neighbours():
    at = lax.axis_index("gy")
    return (at > 0).astype(jnp.float32), (at < lax.axis_size("gy") - 1).astype(jnp.float32)


def edge_tile(own, from_left, from_right, has_left, has_right, window):
    w = lanes_of(own.shape) % window
    halo = jnp.where(w < 8, from_right * has_right, roll(from_left, 8) * has_left)
    mine = jnp.where(w < 4, own, roll(own, 8))
    return jnp.where((w >= 4) & (w < 12), halo, mine)


def strided(ref, x_count, rows, index=()):
    groups = rows // SUB

    def at(x):
        return jnp.concatenate(
            [
                ref[(*index, pl.ds(x_count * v + x, SUB, stride=groups * x_count), slice(None))]
                for v in range(groups)
            ],
            0,
        )

    return at


def central(far_low, near_low, near_high, far_high):
    def minus(first, second):
        if second is None:
            return first
        return -second if first is None else first - second

    near, far = minus(near_high, near_low), minus(far_low, far_high)
    if near is None:
        return far
    return 8.0 * near if far is None else far + 8.0 * near


def halves(far_ref, near_ref, half):
    def at(c, x):
        return far_ref[c * half + x] if x < half else near_ref[c * half + x - half]

    return at


def is_odd():
    return lax.axis_index("gx") % 2 == 1


def mirrored(values, odd, flip=False):
    other = [-value if flip else value for value in values[::-1]]
    return [jnp.where(odd, second, first) for first, second in zip(values, other)]


class Side:
    def __init__(self, far, x_count):
        self.far, self.half, self.x_count = far, x_count // 2, x_count
        self.inside = range(self.half) if far else range(self.half, x_count)
        self.outside = (-2, -1) if far else (x_count, x_count + 1)

    def depth(self, x):
        return -1 - x if self.far else x - self.x_count

    def at(self, ref, first, index, x, negate, terms=None):
        place = self.depth(x) if self.far else 1 - self.depth(x)
        value = ref[first + 2 * index + place]
        value = -value if negate else value
        return value if terms is None else value + terms

    def halo(self, ref, c, x, terms=None):
        terms = None if terms is None or c > 1 else terms[self.slot(c, x)]
        return self.at(ref, 0, c, x, c == 0, terms)

    def own_part(self, ref, i, x, terms=None):
        return self.at(ref, 6, i, x, i > 0, None if terms is None else terms[self.slot(2 + i, x)])

    def modulus(self, ref, m, x):
        return self.at(ref, 12, m, x, False)

    def slot(self, index, x):
        return 10 * (not self.far) + 2 * index + self.depth(x)

    def packed(self, ref, f, x, window):
        place = 2 * f + (self.depth(x) if self.far else 1 - self.depth(x))
        value = roll(ref[16], ref.shape[2] - 4 - window * place)
        return -value if f == 1 else value

    def pack(self, messages, window):
        place = lanes_of(messages[0].shape) // (2 * window)
        packed = None
        for f, message in enumerate(messages):
            moved = roll(message, window * (2 * f - (0 if self.far else self.x_count - 2)))
            packed = moved if packed is None else jnp.where(place == f, moved, packed)
        return packed

    def send(self, ref, u, metric):
        for k, x in enumerate(self.inside[:2] if self.far else self.inside[-2:]):
            slope_x, slope_y, stretch, lame, shear = (metric(m, x) for m in range(5))
            dr = [layer_derivative(u(c, x)) for c in range(3)]
            near = [x + j if x + j in self.inside else None for j in (-2, -1, 1, 2)]
            dx = [central(*(None if j is None else u(c, j) for j in near)) for c in range(3)]
            g11 = dx[0] + slope_x * dr[0]
            parts = (
                lame * (g11 + slope_y * dr[1] + stretch * dr[2]) + (shear + shear) * g11,
                shear * (slope_y * dr[0] + dx[1] + slope_x * dr[1]),
                shear * (stretch * dr[0] + dx[2] + slope_x * dr[2]),
            )
            for c in range(3):
                ref[2 * c + k] = u(c, x)
                ref[6 + 2 * c + k] = parts[c]


def begin_kernel(*refs):
    sources, held, sems = refs[:5], refs[11:16], refs[16]
    far_ref, near_ref, far_send, near_send, edge_ref, metric_ref = refs[5:11]
    u_ref, slope_ref, stretch_ref, moduli_ref, buoyancy_ref = held
    copies = [
        pltpu.make_async_copy(source, target, sems.at[i])
        for i, (source, target) in enumerate(zip(sources, held))
    ]
    for copy in copies:
        copy.start()
    copies[0].wait()
    x_count, rows, y_count = metric_ref.shape[1:]
    half = x_count // 2
    comps = u_ref.shape[0]
    odd = is_odd()
    for c in range(comps):
        at = strided(u_ref, x_count, rows, (c,))
        slabs = mirrored([at(x) for x in range(x_count)], odd, c == 0)
        for k in range(half):
            far_ref[c * half + k] = slabs[k]
            near_ref[c * half + k] = slabs[half + k]
        edge_ref[c] = edge_message(lambda x: slabs[x], x_count, rows, y_count)
    for copy in copies[1:]:
        copy.wait()
    fields = [
        (strided(slope_ref, x_count, rows, (0,)), None),
        (strided(slope_ref, x_count, rows, (1,)), None),
        (strided(stretch_ref, x_count, rows), None),
        (strided(moduli_ref, x_count, rows, (0,)), 1.0 / 12.0),
        (strided(moduli_ref, x_count, rows, (1,)), 1.0 / 12.0),
    ]
    for m, (at, scale) in enumerate(fields):
        slabs = mirrored([at(x) for x in range(x_count)], odd, m == 0)
        if scale is not None:
            slabs = [slab * scale for slab in slabs]
        for x in range(x_count):
            metric_ref[m, x] = slabs[x]
        for k in range(2):
            if m > 2:
                far_send[6 + 2 * m + k] = slabs[k]
                near_send[6 + 2 * m + k] = slabs[x_count - 2 + k]
        edge_ref[comps + m] = edge_message(lambda x: slabs[x], x_count, rows, y_count)
    at = strided(buoyancy_ref, x_count, rows)
    slabs = mirrored([at(x) for x in range(x_count)], odd)
    push = edge_message(lambda x: slabs[x], x_count, rows, y_count) * (time_step**2 / 12.0)
    u, window = halves(far_ref, near_ref, half), y_count // x_count
    for far, ref in ((True, far_send), (False, near_send)):
        side = Side(far, x_count)
        side.send(ref, u, lambda m, x: metric_ref[m, x])
        ref[16] = side.pack([push, *(edge_ref[comps + m] for m in range(3))], window)


def rest_kernel(u_ref, v_ref, buoyancy_ref, before_far, before_near, push_ref):
    x_count, rows, _ = push_ref.shape
    half = x_count // 2
    odd = is_odd()
    at = strided(buoyancy_ref, x_count, rows)
    for x, value in enumerate(mirrored([at(x) for x in range(x_count)], odd)):
        push_ref[x] = value * (time_step**2 / 12.0)
    for c in range(u_ref.shape[0]):
        at, rate = strided(u_ref, x_count, rows, (c,)), strided(v_ref, x_count, rows, (c,))
        before = [at(x) - time_step * rate(x) for x in range(x_count)]
        for x, value in enumerate(mirrored(before, odd, c == 0)):
            (before_far if x < half else before_near)[c * half + x % half] = value


def corner_kernel(x_count, fixed, far_ref, near_ref, *refs):
    corner_ref, terms = refs[-1], refs[0] if fixed else None
    rows, y_count = far_ref.shape[1:]
    places = {}
    for far, ref in ((True, far_ref), (False, near_ref)):
        side = Side(far, x_count)
        places.update({x % x_count: (side, ref, x) for x in side.outside})

    def load(c, place):
        side, ref, x = places[place]
        return side.halo(ref, c, x, terms) if c < 2 else side.modulus(ref, c - 2, x)

    for c in range(corner_ref.shape[0]):
        corner_ref[c] = edge_message(
            lambda place: load(c, place), x_count, rows, y_count, tuple(places)
        )


def corner_tile(corner_in, c, window, has_left, has_right):
    w = lanes_of(corner_in[0].shape[1:]) % window
    return jnp.where(w < 8, corner_in[-1][c] * has_right, roll(corner_in[0][c], 8) * has_left)


def beyond_change(value, window, x_count):
    place = lanes_of(value.shape) // window

    def near(k):
        inside = (place + k < x_count) if k > 0 else (place + k >= 0)
        return jnp.where(inside, 0.0, roll(value, -window * k))

    return central(*(near(k) for k in (-2, -1, 1, 2)))


def all_stresses(grads, lame, shear):
    pressure = lame * (grads[0][0] + grads[1][1] + grads[2][2])
    twice = shear + shear
    return (
        pressure + twice * grads[0][0],
        pressure + twice * grads[1][1],
        pressure + twice * grads[2][2],
        shear * (grads[0][1] + grads[1][0]),
        shear * (grads[0][2] + grads[2][0]),
        shear * (grads[1][2] + grads[2][1]),
    )


def tile_kernel(sides, comps, *refs):
    low_ref, high_ref, edge_ref = refs[:3]
    edge_in = refs[3 : 3 + sides]
    metric_ref, first_edge = refs[3 + sides : 5 + sides]
    first_edge_in = refs[5 + sides : 5 + 2 * sides]
    s_x, s_o, e_s = refs[5 + 2 * sides :]
    x_count, rows, y_count = metric_ref.shape[1:]
    half, window = x_count // 2, y_count // x_count
    has_left, has_right = neighbours()
    place = lanes_of((rows, y_count)) // window
    u = halves(low_ref, high_ref, half)
    band = band_matrix(y_count)

    edges, across = [], []
    for c in range(comps):
        edge = edge_tile(edge_ref[c], edge_in[0][c], edge_in[-1][c], has_left, has_right, window)
        terms = edge_terms(edge, window)
        result = banded(jnp.concatenate([u(c, x) for x in range(x_count)], 0), band)
        edges.append(edge)
        across.append(
            [
                result[x * rows : (x + 1) * rows] + edge_spread(terms, x, window)
                for x in range(x_count)
            ]
        )

    def gradients(along, beside, layers, metric):
        return [
            [
                along[c] + metric[0] * layers[c],
                beside[c] + metric[1] * layers[c],
                metric[2] * layers[c],
            ]
            for c in range(comps)
        ]

    for x in range(x_count):
        metric = [metric_ref[m, x] for m in range(5)]

        def near(c, k):
            return u(c, x + k) if 0 <= x + k < x_count else None

        along = [central(*(near(c, k) for k in (-2, -1, 1, 2))) for c in range(comps)]
        layers = [layer_derivative(u(c, x)) for c in range(comps)]
        grads = gradients(along, [across[c][x] for c in range(comps)], layers, metric)
        s11, s22, s33, s12, s13, s23 = all_stresses(grads, metric[3], metric[4])
        s_x[0, x], s_x[1, x], s_x[2, x] = s11, s12, s13
        s_o[0, x], s_o[1, x], s_o[2, x] = s22, s23, s33

    metric = [
        edge_tile(
            first_edge[comps + m], first_edge_in[0][comps + m], first_edge_in[-1][comps + m],
            has_left, has_right, window,
        )
        for m in range(5)
    ]
    along, beside = [], []
    for edge in edges:

        def near(k):
            inside = (place + k < x_count) if k > 0 else (place + k >= 0)
            return jnp.where(inside, roll(edge, -window * k), 0.0)

        along.append(central(*(near(k) for k in (-2, -1, 1, 2))))
        beside.append(central(*(roll(edge, -k) for k in (-2, -1, 1, 2))))
    grads = gradients(along, beside, [layer_derivative(edge) for edge in edges], metric)
    _, e22, _, e12, _, e23 = all_stresses(grads, metric[3], metric[4])
    e_s[0], e_s[1], e_s[2], e_s[3], e_s[4] = e12, e22, e23, metric[3], metric[4]


def wide_kernel(
    far, fixed, send, far_ref, near_ref, halo_ref, before_ref, metric_ref, push_ref, first_halo, s_x,
    s_o, e_s, *refs,
):
    out_ref, send_ref, out_edge = refs[-3:]
    terms = refs[0] if fixed else None
    x_count, rows, y_count = metric_ref.shape[1:]
    half, window = x_count // 2, y_count // x_count
    comps = s_x.shape[0]
    side = Side(far, x_count)
    inner = halves(far_ref, near_ref, half)
    band = band_matrix(y_count)
    steps = (-2, -1, 1, 2)

    def u(c, x):
        return inner(c, x) if 0 <= x < x_count else side.halo(halo_ref, c, x, terms)

    def beyond(x):
        return x < 0 if far else x >= x_count

    along_x, others = {}, {}
    for x in range(side.inside[0] - 2, side.inside[-1] + 3):
        if beyond(x):
            continue
        values = [s_x[i, x] for i in range(3)]
        rest = [s_o[i, x] for i in range(3)] if x in side.inside else None
        if any(beyond(x + k) for k in steps):
            add = [
                central(*(u(c, x + k) if beyond(x + k) else None for k in steps))
                for c in range(comps)
            ]
            lame, shear = metric_ref[3, x], metric_ref[4, x]
            pressure = lame * add[0]
            values[0] = values[0] + pressure + (shear + shear) * add[0]
            values[1] = values[1] + shear * add[1]
            values[2] = values[2] + shear * add[2]
            rest[0] = rest[0] + pressure
            rest[2] = rest[2] + pressure
        along_x[x], others[x] = values, rest

    across = [
        banded(jnp.concatenate([u(c, x) for x in side.outside], 0), band) for c in range(2)
    ]
    for place, x in enumerate(side.outside):
        lame, shear = (side.modulus(first_halo, m, x) for m in range(2))
        dx = [
            central(*(u(c, x + k) if 0 <= x + k < x_count else None for k in steps))
            for c in range(comps)
        ]
        dy = [across[c][place * rows : (place + 1) * rows] for c in range(2)]
        values = [side.own_part(halo_ref, i, x, terms) for i in range(3)]
        values[0] = values[0] + lame * (dx[0] + dy[1]) + (shear + shear) * dx[0]
        values[1] = values[1] + shear * (dy[0] + dx[1])
        values[2] = values[2] + shear * dx[2]
        along_x[x] = values

    def across_of(i, x):
        return along_x[x][1] if i == 0 else others[x][i - 1]

    beside = []
    for i in range(comps):
        result = banded(jnp.concatenate([across_of(i, x) for x in side.inside], 0), band)
        added = edge_terms(e_s[i], window)
        beside.append(
            {
                x: result[k * rows : (k + 1) * rows] + edge_spread(added, x, window)
                for k, x in enumerate(side.inside)
            }
        )

    place = lanes_of((rows, y_count)) // window
    messages = [None] * comps
    for k, x in enumerate(side.inside):
        slope_x, slope_y, stretch = (metric_ref[m, x] for m in range(3))
        r11, r12, r13 = (layer_derivative(value) for value in along_x[x])
        r22, r23, r33 = (layer_derivative(value) for value in others[x])
        layers = ((r11, r12, r13), (r12, r22, r23), (r13, r23, r33))
        for c in range(comps):
            force = central(*(along_x[x + j][c] for j in steps)) + beside[c][x]
            force = force + slope_x * layers[c][0] + slope_y * layers[c][1]
            force = force + stretch * layers[c][2]
            at = c * half + k
            following = 2.0 * inner(c, x) - before_ref[at] + force * push_ref[x]
            out_ref[at] = following
            moved = roll(following, window * x + 4)
            messages[c] = moved if k == 0 else jnp.where(place == x, moved, messages[c])
    for c in range(comps):
        out_edge[c] = messages[c]
    if send:
        side.send(
            send_ref,
            lambda c, x: out_ref[c * half + x - side.inside[0]],
            lambda m, x: metric_ref[m, x],
        )


def fix_kernel(sides, *refs):
    corner_in = refs[:sides]
    first_far, first_near, e_s, push_ref = refs[sides : 4 + sides]
    in_far, in_near, far_edge, near_edge = refs[4 + sides : 8 + sides]
    out_far, out_near, *out_edge = refs[8 + sides :]
    x_count, rows, y_count = push_ref.shape
    half, window = x_count // 2, y_count // x_count
    comps = far_edge.shape[0]
    has_left, has_right = neighbours()
    place = lanes_of((rows, y_count)) // window
    lame, shear = 3, 4
    steps = (-2, -1, 1, 2)

    corners = [corner_tile(corner_in, c, window, has_left, has_right) for c in range(2)]
    terms = [edge_terms(corner, window) for corner in corners]
    beside = [
        edge_terms(e_s[shear] * beyond_change(corners[1], window, x_count), window),
        edge_terms(e_s[lame] * beyond_change(corners[0], window, x_count), window),
    ]
    for c in range(comps):
        message = jnp.where(place < half, far_edge[c], near_edge[c])
        for far, first, in_ref, out_ref in (
            (True, first_far, in_far, out_far),
            (False, first_near, in_near, out_near),
        ):
            side = Side(far, x_count)
            changes = {}
            if c < 2:
                changes = {
                    x: side.modulus(first, c, x)
                    * edge_spread(terms[1 - c], x % x_count, window)
                    for x in side.outside
                }
            for k, x in enumerate(side.inside):
                value = in_ref[c * half + k]
                near = [changes.get(x + j) for j in steps]
                if any(item is not None for item in near):
                    change = central(*near) + edge_spread(beside[c], x, window)
                    value = value + change * push_ref[x]
                    message = jnp.where(place == x, roll(value, window * x + 4), message)
                out_ref[c * half + k] = value
        if out_edge:
            out_edge[0][c] = message


def partner_kernel(sides, edge_ref, *refs):
    edge_in = refs[:sides]
    metric_ref, first_far, first_near = refs[sides : 3 + sides]
    moduli_in = refs[3 + sides : 3 + 2 * sides]
    out_ref = refs[3 + 2 * sides]
    x_count, _, y_count = metric_ref.shape[1:]
    window = y_count // x_count
    has_left, has_right = neighbours()
    edges = [
        edge_tile(edge_ref[c], edge_in[0][c], edge_in[-1][c], has_left, has_right, window)
        for c in range(2)
    ]
    lame, shear = (corner_tile(moduli_in, 2 + m, window, has_left, has_right) for m in range(2))
    terms = [edge_terms(edge, window) for edge in edges]
    beside = [
        edge_terms(shear * beyond_change(edges[1], window, x_count), window),
        edge_terms(lame * beyond_change(edges[0], window, x_count), window),
    ]
    for far, first in ((True, first_far), (False, first_near)):
        side = Side(far, x_count)
        added = {}
        for c in range(2):
            changes = {
                x: metric_ref[3 + c, x] * edge_spread(terms[1 - c], x, window)
                for x in (side.inside[:2] if far else side.inside[-2:])
            }
            for x in side.outside:
                near = [changes.get(x + k) for k in (-2, -1, 1, 2)]
                change = central(*near) + edge_spread(beside[c], x % x_count, window)
                change = change * side.packed(first, 0, x, window)
                added[c, x] = out_ref[side.slot(c, x)] = change
        for x in side.outside:
            slope_x, slope_y, stretch = (side.packed(first, 1 + m, x, window) for m in range(3))
            own_lame, own_shear = (side.modulus(first, m, x) for m in range(2))
            dr = [layer_derivative(added[c, x]) for c in range(2)]
            near = [added.get((c, x + k)) for c in range(2) for k in (-2, -1, 1, 2)]
            dx = [central(*near[:4]), central(*near[4:])]
            g11 = dx[0] + slope_x * dr[0]
            out_ref[side.slot(2, x)] = (
                own_lame * (g11 + slope_y * dr[1]) + (own_shear + own_shear) * g11
            )
            out_ref[side.slot(3, x)] = own_shear * (slope_y * dr[0] + dx[1] + slope_x * dr[1])
            out_ref[side.slot(4, x)] = own_shear * (stretch * dr[0])


def sketch_kernel(moment, last, shape, *refs):
    comps, half, rows, y_count = shape
    far_ref, near_ref, before_far, before_near, probe_ref = refs[:5]
    sketch_in = None if moment == 0 else refs[5]
    sketch_ref, spread = refs[-2:]
    x_count = 2 * half
    groups = rows // SUB
    picked = groups // 2
    now = halves(far_ref, near_ref, half)
    past = halves(before_far, before_near, half)
    odd = is_odd()
    spread[...] = jnp.zeros_like(spread)
    spread[pl.ds(0, y_count // 2, stride=2), :] = probe_ref[moment]
    rates = []
    for x in range(0, x_count, 2):
        for c in range(comps):
            rate = now(c, x) - past(c, x)
            other = now(c, x_count - 1 - x) - past(c, x_count - 1 - x)
            rate = jnp.where(odd, -other if c == 0 else other, rate) * (0.5 / time_step)
            rates += [rate[SUB * v : SUB * (v + 1)] for v in range(0, groups, 2)]
    sketch = jnp.dot(
        jnp.concatenate(rates, 0),
        spread[...],
        precision=lax.Precision.HIGHEST,
        preferred_element_type=jnp.float32,
    )
    if sketch_in is not None:
        sketch = sketch + sketch_in[...]
    if last:
        for k in range(half * comps):
            for v in range(picked):
                start = (k * picked + v) * SUB
                sketch_ref[pl.ds(k * picked * SUB + v, SUB, stride=picked), :] = sketch[
                    start : start + SUB
                ]
    else:
        sketch_ref[...] = sketch


def finish_kernel(half, rows, far_ref, near_ref, out_ref):
    x_count, groups = 2 * half, rows // SUB
    now = halves(far_ref, near_ref, half)
    odd = is_odd()
    for c in range(out_ref.shape[0]):
        values = mirrored([now(c, x) for x in range(x_count)], odd, c == 0)
        for x, value in enumerate(values):
            for v in range(groups):
                out_ref[c, pl.ds(x_count * v + x, SUB, stride=groups * x_count), :] = value[
                    SUB * v : SUB * (v + 1)
                ]


def gram_kernel(first_ref, second_ref, sum_ref, packed_ref):
    total = first_ref[...] + second_ref[...]
    sum_ref[...] = total
    gram = lax.dot_general(
        total,
        total,
        (((0,), (0,)), ((), ())),
        precision=lax.Precision.HIGHEST,
        preferred_element_type=jnp.float32,
    )
    order = gram.shape[0]
    mid = order // 2
    top, bottom = gram[:mid], gram[mid:]
    row = lax.broadcasted_iota(jnp.int32, (mid, order), 0)
    column = lanes_of((mid, order)) - mid
    packed_ref[:mid] = jnp.where((column >= 0) & (row >= column), roll(top, mid), bottom)
    diagonal = jnp.sum(jnp.where(row == column, bottom, 0.0), 0, keepdims=True)
    packed_ref[mid:] = jnp.broadcast_to(diagonal, (packed_ref.shape[0] - mid, order))


def unpacked(packed):
    order = packed.shape[1]
    mid = order // 2
    row = lax.broadcasted_iota(jnp.int32, (mid, order), 0)
    lane = lanes_of((mid, order))
    column = lane - mid
    main = packed[:mid]
    diagonal = jnp.broadcast_to(packed[mid : mid + 1], (mid, order))
    moved = roll(main, mid)
    top = jnp.where(row > lane, moved, jnp.where(row == lane, 0.5 * moved, 0.0))
    bottom = jnp.where(
        (column < 0) | (row < column), main, jnp.where(row == column, 0.5 * diagonal, 0.0)
    )
    part = jnp.concatenate([top, bottom], 0)
    return part + part.T


def factor_kernel(scale, first_ref, second_ref, tall_ref, basis_ref, factor_ref):
    gram = unpacked(first_ref[...] + second_ref[...])
    order = gram.shape[0]
    blocks = order // SUB
    shape = (SUB, order)
    sub = lax.broadcasted_iota(jnp.int32, shape, 0)
    lane = lanes_of(shape)
    work = [gram[SUB * q : SUB * (q + 1)] for q in range(blocks)]
    other = [jnp.where(lane == sub + SUB * q, 1.0, 0.0) for q in range(blocks)]
    inverse_rows = []

    def row_of(value, k):
        return jnp.broadcast_to(value[k : k + 1, :], value.shape)

    def column_of(value, j):
        return jnp.broadcast_to(value[:, j : j + 1], value.shape)

    for p in range(blocks):
        columns = [column_of(work[p], SUB * p + k) for k in range(SUB)]
        ahead = [column_of(work[p + 1], SUB * p + k) for k in range(SUB)] if p + 1 < blocks else []
        upper = solved = work[p]
        lower = solved_other = other[p]
        pivots = inverses = columns[0]
        for k in range(SUB):
            pivot = row_of(columns[k], k)
            inverse = 1.0 / pivot
            every = jnp.where(sub != k, columns[k] * inverse, 0.0)
            after = jnp.where(sub > k, every, 0.0)
            for m in range(k + 1, SUB):
                columns[m] = columns[m] - every * row_of(columns[m], k)
            upper = upper - after * row_of(upper, k)
            lower = lower - after * row_of(lower, k)
            solved = solved - every * row_of(solved, k)
            solved_other = solved_other - every * row_of(solved_other, k)
            pivots = jnp.where(sub == k, pivot, pivots)
            inverses = jnp.where(sub == k, inverse, inverses)
        root = lax.rsqrt(pivots)
        factor_ref[SUB * p : SUB * (p + 1), :] = jnp.where(lane >= sub + SUB * p, upper * root, 0.0)
        inverse_rows.append(lower * root * scale)
        solved, solved_other = solved * inverses, solved_other * inverses
        for k, column in enumerate(ahead):
            work[p + 1] = work[p + 1] - column * row_of(solved, k)
            other[p + 1] = other[p + 1] - column * row_of(solved_other, k)
        if p + 2 < blocks:
            both = jnp.concatenate([solved, solved_other], 1)
            parts = [jnp.zeros((SUB * p, 2 * order), jnp.float32)] if p else []
            parts += [both, jnp.zeros((order - SUB * (p + 1), 2 * order), jnp.float32)]
            change = jnp.dot(
                jnp.concatenate(work[p + 2 :], 0),
                jnp.concatenate(parts, 0),
                precision=lax.Precision.HIGHEST,
                preferred_element_type=jnp.float32,
            )
            for i, q in enumerate(range(p + 2, blocks)):
                work[q] = work[q] - change[SUB * i : SUB * (i + 1), :order]
                other[q] = other[q] - change[SUB * i : SUB * (i + 1), order:]

    inverse_lower = jnp.concatenate(inverse_rows, 0)
    count, kept = basis_ref.shape[0], basis_ref.shape[1]
    start = pl.multiple_of(lax.axis_index("gy") * kept, SUB)
    tall = jnp.concatenate([tall_ref[k, pl.ds(start, kept), :] for k in range(count)], 0)
    basis = lax.dot_general(
        tall,
        inverse_lower,
        (((1,), (1,)), ((), ())),
        precision=lax.Precision.HIGHEST,
        preferred_element_type=jnp.float32,
    )
    for k in range(count):
        basis_ref[k] = basis[k * kept : (k + 1) * kept]


def f32(*shape):
    return jax.ShapeDtypeStruct(shape, jnp.float32)


VMEM = pl.BlockSpec(memory_space=pltpu.MemorySpace.VMEM)
ANY = pl.BlockSpec(memory_space=pl.ANY)
HBM = pl.BlockSpec(memory_space=pltpu.MemorySpace.HBM)


def call(kernel, outs, ins, specs=None, scratch=(), flops=0):
    size = sum(math.prod(x.shape) * 4 for x in (*ins, *outs))
    return pl.pallas_call(
        kernel,
        out_shape=outs,
        in_specs=specs or [VMEM] * len(ins),
        out_specs=[VMEM] * len(outs),
        scratch_shapes=list(scratch),
        compiler_params=pltpu.CompilerParams(vmem_limit_bytes=24 * 2**20),
        cost_estimate=pl.CostEstimate(flops=flops, bytes_accessed=size, transcendentals=0),
    )(*ins)


def butterfly(value, axis, last=False):
    count = lax.axis_size(axis)
    if count & (count - 1):
        total = lax.psum(value, axis)
        return (total, jnp.zeros_like(total)) if last else total
    bit = 1
    while bit < count:
        other = lax.ppermute(value, axis, [(i, i ^ bit) for i in range(count)])
        if last and 2 * bit == count:
            return value, other
        value = value + other
        bit *= 2
    return (value, jnp.zeros_like(value)) if last else value


def shards(displacement, velocity, slopes, stretch, moduli, buoyancy, probes):
    comps, layers, x_count, y_count = displacement.shape
    width = probes.shape[2]
    half = x_count // 2
    n_x, n_y = lax.axis_size("gx"), lax.axis_size("gy")
    sides = 1 if n_y == 2 else 2

    def flat(array):
        return array.reshape(array.shape[:-3] + (layers * x_count, y_count))

    def exchange(value, far):
        pairs = [(i, i + 1) for i in range(1 if far else 0, n_x - 1, 2)]
        return lax.ppermute(value, "gx", pairs + [(k, i) for i, k in pairs])

    def along_y(value):
        if sides == 1:
            return [lax.ppermute(value, "gy", [(0, 1), (1, 0)])]
        return [
            lax.ppermute(value, "gy", [(i, i + s) for i in range(n_y) if 0 <= i + s < n_y])
            for s in (1, -1)
        ]

    def slabs(count):
        return f32(count, layers, y_count)

    u_flat = flat(displacement)
    fields = [
        pltpu.with_memory_space_constraint(field, pltpu.MemorySpace.HBM)
        for field in (u_flat, flat(slopes), flat(stretch), flat(moduli), flat(buoyancy))
    ]
    u_far, u_near, far_send, near_send, edge, metric = call(
        begin_kernel,
        [
            slabs(comps * half), slabs(comps * half), slabs(17), slabs(17), slabs(comps + 5),
            f32(5, x_count, layers, y_count),
        ],
        fields,
        specs=[HBM] * 5,
        scratch=[pltpu.VMEM(field.shape, jnp.float32) for field in fields]
        + [pltpu.SemaphoreType.DMA((5,))],
    )
    before_far, before_near, push = call(
        rest_kernel,
        [slabs(comps * half), slabs(comps * half), slabs(x_count)],
        [u_flat, flat(velocity), flat(buoyancy)],
    )

    sketch_rows = half * comps * (layers // 2)
    sketch = []

    def half_step(far, moment, halo, first_halo, before, terms, token):
        return call(
            partial(wide_kernel, far, len(terms), moment < STEPS - 1),
            [slabs(comps * half), slabs(12), slabs(comps)],
            [
                u_far, u_near, halo, before, metric, push, first_halo, s_x, s_o, e_s, *terms, *token,
            ],
            specs=[VMEM] * (10 + len(terms)) + [ANY] * len(token),
            flops=10_000_000,
        )

    terms = []
    for moment in range(STEPS):
        last = moment == STEPS - 1
        if moment == 0:
            far_halo = exchange(far_send, True)
            near_halo = exchange(near_send, False)
        edge_in = along_y(edge)
        if moment == 0:
            first_edge, first_edge_in, first_far, first_near = edge, edge_in, far_halo, near_halo
        s_x, s_o, e_s = call(
            partial(tile_kernel, sides, comps),
            [f32(comps, x_count, layers, y_count), f32(3, x_count, layers, y_count), slabs(5)],
            [u_far, u_near, edge, *edge_in, metric, first_edge, *first_edge_in],
            flops=20_000_000,
        )
        raw_far, far_send, far_edge = half_step(
            True, moment, far_halo, first_far, before_far, terms, sketch or [push]
        )
        (corner,) = call(
            partial(corner_kernel, x_count, len(terms)),
            [slabs(2 if moment else 4)],
            [far_halo, near_halo, *terms, raw_far],
            specs=[VMEM] * (2 + len(terms)) + [ANY],
        )
        corner_in = along_y(corner)
        if moment == 0:
            moduli_in = corner_in
        raw_near, near_send, near_edge = half_step(
            False, moment, near_halo, first_near, before_near, terms, [raw_far]
        )
        if not last:
            far_halo = exchange(far_send, True)
            near_halo = exchange(near_send, False)
            terms = call(
                partial(partner_kernel, sides),
                [slabs(20)],
                [edge, *edge_in, metric, first_far, first_near, *moduli_in],
            )
        next_far, next_near, *edge = call(
            partial(fix_kernel, sides),
            [slabs(comps * half), slabs(comps * half)] + ([] if last else [slabs(comps)]),
            [
                *corner_in, first_far, first_near, e_s, push, raw_far, raw_near, far_edge, near_edge,
            ],
        )
        edge = None if last else edge[0]
        sketch = call(
            partial(sketch_kernel, moment, last, (comps, half, layers, y_count)),
            [f32(sketch_rows, width)],
            [next_far, next_near, before_far, before_near, probes, *sketch],
            scratch=[pltpu.VMEM((y_count, width), jnp.float32)],
        )
        before_far, before_near, u_far, u_near = u_far, u_near, next_far, next_near
    (final,) = call(
        partial(finish_kernel, half, layers),
        [f32(comps, layers * x_count, y_count)],
        [u_far, u_near],
    )
    final = final.reshape(displacement.shape)

    mine, theirs = butterfly(sketch[0], "gy", last=True)
    tall, packed = call(
        gram_kernel, [f32(sketch_rows, width), f32(width // 2 + SUB, width)], [mine, theirs]
    )
    first, second = butterfly(packed, "gx", last=True)
    depth = comps * (layers // 2)
    basis, factor = call(
        partial(factor_kernel, math.sqrt(sketch_rows * n_x)),
        [f32(half, depth // n_y, width), f32(width, width)],
        [first, second, tall.reshape(half, depth, width)],
    )
    return (final, basis, factor)


def solution(mesh):
    in_specs = (
        P(None, None, "gx", "gy"),
        P(None, None, "gx", "gy"),
        P(None, None, "gx", "gy"),
        P(None, "gx", "gy"),
        P(None, None, "gx", "gy"),
        P(None, "gx", "gy"),
        P(None, "gy", None),
    )
    out_specs = (P(None, None, "gx", "gy"), P("gx", "gy", None), P())

    return jax.shard_map(shards, mesh=mesh, in_specs=in_specs, out_specs=out_specs, check_vma=False)
```

```python
import math
from functools import partial

import jax
import jax.numpy as jnp
from jax import lax
from jax.experimental import pallas as pl
from jax.experimental.pallas import tpu as pltpu
from jax.sharding import PartitionSpec as P


STEPS = 4
SUB = 8
AHEAD = 2

time_step = 0.12


def roll(value, shift, axis=-1):
    axis = axis % value.ndim
    shift = shift % value.shape[axis]
    return value if shift == 0 else pltpu.roll(value, shift, axis)


def lanes_of(shape):
    return lax.broadcasted_iota(jnp.int32, shape, len(shape) - 1)


def layer_derivative(value):
    groups = value.shape[0] // SUB
    parts = [value[SUB * v : SUB * (v + 1)] for v in range(groups)]
    sub = lax.broadcasted_iota(jnp.int32, parts[0].shape, 0)
    shifted = {}

    def at(v):
        if 0 <= v < groups:
            return parts[v]
        if v not in shifted:
            if v >= groups:
                shifted[v] = jnp.where(sub < SUB - 1, roll(parts[v - groups], -1, 0), 0.0)
            else:
                shifted[v] = jnp.where(sub > 0, roll(parts[v + groups], 1, 0), 0.0)
        return shifted[v]

    return jnp.concatenate(
        [at(v - 2) - at(v + 2) + 8.0 * (at(v + 1) - at(v - 1)) for v in range(groups)], 0
    )


def band_matrix(count):
    row = lax.broadcasted_iota(jnp.int32, (count, count), 0)
    col = lax.broadcasted_iota(jnp.int32, (count, count), 1)
    away = row - col
    band = jnp.where(
        away == -2,
        1.0,
        jnp.where(away == 2, -1.0, jnp.where(away == 1, 8.0, jnp.where(away == -1, -8.0, 0.0))),
    )
    return band.astype(jnp.bfloat16)


def banded(value, band):
    high = value.astype(jnp.bfloat16)
    low = (value - high.astype(jnp.float32)).astype(jnp.bfloat16)
    return jnp.dot(high, band, preferred_element_type=jnp.float32) + jnp.dot(
        low, band, preferred_element_type=jnp.float32
    )


def edge_terms(edge, window):
    w = lanes_of(edge.shape) % window
    up_2, up_3 = roll(edge, 2), roll(edge, 3)
    down_2, down_3 = roll(edge, -2), roll(edge, -3)
    right = jnp.where(w == 7, 8.0 * up_3, 0.0) - up_2
    left = down_2 - jnp.where(w == 8, 8.0 * down_3, 0.0)
    return jnp.where((w == 6) | (w == 7), right, left)


def edge_spread(terms, place, window):
    count = terms.shape[-1]
    lane = lanes_of(terms.shape)
    return jnp.where((lane < 2) | (lane >= count - 2), roll(terms, count - 2 - window * place - 6), 0.0)


def edge_message(load, x_count, rows, y_count, which=None):
    window = y_count // x_count
    place = lanes_of((rows, y_count)) // window
    message = None
    for x in which or range(x_count):
        moved = roll(load(x), window * x + 4)
        message = moved if message is None else jnp.where(place == x, moved, message)
    return message


def neighbours():
    at = lax.axis_index("gy")
    return (at > 0).astype(jnp.float32), (at < lax.axis_size("gy") - 1).astype(jnp.float32)


def edge_tile(own, from_left, from_right, has_left, has_right, window):
    w = lanes_of(own.shape) % window
    halo = jnp.where(w < 8, from_right * has_right, roll(from_left, 8) * has_left)
    mine = jnp.where(w < 4, own, roll(own, 8))
    return jnp.where((w >= 4) & (w < 12), halo, mine)


def strided(ref, x_count, rows, index=()):
    groups = rows // SUB

    def at(x):
        return jnp.concatenate(
            [
                ref[(*index, pl.ds(x_count * v + x, SUB, stride=groups * x_count), slice(None))]
                for v in range(groups)
            ],
            0,
        )

    return at


def central(far_low, near_low, near_high, far_high):
    def minus(first, second):
        if second is None:
            return first
        return -second if first is None else first - second

    near, far = minus(near_high, near_low), minus(far_low, far_high)
    if near is None:
        return far
    return 8.0 * near if far is None else far + 8.0 * near


def halves(far_ref, near_ref, half):
    def at(c, x):
        return far_ref[c * half + x] if x < half else near_ref[c * half + x - half]

    return at


def is_odd():
    return lax.axis_index("gx") % 2 == 1


def mirrored(values, odd, flip=False):
    other = [-value if flip else value for value in values[::-1]]
    return [jnp.where(odd, second, first) for first, second in zip(values, other)]


class Side:
    def __init__(self, far, x_count):
        self.far, self.half, self.x_count = far, x_count // 2, x_count
        self.inside = range(self.half) if far else range(self.half, x_count)
        self.outside = (-2, -1) if far else (x_count, x_count + 1)

    def depth(self, x):
        return -1 - x if self.far else x - self.x_count

    def at(self, ref, first, index, x, negate, terms=None):
        place = self.depth(x) if self.far else 1 - self.depth(x)
        value = ref[first + 2 * index + place]
        value = -value if negate else value
        return value if terms is None else value + terms

    def halo(self, ref, c, x, terms=None):
        terms = None if terms is None or c > 1 else terms[self.slot(c, x)]
        return self.at(ref, 0, c, x, c == 0, terms)

    def own_part(self, ref, i, x, terms=None):
        return self.at(ref, 6, i, x, i > 0, None if terms is None else terms[self.slot(2 + i, x)])

    def modulus(self, ref, m, x):
        return self.at(ref, 12, m, x, False)

    def slot(self, index, x):
        return 10 * (not self.far) + 2 * index + self.depth(x)

    def packed(self, ref, f, x, window):
        place = 2 * f + (self.depth(x) if self.far else 1 - self.depth(x))
        value = roll(ref[16], ref.shape[2] - 4 - window * place)
        return -value if f == 1 else value

    def pack(self, messages, window):
        place = lanes_of(messages[0].shape) // (2 * window)
        packed = None
        for f, message in enumerate(messages):
            moved = roll(message, window * (2 * f - (0 if self.far else self.x_count - 2)))
            packed = moved if packed is None else jnp.where(place == f, moved, packed)
        return packed

    def send(self, ref, u, metric):
        for k, x in enumerate(self.inside[:2] if self.far else self.inside[-2:]):
            slope_x, slope_y, stretch, lame, shear = (metric(m, x) for m in range(5))
            dr = [layer_derivative(u(c, x)) for c in range(3)]
            near = [x + j if x + j in self.inside else None for j in (-2, -1, 1, 2)]
            dx = [central(*(None if j is None else u(c, j) for j in near)) for c in range(3)]
            g11 = dx[0] + slope_x * dr[0]
            parts = (
                lame * (g11 + slope_y * dr[1] + stretch * dr[2]) + (shear + shear) * g11,
                shear * (slope_y * dr[0] + dx[1] + slope_x * dr[1]),
                shear * (stretch * dr[0] + dx[2] + slope_x * dr[2]),
            )
            for c in range(3):
                ref[2 * c + k] = u(c, x)
                ref[6 + 2 * c + k] = parts[c]


def begin_kernel(*refs):
    sources, held, sems = refs[:5], refs[11:16], refs[16]
    far_ref, near_ref, far_send, near_send, edge_ref, metric_ref = refs[5:11]
    u_ref, slope_ref, stretch_ref, moduli_ref, buoyancy_ref = held
    copies = [
        pltpu.make_async_copy(source, target, sems.at[i])
        for i, (source, target) in enumerate(zip(sources, held))
    ]
    for copy in copies:
        copy.start()
    copies[0].wait()
    x_count, rows, y_count = metric_ref.shape[1:]
    half = x_count // 2
    comps = u_ref.shape[0]
    odd = is_odd()
    for c in range(comps):
        at = strided(u_ref, x_count, rows, (c,))
        slabs = mirrored([at(x) for x in range(x_count)], odd, c == 0)
        for k in range(half):
            far_ref[c * half + k] = slabs[k]
            near_ref[c * half + k] = slabs[half + k]
        edge_ref[c] = edge_message(lambda x: slabs[x], x_count, rows, y_count)
    for copy in copies[1:]:
        copy.wait()
    fields = [
        (strided(slope_ref, x_count, rows, (0,)), None),
        (strided(slope_ref, x_count, rows, (1,)), None),
        (strided(stretch_ref, x_count, rows), None),
        (strided(moduli_ref, x_count, rows, (0,)), 1.0 / 12.0),
        (strided(moduli_ref, x_count, rows, (1,)), 1.0 / 12.0),
    ]
    for m, (at, scale) in enumerate(fields):
        slabs = mirrored([at(x) for x in range(x_count)], odd, m == 0)
        if scale is not None:
            slabs = [slab * scale for slab in slabs]
        for x in range(x_count):
            metric_ref[m, x] = slabs[x]
        for k in range(2):
            if m > 2:
                far_send[6 + 2 * m + k] = slabs[k]
                near_send[6 + 2 * m + k] = slabs[x_count - 2 + k]
        edge_ref[comps + m] = edge_message(lambda x: slabs[x], x_count, rows, y_count)
    at = strided(buoyancy_ref, x_count, rows)
    slabs = mirrored([at(x) for x in range(x_count)], odd)
    push = edge_message(lambda x: slabs[x], x_count, rows, y_count) * (time_step**2 / 12.0)
    u, window = halves(far_ref, near_ref, half), y_count // x_count
    for far, ref in ((True, far_send), (False, near_send)):
        side = Side(far, x_count)
        side.send(ref, u, lambda m, x: metric_ref[m, x])
        ref[16] = side.pack([push, *(edge_ref[comps + m] for m in range(3))], window)


def rest_kernel(u_ref, v_ref, buoyancy_ref, before_far, before_near, push_ref):
    x_count, rows, _ = push_ref.shape
    half = x_count // 2
    odd = is_odd()
    at = strided(buoyancy_ref, x_count, rows)
    for x, value in enumerate(mirrored([at(x) for x in range(x_count)], odd)):
        push_ref[x] = value * (time_step**2 / 12.0)
    for c in range(u_ref.shape[0]):
        at, rate = strided(u_ref, x_count, rows, (c,)), strided(v_ref, x_count, rows, (c,))
        before = [at(x) - time_step * rate(x) for x in range(x_count)]
        for x, value in enumerate(mirrored(before, odd, c == 0)):
            (before_far if x < half else before_near)[c * half + x % half] = value


def corner_kernel(x_count, fixed, far_ref, near_ref, *refs):
    corner_ref, terms = refs[-1], refs[0] if fixed else None
    rows, y_count = far_ref.shape[1:]
    places = {}
    for far, ref in ((True, far_ref), (False, near_ref)):
        side = Side(far, x_count)
        places.update({x % x_count: (side, ref, x) for x in side.outside})

    def load(c, place):
        side, ref, x = places[place]
        return side.halo(ref, c, x, terms) if c < 2 else side.modulus(ref, c - 2, x)

    for c in range(corner_ref.shape[0]):
        corner_ref[c] = edge_message(
            lambda place: load(c, place), x_count, rows, y_count, tuple(places)
        )


def corner_tile(corner_in, c, window, has_left, has_right):
    w = lanes_of(corner_in[0].shape[1:]) % window
    return jnp.where(w < 8, corner_in[-1][c] * has_right, roll(corner_in[0][c], 8) * has_left)


def beyond_change(value, window, x_count):
    place = lanes_of(value.shape) // window

    def near(k):
        inside = (place + k < x_count) if k > 0 else (place + k >= 0)
        return jnp.where(inside, 0.0, roll(value, -window * k))

    return central(*(near(k) for k in (-2, -1, 1, 2)))


def all_stresses(grads, lame, shear):
    pressure = lame * (grads[0][0] + grads[1][1] + grads[2][2])
    twice = shear + shear
    return (
        pressure + twice * grads[0][0],
        pressure + twice * grads[1][1],
        pressure + twice * grads[2][2],
        shear * (grads[0][1] + grads[1][0]),
        shear * (grads[0][2] + grads[2][0]),
        shear * (grads[1][2] + grads[2][1]),
    )


def tile_kernel(sides, comps, *refs):
    low_ref, high_ref, edge_ref = refs[:3]
    edge_in = refs[3 : 3 + sides]
    metric_ref, first_edge = refs[3 + sides : 5 + sides]
    first_edge_in = refs[5 + sides : 5 + 2 * sides]
    s_x, s_o, e_s = refs[5 + 2 * sides :]
    x_count, rows, y_count = metric_ref.shape[1:]
    half, window = x_count // 2, y_count // x_count
    has_left, has_right = neighbours()
    place = lanes_of((rows, y_count)) // window
    u = halves(low_ref, high_ref, half)
    band = band_matrix(y_count)

    edges, across = [], []
    for c in range(comps):
        edge = edge_tile(edge_ref[c], edge_in[0][c], edge_in[-1][c], has_left, has_right, window)
        terms = edge_terms(edge, window)
        result = banded(jnp.concatenate([u(c, x) for x in range(x_count)], 0), band)
        edges.append(edge)
        across.append(
            [
                result[x * rows : (x + 1) * rows] + edge_spread(terms, x, window)
                for x in range(x_count)
            ]
        )

    def gradients(along, beside, layers, metric):
        return [
            [
                along[c] + metric[0] * layers[c],
                beside[c] + metric[1] * layers[c],
                metric[2] * layers[c],
            ]
            for c in range(comps)
        ]

    for x in range(x_count):
        metric = [metric_ref[m, x] for m in range(5)]

        def near(c, k):
            return u(c, x + k) if 0 <= x + k < x_count else None

        along = [central(*(near(c, k) for k in (-2, -1, 1, 2))) for c in range(comps)]
        layers = [layer_derivative(u(c, x)) for c in range(comps)]
        grads = gradients(along, [across[c][x] for c in range(comps)], layers, metric)
        s11, s22, s33, s12, s13, s23 = all_stresses(grads, metric[3], metric[4])
        s_x[0, x], s_x[1, x], s_x[2, x] = s11, s12, s13
        s_o[0, x], s_o[1, x], s_o[2, x] = s22, s23, s33

    metric = [
        edge_tile(
            first_edge[comps + m], first_edge_in[0][comps + m], first_edge_in[-1][comps + m],
            has_left, has_right, window,
        )
        for m in range(5)
    ]
    along, beside = [], []
    for edge in edges:

        def near(k):
            inside = (place + k < x_count) if k > 0 else (place + k >= 0)
            return jnp.where(inside, roll(edge, -window * k), 0.0)

        along.append(central(*(near(k) for k in (-2, -1, 1, 2))))
        beside.append(central(*(roll(edge, -k) for k in (-2, -1, 1, 2))))
    grads = gradients(along, beside, [layer_derivative(edge) for edge in edges], metric)
    _, e22, _, e12, _, e23 = all_stresses(grads, metric[3], metric[4])
    e_s[0], e_s[1], e_s[2], e_s[3], e_s[4] = e12, e22, e23, metric[3], metric[4]


def wide_kernel(
    far, fixed, send, far_ref, near_ref, halo_ref, before_ref, metric_ref, push_ref, first_halo, s_x,
    s_o, e_s, *refs,
):
    out_ref, out_edge, *sends = refs[-3:] if send else refs[-2:]
    terms = refs[0] if fixed else None
    x_count, rows, y_count = metric_ref.shape[1:]
    half, window = x_count // 2, y_count // x_count
    comps = s_x.shape[0]
    side = Side(far, x_count)
    inner = halves(far_ref, near_ref, half)
    band = band_matrix(y_count)
    steps = (-2, -1, 1, 2)

    def u(c, x):
        return inner(c, x) if 0 <= x < x_count else side.halo(halo_ref, c, x, terms)

    def beyond(x):
        return x < 0 if far else x >= x_count

    along_x, others = {}, {}
    for x in range(side.inside[0] - 2, side.inside[-1] + 3):
        if beyond(x):
            continue
        values = [s_x[i, x] for i in range(3)]
        rest = [s_o[i, x] for i in range(3)] if x in side.inside else None
        if any(beyond(x + k) for k in steps):
            add = [
                central(*(u(c, x + k) if beyond(x + k) else None for k in steps))
                for c in range(comps)
            ]
            lame, shear = metric_ref[3, x], metric_ref[4, x]
            pressure = lame * add[0]
            values[0] = values[0] + pressure + (shear + shear) * add[0]
            values[1] = values[1] + shear * add[1]
            values[2] = values[2] + shear * add[2]
            rest[0] = rest[0] + pressure
            rest[2] = rest[2] + pressure
        along_x[x], others[x] = values, rest

    across = [
        banded(jnp.concatenate([u(c, x) for x in side.outside], 0), band) for c in range(2)
    ]
    for place, x in enumerate(side.outside):
        lame, shear = (side.modulus(first_halo, m, x) for m in range(2))
        dx = [
            central(*(u(c, x + k) if 0 <= x + k < x_count else None for k in steps))
            for c in range(comps)
        ]
        dy = [across[c][place * rows : (place + 1) * rows] for c in range(2)]
        values = [side.own_part(halo_ref, i, x, terms) for i in range(3)]
        values[0] = values[0] + lame * (dx[0] + dy[1]) + (shear + shear) * dx[0]
        values[1] = values[1] + shear * (dy[0] + dx[1])
        values[2] = values[2] + shear * dx[2]
        along_x[x] = values

    def across_of(i, x):
        return along_x[x][1] if i == 0 else others[x][i - 1]

    beside = []
    for i in range(comps):
        result = banded(jnp.concatenate([across_of(i, x) for x in side.inside], 0), band)
        added = edge_terms(e_s[i], window)
        beside.append(
            {
                x: result[k * rows : (k + 1) * rows] + edge_spread(added, x, window)
                for k, x in enumerate(side.inside)
            }
        )

    place = lanes_of((rows, y_count)) // window
    messages = [None] * comps
    for k, x in enumerate(side.inside):
        slope_x, slope_y, stretch = (metric_ref[m, x] for m in range(3))
        r11, r12, r13 = (layer_derivative(value) for value in along_x[x])
        r22, r23, r33 = (layer_derivative(value) for value in others[x])
        layers = ((r11, r12, r13), (r12, r22, r23), (r13, r23, r33))
        for c in range(comps):
            force = central(*(along_x[x + j][c] for j in steps)) + beside[c][x]
            force = force + slope_x * layers[c][0] + slope_y * layers[c][1]
            force = force + stretch * layers[c][2]
            at = c * half + k
            following = 2.0 * inner(c, x) - before_ref[at] + force * push_ref[x]
            out_ref[at] = following
            moved = roll(following, window * x + 4)
            messages[c] = moved if k == 0 else jnp.where(place == x, moved, messages[c])
    for c in range(comps):
        out_edge[c] = messages[c]
    if send:
        side.send(
            sends[0],
            lambda c, x: out_ref[c * half + x - side.inside[0]],
            lambda m, x: metric_ref[m, x],
        )


def fix_kernel(sides, *refs):
    corner_in = refs[:sides]
    first_far, first_near, e_s, push_ref = refs[sides : 4 + sides]
    in_far, in_near, far_edge, near_edge = refs[4 + sides : 8 + sides]
    out_far, out_near, *out_edge = refs[8 + sides :]
    x_count, rows, y_count = push_ref.shape
    half, window = x_count // 2, y_count // x_count
    comps = far_edge.shape[0]
    has_left, has_right = neighbours()
    place = lanes_of((rows, y_count)) // window
    lame, shear = 3, 4
    steps = (-2, -1, 1, 2)

    corners = [corner_tile(corner_in, c, window, has_left, has_right) for c in range(2)]
    terms = [edge_terms(corner, window) for corner in corners]
    beside = [
        edge_terms(e_s[shear] * beyond_change(corners[1], window, x_count), window),
        edge_terms(e_s[lame] * beyond_change(corners[0], window, x_count), window),
    ]
    for c in range(comps):
        message = jnp.where(place < half, far_edge[c], near_edge[c])
        for far, first, in_ref, out_ref in (
            (True, first_far, in_far, out_far),
            (False, first_near, in_near, out_near),
        ):
            side = Side(far, x_count)
            changes = {}
            if c < 2:
                changes = {
                    x: side.modulus(first, c, x)
                    * edge_spread(terms[1 - c], x % x_count, window)
                    for x in side.outside
                }
            for k, x in enumerate(side.inside):
                value = in_ref[c * half + k]
                near = [changes.get(x + j) for j in steps]
                if any(item is not None for item in near):
                    change = central(*near) + edge_spread(beside[c], x, window)
                    value = value + change * push_ref[x]
                    message = jnp.where(place == x, roll(value, window * x + 4), message)
                out_ref[c * half + k] = value
        if out_edge:
            out_edge[0][c] = message


def partner_kernel(sides, edge_ref, *refs):
    edge_in = refs[:sides]
    metric_ref, first_far, first_near = refs[sides : 3 + sides]
    moduli_in = refs[3 + sides : 3 + 2 * sides]
    out_ref = refs[3 + 2 * sides]
    x_count, _, y_count = metric_ref.shape[1:]
    window = y_count // x_count
    has_left, has_right = neighbours()
    edges = [
        edge_tile(edge_ref[c], edge_in[0][c], edge_in[-1][c], has_left, has_right, window)
        for c in range(2)
    ]
    lame, shear = (corner_tile(moduli_in, 2 + m, window, has_left, has_right) for m in range(2))
    terms = [edge_terms(edge, window) for edge in edges]
    beside = [
        edge_terms(shear * beyond_change(edges[1], window, x_count), window),
        edge_terms(lame * beyond_change(edges[0], window, x_count), window),
    ]
    for far, first in ((True, first_far), (False, first_near)):
        side = Side(far, x_count)
        added = {}
        for c in range(2):
            changes = {
                x: metric_ref[3 + c, x] * edge_spread(terms[1 - c], x, window)
                for x in (side.inside[:2] if far else side.inside[-2:])
            }
            for x in side.outside:
                near = [changes.get(x + k) for k in (-2, -1, 1, 2)]
                change = central(*near) + edge_spread(beside[c], x % x_count, window)
                change = change * side.packed(first, 0, x, window)
                added[c, x] = out_ref[side.slot(c, x)] = change
        for x in side.outside:
            slope_x, slope_y, stretch = (side.packed(first, 1 + m, x, window) for m in range(3))
            own_lame, own_shear = (side.modulus(first, m, x) for m in range(2))
            dr = [layer_derivative(added[c, x]) for c in range(2)]
            near = [added.get((c, x + k)) for c in range(2) for k in (-2, -1, 1, 2)]
            dx = [central(*near[:4]), central(*near[4:])]
            g11 = dx[0] + slope_x * dr[0]
            out_ref[side.slot(2, x)] = (
                own_lame * (g11 + slope_y * dr[1]) + (own_shear + own_shear) * g11
            )
            out_ref[side.slot(3, x)] = own_shear * (slope_y * dr[0] + dx[1] + slope_x * dr[1])
            out_ref[side.slot(4, x)] = own_shear * (stretch * dr[0])


def sketch_kernel(moment, last, shape, *refs):
    comps, half, rows, y_count = shape
    far_ref, near_ref, before_far, before_near, probe_ref = refs[:5]
    sketch_in = None if moment == 0 else refs[5]
    sketch_ref, spread = refs[-2:]
    x_count = 2 * half
    groups = rows // SUB
    picked = groups // 2
    now = halves(far_ref, near_ref, half)
    past = halves(before_far, before_near, half)
    odd = is_odd()
    spread[...] = jnp.zeros_like(spread)
    spread[pl.ds(0, y_count // 2, stride=2), :] = probe_ref[moment]
    rates = []
    for x in range(0, x_count, 2):
        for c in range(comps):
            rate = now(c, x) - past(c, x)
            other = now(c, x_count - 1 - x) - past(c, x_count - 1 - x)
            rate = jnp.where(odd, -other if c == 0 else other, rate) * (0.5 / time_step)
            rates += [rate[SUB * v : SUB * (v + 1)] for v in range(0, groups, 2)]
    sketch = jnp.dot(
        jnp.concatenate(rates, 0),
        spread[...],
        precision=lax.Precision.HIGHEST,
        preferred_element_type=jnp.float32,
    )
    if sketch_in is not None:
        sketch = sketch + sketch_in[...]
    if last:
        for k in range(half * comps):
            for v in range(picked):
                start = (k * picked + v) * SUB
                sketch_ref[pl.ds(k * picked * SUB + v, SUB, stride=picked), :] = sketch[
                    start : start + SUB
                ]
    else:
        sketch_ref[...] = sketch


def finish_kernel(half, rows, far_ref, near_ref, out_ref):
    x_count, groups = 2 * half, rows // SUB
    now = halves(far_ref, near_ref, half)
    odd = is_odd()
    for c in range(out_ref.shape[0]):
        values = mirrored([now(c, x) for x in range(x_count)], odd, c == 0)
        for x, value in enumerate(values):
            for v in range(groups):
                out_ref[c, pl.ds(x_count * v + x, SUB, stride=groups * x_count), :] = value[
                    SUB * v : SUB * (v + 1)
                ]


def gram_kernel(*refs):
    sum_ref, packed_ref = refs[-2:]
    total = sum_of([ref[...] for ref in refs[:-2]])
    sum_ref[...] = total
    gram = lax.dot_general(
        total,
        total,
        (((0,), (0,)), ((), ())),
        precision=lax.Precision.HIGHEST,
        preferred_element_type=jnp.float32,
    )
    order = gram.shape[0]
    mid = order // 2
    top, bottom = gram[:mid], gram[mid:]
    row = lax.broadcasted_iota(jnp.int32, (mid, order), 0)
    column = lanes_of((mid, order)) - mid
    packed_ref[:mid] = jnp.where((column >= 0) & (row >= column), roll(top, mid), bottom)
    diagonal = jnp.sum(jnp.where(row == column, bottom, 0.0), 0, keepdims=True)
    packed_ref[mid:] = jnp.broadcast_to(diagonal, (packed_ref.shape[0] - mid, order))


def unpacked(packed):
    order = packed.shape[1]
    mid = order // 2
    row = lax.broadcasted_iota(jnp.int32, (mid, order), 0)
    lane = lanes_of((mid, order))
    column = lane - mid
    main = packed[:mid]
    diagonal = jnp.broadcast_to(packed[mid : mid + 1], (mid, order))
    moved = roll(main, mid)
    top = jnp.where(row > lane, moved, jnp.where(row == lane, 0.5 * moved, 0.0))
    bottom = jnp.where(
        (column < 0) | (row < column), main, jnp.where(row == column, 0.5 * diagonal, 0.0)
    )
    part = jnp.concatenate([top, bottom], 0)
    return part + part.T


def factor_kernel(scale, tall_ref, *refs):
    basis_ref, factor_ref = refs[-2:]
    gram = unpacked(sum_of([ref[...] for ref in refs[:-2]]))
    order = gram.shape[0]
    blocks = order // SUB
    shape = (SUB, order)
    sub = lax.broadcasted_iota(jnp.int32, shape, 0)
    lane = lanes_of(shape)
    work = [gram[SUB * q : SUB * (q + 1)] for q in range(blocks)]
    other = [jnp.where(lane == sub + SUB * q, 1.0, 0.0) for q in range(blocks)]
    inverse_rows = []

    def row_of(value, k):
        return jnp.broadcast_to(value[k : k + 1, :], value.shape)

    def column_of(value, j):
        return jnp.broadcast_to(value[:, j : j + 1], value.shape)

    for p in range(blocks):
        columns = [column_of(work[p], SUB * p + k) for k in range(SUB)]
        after_panel = min(p + 1 + AHEAD, blocks)
        ahead = {
            q: [column_of(work[q], SUB * p + k) for k in range(SUB)]
            for q in range(p + 1, after_panel)
        }
        upper = solved = work[p]
        lower = solved_other = other[p]
        pivots = inverses = columns[0]
        for k in range(SUB):
            pivot = row_of(columns[k], k)
            inverse = 1.0 / pivot
            every = jnp.where(sub != k, columns[k] * inverse, 0.0)
            after = jnp.where(sub > k, every, 0.0)
            for m in range(k + 1, SUB):
                columns[m] = columns[m] - every * row_of(columns[m], k)
            upper = upper - after * row_of(upper, k)
            lower = lower - after * row_of(lower, k)
            solved = solved - every * row_of(solved, k)
            solved_other = solved_other - every * row_of(solved_other, k)
            pivots = jnp.where(sub == k, pivot, pivots)
            inverses = jnp.where(sub == k, inverse, inverses)
        root = lax.rsqrt(pivots)
        factor_ref[SUB * p : SUB * (p + 1), :] = jnp.where(lane >= sub + SUB * p, upper * root, 0.0)
        inverse_rows.append(lower * root * scale)
        solved, solved_other = solved * inverses, solved_other * inverses
        for q, entries in ahead.items():
            for k, column in enumerate(entries):
                work[q] = work[q] - column * row_of(solved, k)
                other[q] = other[q] - column * row_of(solved_other, k)
        if after_panel < blocks:
            both = jnp.concatenate([solved, solved_other], 1)
            parts = [jnp.zeros((SUB * p, 2 * order), jnp.float32)] if p else []
            parts += [both, jnp.zeros((order - SUB * (p + 1), 2 * order), jnp.float32)]
            change = jnp.dot(
                jnp.concatenate(work[after_panel:], 0),
                jnp.concatenate(parts, 0),
                precision=lax.Precision.HIGHEST,
                preferred_element_type=jnp.float32,
            )
            for i, q in enumerate(range(after_panel, blocks)):
                work[q] = work[q] - change[SUB * i : SUB * (i + 1), :order]
                other[q] = other[q] - change[SUB * i : SUB * (i + 1), order:]

    inverse_lower = jnp.concatenate(inverse_rows, 0)
    count, kept = basis_ref.shape[0], basis_ref.shape[1]
    start = pl.multiple_of(lax.axis_index("gy") * kept, SUB)
    tall = jnp.concatenate([tall_ref[k, pl.ds(start, kept), :] for k in range(count)], 0)
    basis = lax.dot_general(
        tall,
        inverse_lower,
        (((1,), (1,)), ((), ())),
        precision=lax.Precision.HIGHEST,
        preferred_element_type=jnp.float32,
    )
    for k in range(count):
        basis_ref[k] = basis[k * kept : (k + 1) * kept]


def f32(*shape):
    return jax.ShapeDtypeStruct(shape, jnp.float32)


VMEM = pl.BlockSpec(memory_space=pltpu.MemorySpace.VMEM)
ANY = pl.BlockSpec(memory_space=pl.ANY)
HBM = pl.BlockSpec(memory_space=pltpu.MemorySpace.HBM)


def call(kernel, outs, ins, specs=None, scratch=(), flops=0):
    size = sum(math.prod(x.shape) * 4 for x in (*ins, *outs))
    return pl.pallas_call(
        kernel,
        out_shape=outs,
        in_specs=specs or [VMEM] * len(ins),
        out_specs=[VMEM] * len(outs),
        scratch_shapes=list(scratch),
        compiler_params=pltpu.CompilerParams(vmem_limit_bytes=24 * 2**20),
        cost_estimate=pl.CostEstimate(flops=flops, bytes_accessed=size, transcendentals=0),
    )(*ins)


def butterfly(value, axis):
    count = lax.axis_size(axis)
    if count & (count - 1):
        return [lax.psum(value, axis)]
    bit, terms = 1, [value]
    while bit < count:
        value = sum_of(terms)
        moves = [bit] if 2 * bit == count else [bit, 2 * bit, 3 * bit]
        others = [
            lax.ppermute(value, axis, [(i, i ^ move) for i in range(count)]) for move in moves
        ]
        terms = [value, *others]
        bit *= 2 if len(moves) == 1 else 4
    return terms


def sum_of(terms):
    if len(terms) == 1:
        return terms[0]
    return sum_of(terms[: len(terms) // 2]) + sum_of(terms[len(terms) // 2 :])


def shards(displacement, velocity, slopes, stretch, moduli, buoyancy, probes):
    comps, layers, x_count, y_count = displacement.shape
    width = probes.shape[2]
    half = x_count // 2
    n_x, n_y = lax.axis_size("gx"), lax.axis_size("gy")
    sides = 1 if n_y == 2 else 2

    def flat(array):
        return array.reshape(array.shape[:-3] + (layers * x_count, y_count))

    def exchange(value, far):
        pairs = [(i, i + 1) for i in range(1 if far else 0, n_x - 1, 2)]
        return lax.ppermute(value, "gx", pairs + [(k, i) for i, k in pairs])

    def along_y(value):
        if sides == 1:
            return [lax.ppermute(value, "gy", [(0, 1), (1, 0)])]
        return [
            lax.ppermute(value, "gy", [(i, i + s) for i in range(n_y) if 0 <= i + s < n_y])
            for s in (1, -1)
        ]

    def slabs(count):
        return f32(count, layers, y_count)

    u_flat = flat(displacement)
    fields = [
        pltpu.with_memory_space_constraint(field, pltpu.MemorySpace.HBM)
        for field in (u_flat, flat(slopes), flat(stretch), flat(moduli), flat(buoyancy))
    ]
    u_far, u_near, far_send, near_send, edge, metric = call(
        begin_kernel,
        [
            slabs(comps * half), slabs(comps * half), slabs(17), slabs(17), slabs(comps + 5),
            f32(5, x_count, layers, y_count),
        ],
        fields,
        specs=[HBM] * 5,
        scratch=[pltpu.VMEM(field.shape, jnp.float32) for field in fields]
        + [pltpu.SemaphoreType.DMA((5,))],
    )
    before_far, before_near, push = call(
        rest_kernel,
        [slabs(comps * half), slabs(comps * half), slabs(x_count)],
        [u_flat, flat(velocity), flat(buoyancy)],
    )

    sketch_rows = half * comps * (layers // 2)
    sketch = []

    def half_step(far, moment, halo, first_halo, before, terms, token):
        return call(
            partial(wide_kernel, far, len(terms), moment < STEPS - 1),
            [slabs(comps * half), slabs(comps)] + ([slabs(12)] if moment < STEPS - 1 else []),
            [
                u_far, u_near, halo, before, metric, push, first_halo, s_x, s_o, e_s, *terms, *token,
            ],
            specs=[VMEM] * (10 + len(terms)) + [ANY] * len(token),
            flops=10_000_000,
        )

    terms = []
    for moment in range(STEPS):
        last = moment == STEPS - 1
        if moment == 0:
            far_halo = exchange(far_send, True)
            near_halo = exchange(near_send, False)
        edge_in = along_y(edge)
        if moment == 0:
            first_edge, first_edge_in, first_far, first_near = edge, edge_in, far_halo, near_halo
        s_x, s_o, e_s = call(
            partial(tile_kernel, sides, comps),
            [f32(comps, x_count, layers, y_count), f32(3, x_count, layers, y_count), slabs(5)],
            [u_far, u_near, edge, *edge_in, metric, first_edge, *first_edge_in],
            flops=20_000_000,
        )
        raw_far, far_edge, *far_send = half_step(
            True, moment, far_halo, first_far, before_far, terms, sketch or [push, near_halo]
        )
        (corner,) = call(
            partial(corner_kernel, x_count, len(terms)),
            [slabs(2 if moment else 4)],
            [far_halo, near_halo, *terms, raw_far],
            specs=[VMEM] * (2 + len(terms)) + [ANY],
        )
        corner_in = along_y(corner)
        if moment == 0:
            moduli_in = corner_in
        raw_near, near_edge, *near_send = half_step(
            False, moment, near_halo, first_near, before_near, terms, [raw_far]
        )
        if not last:
            far_halo = exchange(far_send[0], True)
            near_halo = exchange(near_send[0], False)
            terms = call(
                partial(partner_kernel, sides),
                [slabs(20)],
                [edge, *edge_in, metric, first_far, first_near, *moduli_in],
            )
        next_far, next_near, *edge = call(
            partial(fix_kernel, sides),
            [slabs(comps * half), slabs(comps * half)] + ([] if last else [slabs(comps)]),
            [
                *corner_in, first_far, first_near, e_s, push, raw_far, raw_near, far_edge, near_edge,
            ],
        )
        edge = None if last else edge[0]
        sketch = call(
            partial(sketch_kernel, moment, last, (comps, half, layers, y_count)),
            [f32(sketch_rows, width)],
            [next_far, next_near, before_far, before_near, probes, *sketch],
            scratch=[pltpu.VMEM((y_count, width), jnp.float32)],
        )
        before_far, before_near, u_far, u_near = u_far, u_near, next_far, next_near
    (final,) = call(
        partial(finish_kernel, half, layers),
        [f32(comps, layers * x_count, y_count)],
        [u_far, u_near],
    )
    final = final.reshape(displacement.shape)

    parts = butterfly(sketch[0], "gy")
    tall, packed = call(gram_kernel, [f32(sketch_rows, width), f32(width // 2 + SUB, width)], parts)
    parts = butterfly(packed, "gx")
    depth = comps * (layers // 2)
    basis, factor = call(
        partial(factor_kernel, math.sqrt(sketch_rows * n_x)),
        [f32(half, depth // n_y, width), f32(width, width)],
        [tall.reshape(half, depth, width), *parts],
    )
    return (final, basis, factor)


def solution(mesh):
    in_specs = (
        P(None, None, "gx", "gy"),
        P(None, None, "gx", "gy"),
        P(None, None, "gx", "gy"),
        P(None, "gx", "gy"),
        P(None, None, "gx", "gy"),
        P(None, "gx", "gy"),
        P(None, "gy", None),
    )
    out_specs = (P(None, None, "gx", "gy"), P("gx", "gy", None), P())

    return jax.shard_map(shards, mesh=mesh, in_specs=in_specs, out_specs=out_specs, check_vma=False)
```

```python
import math
from functools import partial

import jax
import jax.numpy as jnp
from jax import lax
from jax.experimental import pallas as pl
from jax.experimental.pallas import tpu as pltpu
from jax.sharding import PartitionSpec as P


STEPS = 4
SUB = 8
AHEAD = 3

time_step = 0.12


def roll(value, shift, axis=-1):
    axis = axis % value.ndim
    shift = shift % value.shape[axis]
    return value if shift == 0 else pltpu.roll(value, shift, axis)


def lanes_of(shape):
    return lax.broadcasted_iota(jnp.int32, shape, len(shape) - 1)


def layer_derivative(value):
    groups = value.shape[0] // SUB
    parts = [value[SUB * v : SUB * (v + 1)] for v in range(groups)]
    sub = lax.broadcasted_iota(jnp.int32, parts[0].shape, 0)
    shifted = {}

    def at(v):
        if 0 <= v < groups:
            return parts[v]
        if v not in shifted:
            if v >= groups:
                shifted[v] = jnp.where(sub < SUB - 1, roll(parts[v - groups], -1, 0), 0.0)
            else:
                shifted[v] = jnp.where(sub > 0, roll(parts[v + groups], 1, 0), 0.0)
        return shifted[v]

    return jnp.concatenate(
        [at(v - 2) - at(v + 2) + 8.0 * (at(v + 1) - at(v - 1)) for v in range(groups)], 0
    )


def band_matrix(count):
    row = lax.broadcasted_iota(jnp.int32, (count, count), 0)
    col = lax.broadcasted_iota(jnp.int32, (count, count), 1)
    away = row - col
    band = jnp.where(
        away == -2,
        1.0,
        jnp.where(away == 2, -1.0, jnp.where(away == 1, 8.0, jnp.where(away == -1, -8.0, 0.0))),
    )
    return band.astype(jnp.bfloat16)


def banded(value, band):
    high = value.astype(jnp.bfloat16)
    low = (value - high.astype(jnp.float32)).astype(jnp.bfloat16)
    return jnp.dot(high, band, preferred_element_type=jnp.float32) + jnp.dot(
        low, band, preferred_element_type=jnp.float32
    )


def edge_terms(edge, window):
    w = lanes_of(edge.shape) % window
    up_2, up_3 = roll(edge, 2), roll(edge, 3)
    down_2, down_3 = roll(edge, -2), roll(edge, -3)
    right = jnp.where(w == 7, 8.0 * up_3, 0.0) - up_2
    left = down_2 - jnp.where(w == 8, 8.0 * down_3, 0.0)
    return jnp.where((w == 6) | (w == 7), right, left)


def edge_spread(terms, place, window):
    count = terms.shape[-1]
    lane = lanes_of(terms.shape)
    return jnp.where((lane < 2) | (lane >= count - 2), roll(terms, count - 2 - window * place - 6), 0.0)


def edge_message(load, x_count, rows, y_count, which=None):
    window = y_count // x_count
    place = lanes_of((rows, y_count)) // window
    message = None
    for x in which or range(x_count):
        moved = roll(load(x), window * x + 4)
        message = moved if message is None else jnp.where(place == x, moved, message)
    return message


def neighbours():
    at = lax.axis_index("gy")
    return (at > 0).astype(jnp.float32), (at < lax.axis_size("gy") - 1).astype(jnp.float32)


def edge_tile(own, from_left, from_right, has_left, has_right, window):
    w = lanes_of(own.shape) % window
    halo = jnp.where(w < 8, from_right * has_right, roll(from_left, 8) * has_left)
    mine = jnp.where(w < 4, own, roll(own, 8))
    return jnp.where((w >= 4) & (w < 12), halo, mine)


def strided(ref, x_count, rows, index=()):
    groups = rows // SUB

    def at(x):
        return jnp.concatenate(
            [
                ref[(*index, pl.ds(x_count * v + x, SUB, stride=groups * x_count), slice(None))]
                for v in range(groups)
            ],
            0,
        )

    return at


def central(far_low, near_low, near_high, far_high):
    def minus(first, second):
        if second is None:
            return first
        return -second if first is None else first - second

    near, far = minus(near_high, near_low), minus(far_low, far_high)
    if near is None:
        return far
    return 8.0 * near if far is None else far + 8.0 * near


def halves(far_ref, near_ref, half):
    def at(c, x):
        return far_ref[c * half + x] if x < half else near_ref[c * half + x - half]

    return at


def is_odd():
    return lax.axis_index("gx") % 2 == 1


def mirrored(values, odd, flip=False):
    other = [-value if flip else value for value in values[::-1]]
    return [jnp.where(odd, second, first) for first, second in zip(values, other)]


class Side:
    def __init__(self, far, x_count):
        self.far, self.half, self.x_count = far, x_count // 2, x_count
        self.inside = range(self.half) if far else range(self.half, x_count)
        self.outside = (-2, -1) if far else (x_count, x_count + 1)

    def depth(self, x):
        return -1 - x if self.far else x - self.x_count

    def at(self, ref, first, index, x, negate, terms=None):
        place = self.depth(x) if self.far else 1 - self.depth(x)
        value = ref[first + 2 * index + place]
        value = -value if negate else value
        return value if terms is None else value + terms

    def halo(self, ref, c, x, terms=None):
        terms = None if terms is None or c > 1 else terms[self.slot(c, x)]
        return self.at(ref, 0, c, x, c == 0, terms)

    def own_part(self, ref, i, x, terms=None):
        return self.at(ref, 6, i, x, i > 0, None if terms is None else terms[self.slot(2 + i, x)])

    def modulus(self, ref, m, x):
        return self.at(ref, 12, m, x, False)

    def slot(self, index, x):
        return 10 * (not self.far) + 2 * index + self.depth(x)

    def packed(self, ref, f, x, window):
        place = 2 * f + (self.depth(x) if self.far else 1 - self.depth(x))
        value = roll(ref[16], ref.shape[2] - 4 - window * place)
        return -value if f == 1 else value

    def pack(self, messages, window):
        place = lanes_of(messages[0].shape) // (2 * window)
        packed = None
        for f, message in enumerate(messages):
            moved = roll(message, window * (2 * f - (0 if self.far else self.x_count - 2)))
            packed = moved if packed is None else jnp.where(place == f, moved, packed)
        return packed

    def send(self, ref, u, metric):
        for k, x in enumerate(self.inside[:2] if self.far else self.inside[-2:]):
            slope_x, slope_y, stretch, lame, shear = (metric(m, x) for m in range(5))
            dr = [layer_derivative(u(c, x)) for c in range(3)]
            near = [x + j if x + j in self.inside else None for j in (-2, -1, 1, 2)]
            dx = [central(*(None if j is None else u(c, j) for j in near)) for c in range(3)]
            g11 = dx[0] + slope_x * dr[0]
            parts = (
                lame * (g11 + slope_y * dr[1] + stretch * dr[2]) + (shear + shear) * g11,
                shear * (slope_y * dr[0] + dx[1] + slope_x * dr[1]),
                shear * (stretch * dr[0] + dx[2] + slope_x * dr[2]),
            )
            for c in range(3):
                ref[2 * c + k] = u(c, x)
                ref[6 + 2 * c + k] = parts[c]


def begin_kernel(*refs):
    sources, held, sems = refs[:5], refs[11:16], refs[16]
    far_ref, near_ref, far_send, near_send, edge_ref, metric_ref = refs[5:11]
    u_ref, slope_ref, stretch_ref, moduli_ref, buoyancy_ref = held
    copies = [
        pltpu.make_async_copy(source, target, sems.at[i])
        for i, (source, target) in enumerate(zip(sources, held))
    ]
    for copy in copies:
        copy.start()
    copies[0].wait()
    x_count, rows, y_count = metric_ref.shape[1:]
    half = x_count // 2
    comps = u_ref.shape[0]
    odd = is_odd()
    for c in range(comps):
        at = strided(u_ref, x_count, rows, (c,))
        slabs = mirrored([at(x) for x in range(x_count)], odd, c == 0)
        for k in range(half):
            far_ref[c * half + k] = slabs[k]
            near_ref[c * half + k] = slabs[half + k]
        edge_ref[c] = edge_message(lambda x: slabs[x], x_count, rows, y_count)
    for copy in copies[1:]:
        copy.wait()
    fields = [
        (strided(slope_ref, x_count, rows, (0,)), None),
        (strided(slope_ref, x_count, rows, (1,)), None),
        (strided(stretch_ref, x_count, rows), None),
        (strided(moduli_ref, x_count, rows, (0,)), 1.0 / 12.0),
        (strided(moduli_ref, x_count, rows, (1,)), 1.0 / 12.0),
    ]
    for m, (at, scale) in enumerate(fields):
        slabs = mirrored([at(x) for x in range(x_count)], odd, m == 0)
        if scale is not None:
            slabs = [slab * scale for slab in slabs]
        for x in range(x_count):
            metric_ref[m, x] = slabs[x]
        for k in range(2):
            if m > 2:
                far_send[6 + 2 * m + k] = slabs[k]
                near_send[6 + 2 * m + k] = slabs[x_count - 2 + k]
        edge_ref[comps + m] = edge_message(lambda x: slabs[x], x_count, rows, y_count)
    at = strided(buoyancy_ref, x_count, rows)
    slabs = mirrored([at(x) for x in range(x_count)], odd)
    push = edge_message(lambda x: slabs[x], x_count, rows, y_count) * (time_step**2 / 12.0)
    u, window = halves(far_ref, near_ref, half), y_count // x_count
    for far, ref in ((True, far_send), (False, near_send)):
        side = Side(far, x_count)
        side.send(ref, u, lambda m, x: metric_ref[m, x])
        ref[16] = side.pack([push, *(edge_ref[comps + m] for m in range(3))], window)


def rest_kernel(u_ref, v_ref, buoyancy_ref, before_far, before_near, push_ref):
    x_count, rows, _ = push_ref.shape
    half = x_count // 2
    odd = is_odd()
    at = strided(buoyancy_ref, x_count, rows)
    for x, value in enumerate(mirrored([at(x) for x in range(x_count)], odd)):
        push_ref[x] = value * (time_step**2 / 12.0)
    for c in range(u_ref.shape[0]):
        at, rate = strided(u_ref, x_count, rows, (c,)), strided(v_ref, x_count, rows, (c,))
        before = [at(x) - time_step * rate(x) for x in range(x_count)]
        for x, value in enumerate(mirrored(before, odd, c == 0)):
            (before_far if x < half else before_near)[c * half + x % half] = value


def corner_kernel(x_count, fixed, far_ref, near_ref, *refs):
    corner_ref, terms = refs[-1], refs[0] if fixed else None
    rows, y_count = far_ref.shape[1:]
    places = {}
    for far, ref in ((True, far_ref), (False, near_ref)):
        side = Side(far, x_count)
        places.update({x % x_count: (side, ref, x) for x in side.outside})

    def load(c, place):
        side, ref, x = places[place]
        return side.halo(ref, c, x, terms) if c < 2 else side.modulus(ref, c - 2, x)

    for c in range(corner_ref.shape[0]):
        corner_ref[c] = edge_message(
            lambda place: load(c, place), x_count, rows, y_count, tuple(places)
        )


def corner_tile(corner_in, c, window, has_left, has_right):
    w = lanes_of(corner_in[0].shape[1:]) % window
    return jnp.where(w < 8, corner_in[-1][c] * has_right, roll(corner_in[0][c], 8) * has_left)


def beyond_change(value, window, x_count):
    place = lanes_of(value.shape) // window

    def near(k):
        inside = (place + k < x_count) if k > 0 else (place + k >= 0)
        return jnp.where(inside, 0.0, roll(value, -window * k))

    return central(*(near(k) for k in (-2, -1, 1, 2)))


def all_stresses(grads, lame, shear):
    pressure = lame * (grads[0][0] + grads[1][1] + grads[2][2])
    twice = shear + shear
    return (
        pressure + twice * grads[0][0],
        pressure + twice * grads[1][1],
        pressure + twice * grads[2][2],
        shear * (grads[0][1] + grads[1][0]),
        shear * (grads[0][2] + grads[2][0]),
        shear * (grads[1][2] + grads[2][1]),
    )


def tile_kernel(sides, comps, *refs):
    low_ref, high_ref, edge_ref = refs[:3]
    edge_in = refs[3 : 3 + sides]
    metric_ref, first_edge = refs[3 + sides : 5 + sides]
    first_edge_in = refs[5 + sides : 5 + 2 * sides]
    s_x, s_o, e_s = refs[5 + 2 * sides :]
    x_count, rows, y_count = metric_ref.shape[1:]
    half, window = x_count // 2, y_count // x_count
    has_left, has_right = neighbours()
    place = lanes_of((rows, y_count)) // window
    u = halves(low_ref, high_ref, half)
    band = band_matrix(y_count)

    edges, across = [], []
    for c in range(comps):
        edge = edge_tile(edge_ref[c], edge_in[0][c], edge_in[-1][c], has_left, has_right, window)
        terms = edge_terms(edge, window)
        result = banded(jnp.concatenate([u(c, x) for x in range(x_count)], 0), band)
        edges.append(edge)
        across.append(
            [
                result[x * rows : (x + 1) * rows] + edge_spread(terms, x, window)
                for x in range(x_count)
            ]
        )

    def gradients(along, beside, layers, metric):
        return [
            [
                along[c] + metric[0] * layers[c],
                beside[c] + metric[1] * layers[c],
                metric[2] * layers[c],
            ]
            for c in range(comps)
        ]

    for x in range(x_count):
        metric = [metric_ref[m, x] for m in range(5)]

        def near(c, k):
            return u(c, x + k) if 0 <= x + k < x_count else None

        along = [central(*(near(c, k) for k in (-2, -1, 1, 2))) for c in range(comps)]
        layers = [layer_derivative(u(c, x)) for c in range(comps)]
        grads = gradients(along, [across[c][x] for c in range(comps)], layers, metric)
        s11, s22, s33, s12, s13, s23 = all_stresses(grads, metric[3], metric[4])
        s_x[0, x], s_x[1, x], s_x[2, x] = s11, s12, s13
        s_o[0, x], s_o[1, x], s_o[2, x] = s22, s23, s33

    metric = [
        edge_tile(
            first_edge[comps + m], first_edge_in[0][comps + m], first_edge_in[-1][comps + m],
            has_left, has_right, window,
        )
        for m in range(5)
    ]
    along, beside = [], []
    for edge in edges:

        def near(k):
            inside = (place + k < x_count) if k > 0 else (place + k >= 0)
            return jnp.where(inside, roll(edge, -window * k), 0.0)

        along.append(central(*(near(k) for k in (-2, -1, 1, 2))))
        beside.append(central(*(roll(edge, -k) for k in (-2, -1, 1, 2))))
    grads = gradients(along, beside, [layer_derivative(edge) for edge in edges], metric)
    _, e22, _, e12, _, e23 = all_stresses(grads, metric[3], metric[4])
    e_s[0], e_s[1], e_s[2], e_s[3], e_s[4] = e12, e22, e23, metric[3], metric[4]


def wide_kernel(
    far, fixed, send, far_ref, near_ref, halo_ref, before_ref, metric_ref, push_ref, first_halo, s_x,
    s_o, e_s, *refs,
):
    out_ref, out_edge, *sends = refs[-3:] if send else refs[-2:]
    terms = refs[0] if fixed else None
    x_count, rows, y_count = metric_ref.shape[1:]
    half, window = x_count // 2, y_count // x_count
    comps = s_x.shape[0]
    side = Side(far, x_count)
    inner = halves(far_ref, near_ref, half)
    band = band_matrix(y_count)
    steps = (-2, -1, 1, 2)

    def u(c, x):
        return inner(c, x) if 0 <= x < x_count else side.halo(halo_ref, c, x, terms)

    def beyond(x):
        return x < 0 if far else x >= x_count

    along_x, others = {}, {}
    for x in range(side.inside[0] - 2, side.inside[-1] + 3):
        if beyond(x):
            continue
        values = [s_x[i, x] for i in range(3)]
        rest = [s_o[i, x] for i in range(3)] if x in side.inside else None
        if any(beyond(x + k) for k in steps):
            add = [
                central(*(u(c, x + k) if beyond(x + k) else None for k in steps))
                for c in range(comps)
            ]
            lame, shear = metric_ref[3, x], metric_ref[4, x]
            pressure = lame * add[0]
            values[0] = values[0] + pressure + (shear + shear) * add[0]
            values[1] = values[1] + shear * add[1]
            values[2] = values[2] + shear * add[2]
            rest[0] = rest[0] + pressure
            rest[2] = rest[2] + pressure
        along_x[x], others[x] = values, rest

    across = [
        banded(jnp.concatenate([u(c, x) for x in side.outside], 0), band) for c in range(2)
    ]
    for place, x in enumerate(side.outside):
        lame, shear = (side.modulus(first_halo, m, x) for m in range(2))
        dx = [
            central(*(u(c, x + k) if 0 <= x + k < x_count else None for k in steps))
            for c in range(comps)
        ]
        dy = [across[c][place * rows : (place + 1) * rows] for c in range(2)]
        values = [side.own_part(halo_ref, i, x, terms) for i in range(3)]
        values[0] = values[0] + lame * (dx[0] + dy[1]) + (shear + shear) * dx[0]
        values[1] = values[1] + shear * (dy[0] + dx[1])
        values[2] = values[2] + shear * dx[2]
        along_x[x] = values

    def across_of(i, x):
        return along_x[x][1] if i == 0 else others[x][i - 1]

    beside = []
    for i in range(comps):
        result = banded(jnp.concatenate([across_of(i, x) for x in side.inside], 0), band)
        added = edge_terms(e_s[i], window)
        beside.append(
            {
                x: result[k * rows : (k + 1) * rows] + edge_spread(added, x, window)
                for k, x in enumerate(side.inside)
            }
        )

    place = lanes_of((rows, y_count)) // window
    messages = [None] * comps
    for k, x in enumerate(side.inside):
        slope_x, slope_y, stretch = (metric_ref[m, x] for m in range(3))
        r11, r12, r13 = (layer_derivative(value) for value in along_x[x])
        r22, r23, r33 = (layer_derivative(value) for value in others[x])
        layers = ((r11, r12, r13), (r12, r22, r23), (r13, r23, r33))
        for c in range(comps):
            force = central(*(along_x[x + j][c] for j in steps)) + beside[c][x]
            force = force + slope_x * layers[c][0] + slope_y * layers[c][1]
            force = force + stretch * layers[c][2]
            at = c * half + k
            following = 2.0 * inner(c, x) - before_ref[at] + force * push_ref[x]
            out_ref[at] = following
            moved = roll(following, window * x + 4)
            messages[c] = moved if k == 0 else jnp.where(place == x, moved, messages[c])
    for c in range(comps):
        out_edge[c] = messages[c]
    if send:
        side.send(
            sends[0],
            lambda c, x: out_ref[c * half + x - side.inside[0]],
            lambda m, x: metric_ref[m, x],
        )


def fix_kernel(sides, *refs):
    corner_in = refs[:sides]
    first_far, first_near, e_s, push_ref = refs[sides : 4 + sides]
    in_far, in_near, far_edge, near_edge = refs[4 + sides : 8 + sides]
    out_far, out_near, *out_edge = refs[8 + sides :]
    x_count, rows, y_count = push_ref.shape
    half, window = x_count // 2, y_count // x_count
    comps = far_edge.shape[0]
    has_left, has_right = neighbours()
    place = lanes_of((rows, y_count)) // window
    lame, shear = 3, 4
    steps = (-2, -1, 1, 2)

    corners = [corner_tile(corner_in, c, window, has_left, has_right) for c in range(2)]
    terms = [edge_terms(corner, window) for corner in corners]
    beside = [
        edge_terms(e_s[shear] * beyond_change(corners[1], window, x_count), window),
        edge_terms(e_s[lame] * beyond_change(corners[0], window, x_count), window),
    ]
    for c in range(comps):
        message = jnp.where(place < half, far_edge[c], near_edge[c])
        for far, first, in_ref, out_ref in (
            (True, first_far, in_far, out_far),
            (False, first_near, in_near, out_near),
        ):
            side = Side(far, x_count)
            changes = {}
            if c < 2:
                changes = {
                    x: side.modulus(first, c, x)
                    * edge_spread(terms[1 - c], x % x_count, window)
                    for x in side.outside
                }
            for k, x in enumerate(side.inside):
                value = in_ref[c * half + k]
                near = [changes.get(x + j) for j in steps]
                if any(item is not None for item in near):
                    change = central(*near) + edge_spread(beside[c], x, window)
                    value = value + change * push_ref[x]
                    message = jnp.where(place == x, roll(value, window * x + 4), message)
                out_ref[c * half + k] = value
        if out_edge:
            out_edge[0][c] = message


def partner_kernel(sides, edge_ref, *refs):
    edge_in = refs[:sides]
    metric_ref, first_far, first_near = refs[sides : 3 + sides]
    moduli_in = refs[3 + sides : 3 + 2 * sides]
    out_ref = refs[3 + 2 * sides]
    x_count, _, y_count = metric_ref.shape[1:]
    window = y_count // x_count
    has_left, has_right = neighbours()
    edges = [
        edge_tile(edge_ref[c], edge_in[0][c], edge_in[-1][c], has_left, has_right, window)
        for c in range(2)
    ]
    lame, shear = (corner_tile(moduli_in, 2 + m, window, has_left, has_right) for m in range(2))
    terms = [edge_terms(edge, window) for edge in edges]
    beside = [
        edge_terms(shear * beyond_change(edges[1], window, x_count), window),
        edge_terms(lame * beyond_change(edges[0], window, x_count), window),
    ]
    for far, first in ((True, first_far), (False, first_near)):
        side = Side(far, x_count)
        added = {}
        for c in range(2):
            changes = {
                x: metric_ref[3 + c, x] * edge_spread(terms[1 - c], x, window)
                for x in (side.inside[:2] if far else side.inside[-2:])
            }
            for x in side.outside:
                near = [changes.get(x + k) for k in (-2, -1, 1, 2)]
                change = central(*near) + edge_spread(beside[c], x % x_count, window)
                change = change * side.packed(first, 0, x, window)
                added[c, x] = out_ref[side.slot(c, x)] = change
        for x in side.outside:
            slope_x, slope_y, stretch = (side.packed(first, 1 + m, x, window) for m in range(3))
            own_lame, own_shear = (side.modulus(first, m, x) for m in range(2))
            dr = [layer_derivative(added[c, x]) for c in range(2)]
            near = [added.get((c, x + k)) for c in range(2) for k in (-2, -1, 1, 2)]
            dx = [central(*near[:4]), central(*near[4:])]
            g11 = dx[0] + slope_x * dr[0]
            out_ref[side.slot(2, x)] = (
                own_lame * (g11 + slope_y * dr[1]) + (own_shear + own_shear) * g11
            )
            out_ref[side.slot(3, x)] = own_shear * (slope_y * dr[0] + dx[1] + slope_x * dr[1])
            out_ref[side.slot(4, x)] = own_shear * (stretch * dr[0])


def sketch_kernel(moment, last, shape, *refs):
    comps, half, rows, y_count = shape
    far_ref, near_ref, before_far, before_near, probe_ref = refs[:5]
    sketch_in = None if moment == 0 else refs[5]
    sketch_ref, spread = refs[-2:]
    x_count = 2 * half
    groups = rows // SUB
    picked = groups // 2
    now = halves(far_ref, near_ref, half)
    past = halves(before_far, before_near, half)
    odd = is_odd()
    spread[...] = jnp.zeros_like(spread)
    spread[pl.ds(0, y_count // 2, stride=2), :] = probe_ref[moment]
    rates = []
    for x in range(0, x_count, 2):
        for c in range(comps):
            rate = now(c, x) - past(c, x)
            other = now(c, x_count - 1 - x) - past(c, x_count - 1 - x)
            rate = jnp.where(odd, -other if c == 0 else other, rate) * (0.5 / time_step)
            rates += [rate[SUB * v : SUB * (v + 1)] for v in range(0, groups, 2)]
    sketch = jnp.dot(
        jnp.concatenate(rates, 0),
        spread[...],
        precision=lax.Precision.HIGHEST,
        preferred_element_type=jnp.float32,
    )
    if sketch_in is not None:
        sketch = sketch + sketch_in[...]
    if last:
        for k in range(half * comps):
            for v in range(picked):
                start = (k * picked + v) * SUB
                sketch_ref[pl.ds(k * picked * SUB + v, SUB, stride=picked), :] = sketch[
                    start : start + SUB
                ]
    else:
        sketch_ref[...] = sketch


def finish_kernel(half, rows, far_ref, near_ref, out_ref):
    x_count, groups = 2 * half, rows // SUB
    now = halves(far_ref, near_ref, half)
    odd = is_odd()
    for c in range(out_ref.shape[0]):
        values = mirrored([now(c, x) for x in range(x_count)], odd, c == 0)
        for x, value in enumerate(values):
            for v in range(groups):
                out_ref[c, pl.ds(x_count * v + x, SUB, stride=groups * x_count), :] = value[
                    SUB * v : SUB * (v + 1)
                ]


def gram_kernel(*refs):
    sum_ref, packed_ref = refs[-2:]
    total = sum_of([ref[...] for ref in refs[:-2]])
    sum_ref[...] = total
    gram = lax.dot_general(
        total,
        total,
        (((0,), (0,)), ((), ())),
        precision=lax.Precision.HIGHEST,
        preferred_element_type=jnp.float32,
    )
    order = gram.shape[0]
    mid = order // 2
    top, bottom = gram[:mid], gram[mid:]
    row = lax.broadcasted_iota(jnp.int32, (mid, order), 0)
    column = lanes_of((mid, order)) - mid
    packed_ref[:mid] = jnp.where((column >= 0) & (row >= column), roll(top, mid), bottom)
    diagonal = jnp.sum(jnp.where(row == column, bottom, 0.0), 0, keepdims=True)
    packed_ref[mid:] = jnp.broadcast_to(diagonal, (packed_ref.shape[0] - mid, order))


def unpacked(packed):
    order = packed.shape[1]
    mid = order // 2
    row = lax.broadcasted_iota(jnp.int32, (mid, order), 0)
    lane = lanes_of((mid, order))
    column = lane - mid
    main = packed[:mid]
    diagonal = jnp.broadcast_to(packed[mid : mid + 1], (mid, order))
    moved = roll(main, mid)
    top = jnp.where(row > lane, moved, jnp.where(row == lane, 0.5 * moved, 0.0))
    bottom = jnp.where(
        (column < 0) | (row < column), main, jnp.where(row == column, 0.5 * diagonal, 0.0)
    )
    part = jnp.concatenate([top, bottom], 0)
    return part + part.T


def factor_kernel(scale, tall_ref, *refs):
    basis_ref, factor_ref = refs[-2:]
    gram = unpacked(sum_of([ref[...] for ref in refs[:-2]]))
    order = gram.shape[0]
    blocks = order // SUB
    shape = (SUB, order)
    sub = lax.broadcasted_iota(jnp.int32, shape, 0)
    lane = lanes_of(shape)
    work = [gram[SUB * q : SUB * (q + 1)] for q in range(blocks)]
    other = [jnp.where(lane == sub + SUB * q, 1.0, 0.0) for q in range(blocks)]
    inverse_rows = []

    def row_of(value, k):
        return jnp.broadcast_to(value[k : k + 1, :], value.shape)

    def column_of(value, j):
        return jnp.broadcast_to(value[:, j : j + 1], value.shape)

    columns = [column_of(work[0], k) for k in range(SUB)]
    for p in range(blocks):
        after_panel = min(p + 1 + AHEAD, blocks)
        ahead = {
            q: [column_of(work[q], SUB * p + k) for k in range(SUB)]
            for q in range(p + 1, after_panel)
        }
        more = p + 1 < blocks
        coming = [column_of(work[p + 1], SUB * (p + 1) + k) for k in range(SUB)] if more else []
        below = list(ahead[p + 1]) if more else []
        upper = solved = work[p]
        lower = solved_other = other[p]
        pivots = inverses = columns[0]
        for k in range(SUB):
            pivot = row_of(columns[k], k)
            inverse = 1.0 / pivot
            every = jnp.where(sub != k, columns[k] * inverse, 0.0)
            after = jnp.where(sub > k, every, 0.0)
            for m in range(k + 1, SUB):
                entry = row_of(columns[m], k)
                columns[m] = columns[m] - every * entry
                if more:
                    below[m] = below[m] - below[k] * (inverse * entry)
            for j in range(len(coming)):
                coming[j] = coming[j] - below[k] * inverse * row_of(below[k], j)
            upper = upper - after * row_of(upper, k)
            lower = lower - after * row_of(lower, k)
            solved = solved - every * row_of(solved, k)
            solved_other = solved_other - every * row_of(solved_other, k)
            pivots = jnp.where(sub == k, pivot, pivots)
            inverses = jnp.where(sub == k, inverse, inverses)
        root = lax.rsqrt(pivots)
        factor_ref[SUB * p : SUB * (p + 1), :] = jnp.where(lane >= sub + SUB * p, upper * root, 0.0)
        inverse_rows.append(lower * root * scale)
        solved, solved_other = solved * inverses, solved_other * inverses
        for q, entries in ahead.items():
            for k, column in enumerate(entries):
                work[q] = work[q] - column * row_of(solved, k)
                other[q] = other[q] - column * row_of(solved_other, k)
        columns = coming
        if after_panel < blocks:
            both = jnp.concatenate([solved, solved_other], 1)
            parts = [jnp.zeros((SUB * p, 2 * order), jnp.float32)] if p else []
            parts += [both, jnp.zeros((order - SUB * (p + 1), 2 * order), jnp.float32)]
            change = jnp.dot(
                jnp.concatenate(work[after_panel:], 0),
                jnp.concatenate(parts, 0),
                precision=lax.Precision.HIGHEST,
                preferred_element_type=jnp.float32,
            )
            for i, q in enumerate(range(after_panel, blocks)):
                work[q] = work[q] - change[SUB * i : SUB * (i + 1), :order]
                other[q] = other[q] - change[SUB * i : SUB * (i + 1), order:]

    inverse_lower = jnp.concatenate(inverse_rows, 0)
    count, kept = basis_ref.shape[0], basis_ref.shape[1]
    start = pl.multiple_of(lax.axis_index("gy") * kept, SUB)
    tall = jnp.concatenate([tall_ref[k, pl.ds(start, kept), :] for k in range(count)], 0)
    basis = lax.dot_general(
        tall,
        inverse_lower,
        (((1,), (1,)), ((), ())),
        precision=lax.Precision.HIGHEST,
        preferred_element_type=jnp.float32,
    )
    for k in range(count):
        basis_ref[k] = basis[k * kept : (k + 1) * kept]


def f32(*shape):
    return jax.ShapeDtypeStruct(shape, jnp.float32)


VMEM = pl.BlockSpec(memory_space=pltpu.MemorySpace.VMEM)
ANY = pl.BlockSpec(memory_space=pl.ANY)
HBM = pl.BlockSpec(memory_space=pltpu.MemorySpace.HBM)


def call(kernel, outs, ins, specs=None, scratch=(), flops=0):
    size = sum(math.prod(x.shape) * 4 for x in (*ins, *outs))
    return pl.pallas_call(
        kernel,
        out_shape=outs,
        in_specs=specs or [VMEM] * len(ins),
        out_specs=[VMEM] * len(outs),
        scratch_shapes=list(scratch),
        compiler_params=pltpu.CompilerParams(vmem_limit_bytes=24 * 2**20),
        cost_estimate=pl.CostEstimate(flops=flops, bytes_accessed=size, transcendentals=0),
    )(*ins)


def butterfly(value, axis):
    count = lax.axis_size(axis)
    if count & (count - 1):
        return [lax.psum(value, axis)]
    bit, terms = 1, [value]
    while bit < count:
        value = sum_of(terms)
        moves = [bit] if 2 * bit == count else [bit, 2 * bit, 3 * bit]
        others = [
            lax.ppermute(value, axis, [(i, i ^ move) for i in range(count)]) for move in moves
        ]
        terms = [value, *others]
        bit *= 2 if len(moves) == 1 else 4
    return terms


def sum_of(terms):
    if len(terms) == 1:
        return terms[0]
    return sum_of(terms[: len(terms) // 2]) + sum_of(terms[len(terms) // 2 :])


def shards(displacement, velocity, slopes, stretch, moduli, buoyancy, probes):
    comps, layers, x_count, y_count = displacement.shape
    width = probes.shape[2]
    half = x_count // 2
    n_x, n_y = lax.axis_size("gx"), lax.axis_size("gy")
    sides = 1 if n_y == 2 else 2

    def flat(array):
        return array.reshape(array.shape[:-3] + (layers * x_count, y_count))

    def exchange(value, far):
        pairs = [(i, i + 1) for i in range(1 if far else 0, n_x - 1, 2)]
        return lax.ppermute(value, "gx", pairs + [(k, i) for i, k in pairs])

    def along_y(value):
        if sides == 1:
            return [lax.ppermute(value, "gy", [(0, 1), (1, 0)])]
        return [
            lax.ppermute(value, "gy", [(i, i + s) for i in range(n_y) if 0 <= i + s < n_y])
            for s in (1, -1)
        ]

    def slabs(count):
        return f32(count, layers, y_count)

    u_flat = flat(displacement)
    fields = [
        pltpu.with_memory_space_constraint(field, pltpu.MemorySpace.HBM)
        for field in (u_flat, flat(slopes), flat(stretch), flat(moduli), flat(buoyancy))
    ]
    u_far, u_near, far_send, near_send, edge, metric = call(
        begin_kernel,
        [
            slabs(comps * half), slabs(comps * half), slabs(17), slabs(17), slabs(comps + 5),
            f32(5, x_count, layers, y_count),
        ],
        fields,
        specs=[HBM] * 5,
        scratch=[pltpu.VMEM(field.shape, jnp.float32) for field in fields]
        + [pltpu.SemaphoreType.DMA((5,))],
    )
    before_far, before_near, push = call(
        rest_kernel,
        [slabs(comps * half), slabs(comps * half), slabs(x_count)],
        [u_flat, flat(velocity), flat(buoyancy)],
    )

    sketch_rows = half * comps * (layers // 2)
    sketch = []

    def half_step(far, moment, halo, first_halo, before, terms, token):
        return call(
            partial(wide_kernel, far, len(terms), moment < STEPS - 1),
            [slabs(comps * half), slabs(comps)] + ([slabs(12)] if moment < STEPS - 1 else []),
            [
                u_far, u_near, halo, before, metric, push, first_halo, s_x, s_o, e_s, *terms, *token,
            ],
            specs=[VMEM] * (10 + len(terms)) + [ANY] * len(token),
            flops=10_000_000,
        )

    terms = []
    for moment in range(STEPS):
        last = moment == STEPS - 1
        if moment == 0:
            far_halo = exchange(far_send, True)
            near_halo = exchange(near_send, False)
        edge_in = along_y(edge)
        if moment == 0:
            first_edge, first_edge_in, first_far, first_near = edge, edge_in, far_halo, near_halo
        s_x, s_o, e_s = call(
            partial(tile_kernel, sides, comps),
            [f32(comps, x_count, layers, y_count), f32(3, x_count, layers, y_count), slabs(5)],
            [u_far, u_near, edge, *edge_in, metric, first_edge, *first_edge_in],
            flops=20_000_000,
        )
        raw_far, far_edge, *far_send = half_step(
            True, moment, far_halo, first_far, before_far, terms, sketch or [push, near_halo]
        )
        (corner,) = call(
            partial(corner_kernel, x_count, len(terms)),
            [slabs(2 if moment else 4)],
            [far_halo, near_halo, *terms, raw_far],
            specs=[VMEM] * (2 + len(terms)) + [ANY],
        )
        corner_in = along_y(corner)
        if moment == 0:
            moduli_in = corner_in
        raw_near, near_edge, *near_send = half_step(
            False, moment, near_halo, first_near, before_near, terms, [raw_far]
        )
        if not last:
            far_halo = exchange(far_send[0], True)
            near_halo = exchange(near_send[0], False)
            terms = call(
                partial(partner_kernel, sides),
                [slabs(20)],
                [edge, *edge_in, metric, first_far, first_near, *moduli_in],
            )
        next_far, next_near, *edge = call(
            partial(fix_kernel, sides),
            [slabs(comps * half), slabs(comps * half)] + ([] if last else [slabs(comps)]),
            [
                *corner_in, first_far, first_near, e_s, push, raw_far, raw_near, far_edge, near_edge,
            ],
        )
        edge = None if last else edge[0]
        sketch = call(
            partial(sketch_kernel, moment, last, (comps, half, layers, y_count)),
            [f32(sketch_rows, width)],
            [next_far, next_near, before_far, before_near, probes, *sketch],
            scratch=[pltpu.VMEM((y_count, width), jnp.float32)],
        )
        before_far, before_near, u_far, u_near = u_far, u_near, next_far, next_near
    (final,) = call(
        partial(finish_kernel, half, layers),
        [f32(comps, layers * x_count, y_count)],
        [u_far, u_near],
    )
    final = final.reshape(displacement.shape)

    parts = butterfly(sketch[0], "gy")
    tall, packed = call(gram_kernel, [f32(sketch_rows, width), f32(width // 2 + SUB, width)], parts)
    parts = butterfly(packed, "gx")
    depth = comps * (layers // 2)
    basis, factor = call(
        partial(factor_kernel, math.sqrt(sketch_rows * n_x)),
        [f32(half, depth // n_y, width), f32(width, width)],
        [tall.reshape(half, depth, width), *parts],
    )
    return (final, basis, factor)


def solution(mesh):
    in_specs = (
        P(None, None, "gx", "gy"),
        P(None, None, "gx", "gy"),
        P(None, None, "gx", "gy"),
        P(None, "gx", "gy"),
        P(None, None, "gx", "gy"),
        P(None, "gx", "gy"),
        P(None, "gy", None),
    )
    out_specs = (P(None, None, "gx", "gy"), P("gx", "gy", None), P())

    return jax.shard_map(shards, mesh=mesh, in_specs=in_specs, out_specs=out_specs, check_vma=False)
```
